32 devices in a mesh: ctx: 8 (over z, y), ch: 4 (over x, core).
Axes of the slice: x: 2, y: 2, z: 4, core: 2. Of those that a mesh axis runs over, the one named last changes fastest.
Arguments:
- tokens: bfloat16 [8192, 4096], P('ctx', 'ch'), may hold values from -6 to 6
- w_input: bfloat16 [2, 4096, 4096], P(None, None, 'ch'), may hold values from -0.09375 to 0.09375
- w_output: bfloat16 [4096, 4096], P('ctx', 'ch'), may hold values from -0.09375 to 0.09375
- bias_update: float32 [4096], P('ch'), may hold values from -14 to 1
- bias_cand: float32 [4096], P('ch'), may hold values from -1 to 1
- recur_gain: float32 [4096], P('ch'), may hold values from -0.95 to 0.95
- start_state: float32 [4096], P('ch'), may hold values from -1 to 1
Outputs:
- mixed: bfloat16 [8192, 4096], P('ctx', 'ch')
The draws below stay inside these ranges and needn't reach their ends.
All inputs are finite; a program needn't handle non-finite values.
Results may differ from the reference program's by a relative error of at most 0.005.
Values may be sent and summed in bfloat16 or wider, within the bound.
No kernel may reach another device: no remote copies, remote signals or barrier semaphores. Data moves between devices by JAX's collectives and lax.ppermute only.
A program may use at most 128 MiB of HBM per device.

```python
import math
import jax
import jax.numpy as jnp
from jax import lax

D = 4096
ITERS = 2
LENGTH = 8192


def draw_bias_update(key, part):
    pick_key = jax.random.fold_in(key, 11)
    slow_key = jax.random.fold_in(key, 12)
    fast_key = jax.random.fold_in(key, 13)
    slow_share = 0.5
    is_slow = jax.random.bernoulli(pick_key, slow_share, (D,))
    span = jnp.log(jnp.float32(LENGTH))
    slow_rate = jax.random.uniform(slow_key, (D,), jnp.float32, -3.0, 0.5) - span
    fast_rate = jax.random.uniform(fast_key, (D,), jnp.float32, -4.0, 1.0)
    return jnp.where(is_slow, slow_rate, fast_rate)


def block_levels(stream_key, shape, shards, least, top_value):
    level = 1.0
    for dim, shards_of in shards:
        heights = jax.random.uniform(jax.random.fold_in(jax.random.fold_in(stream_key, 6), dim), (shards_of,), jnp.float32, least / len(shards), top_value / len(shards))
        level = level * jnp.repeat(jnp.exp(heights), shape[dim] // shards_of).reshape((-1,) + (1,) * (len(shape) - 1 - dim))
    return level


def noise(rng, dims, width, reach, cuts=(), dtype=jnp.bfloat16):
    factor_of = block_levels(rng, dims, cuts, -0.22, 0.18) if cuts else 1.0
    drawn = jax.random.normal(rng, dims, jnp.float32) * width * factor_of
    return jnp.minimum(jnp.maximum(drawn, -reach), reach).astype(dtype)


def setup_inputs(seed: int = 0) -> dict:
    key_list = jax.random.split(jax.random.key(seed), 8)
    return {
        "tokens": noise(key_list[0], (LENGTH, D), 1.0, 6.0, ((0, 8), (1, 4))),
        "w_input": noise(key_list[1], (2, D, D), D ** -0.5, 0.09375, ((2, 4),)),
        "w_output": noise(key_list[2], (D, D), D ** -0.5, 0.09375, ((0, 8), (1, 4))),
        "bias_update": draw_bias_update(jax.random.fold_in(key_list[7], 71), 0),
        "bias_cand": jnp.clip(jax.random.uniform(key_list[4], (D,), jnp.float32, -1.0, 1.0) * block_levels(key_list[4], (D,), ((0, 4),), -0.4, 0.0), -1.0, 1.0),
        "recur_gain": jnp.clip(jax.random.uniform(key_list[5], (D,), jnp.float32, -0.95, 0.95) * block_levels(key_list[5], (D,), ((0, 4),), -0.4, 0.0), -0.95, 0.95),
        "start_state": jnp.clip(jax.random.uniform(key_list[6], (D,), jnp.float32, -1.0, 1.0) * block_levels(key_list[6], (D,), ((0, 4),), -0.4, 0.0), -1.0, 1.0),
    }


def advance(state_vec, pair_in):
    new_state = pair_in[0] * state_vec + pair_in[1]
    return new_state, new_state


def reference(tokens, w_input, w_output, bias_update, bias_cand, recur_gain, start_state):
    block_width = math.gcd(D, 256)
    blocks = D // block_width
    w_blocks = w_input.reshape(2, D, blocks, block_width).transpose(2, 0, 1, 3)

    def solve_block(pieces):
        w_cols, bias_gate, bias_value, gain_row, start_row = pieces
        update_pre = (jnp.dot(tokens, w_cols[0], preferred_element_type=jnp.float32) + bias_gate).astype(jnp.bfloat16)
        cand_pre = (jnp.dot(tokens, w_cols[1], preferred_element_type=jnp.float32) + bias_value).astype(jnp.bfloat16)
        update_pre, cand_pre = lax.optimization_barrier((update_pre, cand_pre))
        update = jax.nn.sigmoid(update_pre.astype(jnp.float32))
        candidate = cand_pre.astype(jnp.float32)
        trajectory = jnp.zeros((LENGTH, block_width), jnp.float32)
        for iteration in range(ITERS):
            previous = jnp.concatenate([start_row[None, :], trajectory[:-1]], axis=0)
            squashed = jnp.tanh(candidate + gain_row * previous)
            mapped = (1.0 - update) * previous + update * squashed
            slopes = (1.0 - update) + update * gain_row * (1.0 - squashed * squashed)
            offsets = mapped - slopes * previous
            ignored, trajectory = lax.scan(advance, start_row, (slopes, offsets))
        return trajectory.astype(jnp.bfloat16)

    pieces = (w_blocks, bias_update.reshape(blocks, block_width), bias_cand.reshape(blocks, block_width),
              recur_gain.reshape(blocks, block_width), start_state.reshape(blocks, block_width))
    states = lax.map(solve_block, pieces)
    states = states.transpose(1, 0, 2).reshape(LENGTH, D)
    return jnp.dot(states, w_output, preferred_element_type=jnp.float32).astype(jnp.bfloat16)
```

```python
import functools
import math

import jax
import jax.numpy as jnp
from jax import lax
from jax.experimental import pallas as pl
from jax.experimental.pallas import tpu as pltpu
from jax.sharding import PartitionSpec as P

SEGS = 8
LANES = 128
F32 = jnp.float32
BF16 = jnp.bfloat16
VMEM_LIMIT = 48 * 1024 * 1024


def swap(block, axis, bits):
    return lax.ppermute(block, axis, [(i, i ^ bits) for i in range(lax.axis_size(axis))])


def tile_of(width, most):
    return math.gcd(width, most)


def params(limit=VMEM_LIMIT):
    return pltpu.CompilerParams(vmem_limit_bytes=limit)


def cost(flops, nbytes, trans=0):
    return pl.CostEstimate(flops=int(flops), bytes_accessed=int(nbytes), transcendentals=int(trans))


def near_kernel(half, place, *refs):
    blocks = refs[:half]
    w_ref, out_ref = refs[half:]
    depth = blocks[0].shape[1]
    rows = out_ref.shape[1]
    step = tile_of(rows, 256)
    slot = lax.rem(place[0], half)

    def body(m, carry):
        lines = pl.ds(pl.multiple_of(m * step, step), step)
        total = None
        for d in range(half):
            deep = pl.ds(pl.multiple_of((slot ^ d) * depth, depth), depth)
            part = jnp.dot(blocks[d][lines, :], w_ref[0, deep, :], preferred_element_type=F32)
            total = part if total is None else total + part
        out_ref[0, lines, :] = total
        return carry

    lax.fori_loop(0, rows // step, body, 0)


def near_product(place, blocks, weights, name):
    half = len(blocks)
    rows, depth = blocks[0].shape
    gates, _, width = weights.shape
    tn = tile_of(width, 512)
    spec = pl.BlockSpec((rows, depth), lambda g, n, p: (0, 0))
    return pl.pallas_call(
        functools.partial(near_kernel, half),
        out_shape=jax.ShapeDtypeStruct((gates, rows, width), F32),
        grid_spec=pltpu.PrefetchScalarGridSpec(
            num_scalar_prefetch=1,
            grid=(gates, width // tn),
            in_specs=[spec] * half
            + [pl.BlockSpec((1, half * depth, tn), lambda g, n, p: (g, p[0] // half, n))],
            out_specs=pl.BlockSpec((1, rows, tn), lambda g, n, p: (g, 0, n)),
        ),
        compiler_params=params(),
        cost_estimate=cost(
            2 * gates * rows * half * depth * width,
            gates * width * (half * depth * 2 + rows * 4) + half * rows * depth * 2,
        ),
        name=name,
    )(place, *blocks, weights)


def compose_rows(maps, count, a, b):
    for k in range(count):
        slope = maps[0, k : k + 1, :]
        shift = maps[1, k : k + 1, :]
        b = slope * b + shift
        a = slope * a
    return a, b


def spread_rows(flat, g, j, seg):
    parts = [flat[g, l, pl.ds(j, SEGS, stride=seg), :] for l in range(flat.shape[1])]
    return jnp.concatenate(parts, axis=1)


def gate_kernel(half, chunk, before, last, place, *refs):
    blocks = refs[:half]
    part_ref, w_ref, bias_ref, gain_ref, start_ref = refs[half : half + 5]
    earlier = refs[half + 5 : half + 5 + before]
    outs = refs[half + 5 + before :]
    gates_ref, maps_ref = outs[:2]
    flat = outs[-1]
    depth = blocks[0].shape[1]
    rows = part_ref.shape[1]
    seg = rows // SEGS
    width = part_ref.shape[2]
    slot = lax.rem(place[0], half)
    for g in range(2):
        total = part_ref[g]
        for d in range(half):
            deep = pl.ds(pl.multiple_of((slot ^ d) * depth, depth), depth)
            total = total + jnp.dot(blocks[d][...], w_ref[g, deep, :], preferred_element_type=F32)
        total = (total + bias_ref[g : g + 1, :]).astype(BF16).astype(F32)
        for l in range(width // LANES):
            flat[g, l] = total[:, l * LANES : (l + 1) * LANES]
    gain = jnp.broadcast_to(gain_ref[...], (SEGS, width))

    def pair(jj, carry, first):
        a, b = carry
        held = ([], [])
        for k in range(2):
            j = 2 * jj + k
            pre = spread_rows(flat, 0, j, seg)
            cand = spread_rows(flat, 1, j, seg)
            held[0].append(pre)
            held[1].append(cand)
            update = jax.nn.sigmoid(pre)
            if first and k == 0:
                lead = lax.broadcasted_iota(jnp.int32, (SEGS, width), 0) == 0
                prev = jnp.where(lead & (place[1] == 0), start_ref[...], 0.0)
                squashed = jnp.tanh(cand + gain * prev)
                bend = gain * (1.0 - squashed * squashed)
                offset = update * (squashed - bend * prev)
            else:
                squashed = jnp.tanh(cand)
                bend = gain * (1.0 - squashed * squashed)
                offset = update * squashed
            slope = (1.0 - update) + update * bend
            b = slope * b + offset
            a = slope * a
        lines = pl.ds(pl.multiple_of(jj * 2 * SEGS, 2 * SEGS), 2 * SEGS)
        for g in range(2):
            gates_ref[g, lines, :] = jnp.concatenate(held[g], axis=0).astype(BF16)
        return a, b

    carry = (jnp.ones((SEGS, width), F32), jnp.zeros((SEGS, width), F32))
    if chunk == 0:
        carry = pair(0, carry, True)
        begin = 1
    else:
        begin = 0
    a, b = lax.fori_loop(begin, seg // 2, lambda jj, c: pair(jj, c, False), carry)
    maps_ref[0] = a
    maps_ref[1] = b
    if last:
        total_ref = outs[2]
        ta, tb = jnp.ones((1, width), F32), jnp.zeros((1, width), F32)
        for maps in list(earlier) + [maps_ref]:
            ta, tb = compose_rows(maps, SEGS, ta, tb)
        for i in range(total_ref.shape[0]):
            total_ref[i, 0:1, :] = ta
            total_ref[i, 1:2, :] = tb


def gate_chunk(place, blocks, partial, weights, biases, gain, start, earlier, chunk, last, peers):
    half = len(blocks)
    rows, depth = blocks[0].shape
    gates, _, width = weights.shape
    tn = tile_of(width, 256)
    row_spec = pl.BlockSpec((1, tn), lambda n, p: (0, n))
    map_spec = pl.BlockSpec((2, SEGS, tn), lambda n, p: (0, 0, n))
    out_shape = [
        jax.ShapeDtypeStruct((2, rows, width), BF16),
        jax.ShapeDtypeStruct((2, SEGS, width), F32),
    ]
    out_specs = [pl.BlockSpec((2, rows, tn), lambda n, p: (0, 0, n)), map_spec]
    if last:
        out_shape.append(jax.ShapeDtypeStruct((peers, 2, width), F32))
        out_specs.append(pl.BlockSpec((peers, 2, tn), lambda n, p: (0, 0, n)))
    return pl.pallas_call(
        functools.partial(gate_kernel, half, chunk, len(earlier), last),
        out_shape=out_shape,
        grid_spec=pltpu.PrefetchScalarGridSpec(
            num_scalar_prefetch=1,
            grid=(width // tn,),
            in_specs=[pl.BlockSpec((rows, depth), lambda n, p: (0, 0))] * half
            + [
                pl.BlockSpec((2, rows, tn), lambda n, p: (0, chunk, n)),
                pl.BlockSpec((2, half * depth, tn), lambda n, p: (0, (p[0] // half) ^ 1, n)),
                pl.BlockSpec((2, tn), lambda n, p: (0, n)),
                row_spec,
                row_spec,
            ]
            + [map_spec] * len(earlier),
            out_specs=out_specs,
            scratch_shapes=[pltpu.VMEM((2, tn // LANES, rows, LANES), F32)],
        ),
        compiler_params=params(),
        cost_estimate=cost(
            2 * gates * rows * half * depth * width,
            gates * width * (half * depth * 2 + rows * 6) + half * rows * depth * 2,
            4 * rows * width,
        ),
        name=f"gates_{chunk}",
    )(place, *blocks, partial, weights, biases, gain, start, *earlier)


def entering_state(place, peer_maps, start, peers):
    state = start
    for k in range(peers):
        moved = peer_maps[k, 0:1, :] * state + peer_maps[k, 1:2, :]
        state = jnp.where(place[1] > k, moved, state)
    return state


def enter_segments(maps_list, state, enter):
    for c, maps in enumerate(maps_list):
        for k in range(SEGS):
            enter[c * SEGS + k : c * SEGS + k + 1, :] = state
            state = maps[0, k : k + 1, :] * state + maps[1, k : k + 1, :]


def bend_kernel(chunks, peers, place, *refs):
    gates = refs[:chunks]
    maps = refs[chunks : 2 * chunks]
    peer_ref, gain_ref, start_ref, run_ref, maps_ref, total_ref, enter = refs[2 * chunks :]
    rows, width = gates[0].shape[1:]
    seg = rows // SEGS
    start = start_ref[...]
    enter_segments(maps, entering_state(place, peer_ref, start, peers), enter)
    gain = jnp.broadcast_to(gain_ref[...], (SEGS, width))

    def pair(jj, carry, first):
        lines = pl.ds(pl.multiple_of(jj * 2 * SEGS, 2 * SEGS), 2 * SEGS)
        out = []
        for c in range(chunks):
            state, a, b = carry[c]
            pre2 = gates[c][0, lines, :].astype(F32)
            cand2 = gates[c][1, lines, :].astype(F32)
            for k in range(2):
                pre = pre2[k * SEGS : (k + 1) * SEGS]
                cand = cand2[k * SEGS : (k + 1) * SEGS]
                update = jax.nn.sigmoid(pre)
                keep = 1.0 - update
                if first and k == 0 and c == 0:
                    lead = lax.broadcasted_iota(jnp.int32, (SEGS, width), 0) == 0
                    prev = jnp.where(lead & (place[1] == 0), start, 0.0)
                    squashed = jnp.tanh(cand + gain * prev)
                    bend = gain * (1.0 - squashed * squashed)
                    offset = update * (squashed - bend * prev)
                else:
                    squashed = jnp.tanh(cand)
                    bend = gain * (1.0 - squashed * squashed)
                    offset = update * squashed
                slope = keep + update * bend
                squashed = jnp.tanh(cand + gain * state)
                bend = gain * (1.0 - squashed * squashed)
                slope2 = keep + update * bend
                offset2 = update * (squashed - bend * state)
                state = slope * state + offset
                b = slope2 * b + offset2
                a = slope2 * a
                row = pl.ds(pl.multiple_of(c * rows + (2 * jj + k) * SEGS, SEGS), SEGS)
                run_ref[0, row, :] = a
                run_ref[1, row, :] = b
            out.append((state, a, b))
        return tuple(out)

    one, zero = jnp.ones((SEGS, width), F32), jnp.zeros((SEGS, width), F32)
    carry = tuple((enter[c * SEGS : (c + 1) * SEGS, :], one, zero) for c in range(chunks))
    carry = pair(0, carry, True)
    carry = lax.fori_loop(1, seg // 2, lambda jj, c: pair(jj, c, False), carry)
    for c in range(chunks):
        maps_ref[0, c * SEGS : (c + 1) * SEGS, :] = carry[c][1]
        maps_ref[1, c * SEGS : (c + 1) * SEGS, :] = carry[c][2]
    ta, tb = compose_rows(maps_ref, chunks * SEGS, jnp.ones((1, width), F32), jnp.zeros((1, width), F32))
    for i in range(peers):
        total_ref[i, 0:1, :] = ta
        total_ref[i, 1:2, :] = tb


def bend_all(place, gates, maps, peer_maps, gain, start):
    chunks = len(gates)
    peers = peer_maps.shape[0]
    _, rows, width = gates[0].shape
    tn = tile_of(width, 256)
    row_spec = pl.BlockSpec((1, tn), lambda n, p: (0, n))
    return pl.pallas_call(
        functools.partial(bend_kernel, chunks, peers),
        out_shape=[
            jax.ShapeDtypeStruct((2, chunks * rows, width), F32),
            jax.ShapeDtypeStruct((2, chunks * SEGS, width), F32),
            jax.ShapeDtypeStruct((peers, 2, width), F32),
        ],
        grid_spec=pltpu.PrefetchScalarGridSpec(
            num_scalar_prefetch=1,
            grid=(width // tn,),
            in_specs=[pl.BlockSpec((2, rows, tn), lambda n, p: (0, 0, n))] * chunks
            + [pl.BlockSpec((2, SEGS, tn), lambda n, p: (0, 0, n))] * chunks
            + [pl.BlockSpec((peers, 2, tn), lambda n, p: (0, 0, n)), row_spec, row_spec],
            out_specs=[
                pl.BlockSpec((2, chunks * rows, tn), lambda n, p: (0, 0, n)),
                pl.BlockSpec((2, chunks * SEGS, tn), lambda n, p: (0, 0, n)),
                pl.BlockSpec((peers, 2, tn), lambda n, p: (0, 0, n)),
            ],
            scratch_shapes=[pltpu.VMEM((chunks * SEGS, tn), F32)],
        ),
        compiler_params=params(),
        cost_estimate=cost(
            40 * chunks * rows * width, 12 * chunks * rows * width, 5 * chunks * rows * width
        ),
        name="bend",
    )(place, *gates, *maps, peer_maps, gain, start)


def state_kernel(chunk, peers, place, run_ref, maps_ref, peer_ref, start_ref, out_ref, enter, flat):
    rows, width = out_ref.shape
    seg = rows // SEGS
    state = entering_state(place, peer_ref, start_ref[...], peers)
    for k in range((chunk + 1) * SEGS):
        if k >= chunk * SEGS:
            enter[k - chunk * SEGS : k - chunk * SEGS + 1, :] = state
        state = maps_ref[0, k : k + 1, :] * state + maps_ref[1, k : k + 1, :]
    entered = enter[...]

    def step(j, carry):
        row = pl.ds(pl.multiple_of(j * SEGS, SEGS), SEGS)
        now = run_ref[0, row, :] * entered + run_ref[1, row, :]
        for l in range(width // LANES):
            flat[l, pl.ds(j, SEGS, stride=seg), :] = now[:, l * LANES : (l + 1) * LANES]
        return carry

    lax.fori_loop(0, seg, step, 0, unroll=4)
    for l in range(width // LANES):
        out_ref[:, l * LANES : (l + 1) * LANES] = flat[l].astype(BF16)


def state_chunk(place, run, maps, peer_maps, start, rows, chunk):
    width = run.shape[2]
    peers = peer_maps.shape[0]
    segs = maps.shape[1]
    tn = tile_of(width, 256)
    return pl.pallas_call(
        functools.partial(state_kernel, chunk, peers),
        out_shape=jax.ShapeDtypeStruct((rows, width), BF16),
        grid_spec=pltpu.PrefetchScalarGridSpec(
            num_scalar_prefetch=1,
            grid=(width // tn,),
            in_specs=[
                pl.BlockSpec((2, rows, tn), lambda n, p: (0, chunk, n)),
                pl.BlockSpec((2, segs, tn), lambda n, p: (0, 0, n)),
                pl.BlockSpec((peers, 2, tn), lambda n, p: (0, 0, n)),
                pl.BlockSpec((1, tn), lambda n, p: (0, n)),
            ],
            out_specs=pl.BlockSpec((rows, tn), lambda n, p: (0, n)),
            scratch_shapes=[pltpu.VMEM((SEGS, tn), F32), pltpu.VMEM((tn // LANES, rows, LANES), F32)],
        ),
        compiler_params=params(),
        cost_estimate=cost(2 * rows * width, 10 * rows * width),
        name=f"states_{chunk}",
    )(place, run, maps, peer_maps, start)


def mix_kernel(half, aliased, place, *refs):
    blocks = refs[: 2 * half]
    near_ref, far_ref = refs[2 * half : 2 * half + 2]
    out_ref = refs[-1]
    depth = blocks[0].shape[1]
    slot = lax.rem(place[0], half)
    total = None
    for d in range(half):
        deep = pl.ds(pl.multiple_of((slot ^ d) * depth, depth), depth)
        for block, w_ref in ((blocks[d], near_ref), (blocks[half + d], far_ref)):
            part = jnp.dot(block[...], w_ref[deep, :], preferred_element_type=F32)
            total = part if total is None else total + part
    out_ref[...] = total.astype(BF16)


def mix_chunk(place, blocks, weights, whole, chunk, chunks):
    half = len(blocks) // 2
    rows, depth = blocks[0].shape
    width = weights.shape[1]
    tn = tile_of(width, 256)
    args = [place, *blocks, weights, weights]
    in_specs = [pl.BlockSpec((rows, depth), lambda n, p: (0, 0))] * (2 * half) + [
        pl.BlockSpec((half * depth, tn), lambda n, p: (p[0] // half, n)),
        pl.BlockSpec((half * depth, tn), lambda n, p: ((p[0] // half) ^ 1, n)),
    ]
    aliases = {}
    if whole is not None:
        aliases = {len(args): 0}
        args.append(whole)
        in_specs.append(pl.BlockSpec(memory_space=pl.ANY))
    return pl.pallas_call(
        functools.partial(mix_kernel, half, whole is not None),
        out_shape=jax.ShapeDtypeStruct((rows * chunks, width), BF16),
        grid_spec=pltpu.PrefetchScalarGridSpec(
            num_scalar_prefetch=1,
            grid=(width // tn,),
            in_specs=in_specs,
            out_specs=pl.BlockSpec((rows, tn), lambda n, p: (chunk, n)),
        ),
        input_output_aliases=aliases,
        compiler_params=params(),
        cost_estimate=cost(
            4 * rows * half * depth * width, 4 * half * depth * (width + rows) + 2 * rows * width
        ),
        name=f"mix_{chunk}",
    )(*args)


def gather_pairs(block, half):
    near = [block] + [swap(block, "ch", d) for d in range(1, half)]
    return near


def on_device(tokens, w_input, w_output, bias_update, bias_cand, recur_gain, start_state):
    peers = lax.axis_size("ctx")
    group = lax.axis_size("ch")
    half = group // 2
    total_rows = tokens.shape[0]
    rows = tile_of(total_rows, 256)
    chunks = total_rows // rows
    place = jnp.stack([lax.axis_index("ch"), lax.axis_index("ctx")]).astype(jnp.int32)
    biases = jnp.stack([bias_update, bias_cand], axis=0)
    gain = recur_gain[None, :]
    start = start_state[None, :]

    w_full = lax.all_gather(w_output, "ctx", axis=0, tiled=True)

    far = [[swap(tokens[c * rows : (c + 1) * rows], "ch", half)] for c in range(chunks)]
    near = [tokens] + [swap(tokens, "ch", d) for d in range(1, half)]
    for c in range(chunks):
        far[c] += [swap(far[c][0], "ch", d) for d in range(1, half)]

    partial = near_product(place, near, w_input, "near")
    gates, maps = [], []
    for c in range(chunks):
        last = c == chunks - 1
        out = gate_chunk(
            place, far[c], partial, w_input, biases, gain, start, maps if last else [], c, last, peers
        )
        gates.append(out[0])
        maps.append(out[1])
    peer_maps = lax.all_to_all(out[2], "ctx", 0, 0, tiled=True)
    run, run_maps, totals = bend_all(place, gates, maps, peer_maps, gain, start)
    peer_maps = lax.all_to_all(totals, "ctx", 0, 0, tiled=True)
    blocks = []
    for c in range(chunks):
        own = state_chunk(place, run, run_maps, peer_maps, start, rows, c)
        across = swap(own, "ch", half)
        blocks.append((own, across))
    mixed = None
    for c in range(chunks):
        own, across = blocks[c]
        near = [own] + [swap(own, "ch", d) for d in range(1, half)]
        far = [across] + [swap(across, "ch", d) for d in range(1, half)]
        mixed = mix_chunk(place, near + far, w_full, mixed, c, chunks)
    return mixed


def solution(mesh):
    return jax.shard_map(
        on_device,
        mesh=mesh,
        in_specs=(
            P("ctx", "ch"),
            P(None, None, "ch"),
            P("ctx", "ch"),
            P("ch"),
            P("ch"),
            P("ch"),
            P("ch"),
        ),
        out_specs=P("ctx", "ch"),
        check_vma=False,
    )
```

```python
import functools
import math

import jax
import jax.numpy as jnp
from jax import lax
from jax.experimental import pallas as pl
from jax.experimental.pallas import tpu as pltpu
from jax.sharding import PartitionSpec as P


SEGS = 8
LANES = 128
F32 = jnp.float32
BF16 = jnp.bfloat16
VMEM_LIMIT = 60 * 1024 * 1024


def swap(block, axis, bits):
    return lax.ppermute(block, axis, [(i, i ^ bits) for i in range(lax.axis_size(axis))])


def tile_of(width, most):
    return math.gcd(width, most)


def params(limit=VMEM_LIMIT):
    return pltpu.CompilerParams(vmem_limit_bytes=limit)


def cost(flops, nbytes, trans=0):
    return pl.CostEstimate(flops=int(flops), bytes_accessed=int(nbytes), transcendentals=int(trans))


def near_kernel(half, place, *refs):
    blocks = refs[:half]
    w_ref, out_ref = refs[half:]
    depth = blocks[0].shape[1]
    rows = out_ref.shape[1]
    step = tile_of(rows, 256)
    slot = lax.rem(place[0], half)

    def body(m, carry):
        lines = pl.ds(pl.multiple_of(m * step, step), step)
        total = None
        for d in range(half):
            deep = pl.ds(pl.multiple_of((slot ^ d) * depth, depth), depth)
            part = jnp.dot(blocks[d][lines, :], w_ref[0, deep, :], preferred_element_type=F32)
            total = part if total is None else total + part
        out_ref[0, lines, :] = total
        return carry

    lax.fori_loop(0, rows // step, body, 0)


def near_product(place, blocks, weights):
    half = len(blocks)
    rows, depth = blocks[0].shape
    gates, _, width = weights.shape
    tn = tile_of(width, 512)
    spec = pl.BlockSpec((rows, depth), lambda g, n, p: (0, 0))
    return pl.pallas_call(
        functools.partial(near_kernel, half),
        out_shape=jax.ShapeDtypeStruct((gates, rows, width), F32),
        grid_spec=pltpu.PrefetchScalarGridSpec(
            num_scalar_prefetch=1,
            grid=(gates, width // tn),
            in_specs=[spec] * half
            + [pl.BlockSpec((1, half * depth, tn), lambda g, n, p: (g, p[0] // half, n))],
            out_specs=pl.BlockSpec((1, rows, tn), lambda g, n, p: (g, 0, n)),
        ),
        compiler_params=params(),
        cost_estimate=cost(
            2 * gates * rows * half * depth * width,
            gates * width * (half * depth * 2 + rows * 4) + half * rows * depth * 2,
        ),
    )(place, *blocks, weights)


def compose_rows(maps, count, a, b):
    for k in range(count):
        slope = maps[0, k : k + 1, :]
        shift = maps[1, k : k + 1, :]
        b = slope * b + shift
        a = slope * a
    return a, b


def spread_rows(flat, g, j, seg):
    parts = [flat[g, l, pl.ds(j, SEGS, stride=seg), :] for l in range(flat.shape[1])]
    return jnp.concatenate(parts, axis=1)


def gate_kernel(half, chunk, before, last, place, *refs):
    blocks = refs[:half]
    part_ref, w_ref, bias_ref, gain_ref, start_ref = refs[half : half + 5]
    earlier = refs[half + 5 : half + 5 + before]
    outs = refs[half + 5 + before :]
    gates_ref, maps_ref = outs[:2]
    flat = outs[-1]
    depth = blocks[0].shape[1]
    rows = part_ref.shape[1]
    seg = rows // SEGS
    width = part_ref.shape[2]
    slot = lax.rem(place[0], half)
    for g in range(2):
        total = part_ref[g]
        for d in range(half):
            deep = pl.ds(pl.multiple_of((slot ^ d) * depth, depth), depth)
            total = total + jnp.dot(blocks[d][...], w_ref[g, deep, :], preferred_element_type=F32)
        total = (total + bias_ref[g : g + 1, :]).astype(BF16).astype(F32)
        for l in range(width // LANES):
            flat[g, l] = total[:, l * LANES : (l + 1) * LANES]
    gain = jnp.broadcast_to(gain_ref[...], (SEGS, width))

    def pair(jj, carry, first):
        a, b = carry
        held = ([], [])
        for k in range(2):
            j = 2 * jj + k
            pre = spread_rows(flat, 0, j, seg)
            cand = spread_rows(flat, 1, j, seg)
            held[0].append(pre)
            held[1].append(cand)
            update = jax.nn.sigmoid(pre)
            if first and k == 0:
                lead = lax.broadcasted_iota(jnp.int32, (SEGS, width), 0) == 0
                prev = jnp.where(lead & (place[1] == 0), start_ref[...], 0.0)
                squashed = jnp.tanh(cand + gain * prev)
                bend = gain * (1.0 - squashed * squashed)
                offset = update * (squashed - bend * prev)
            else:
                squashed = jnp.tanh(cand)
                bend = gain * (1.0 - squashed * squashed)
                offset = update * squashed
            slope = (1.0 - update) + update * bend
            b = slope * b + offset
            a = slope * a
        lines = pl.ds(pl.multiple_of(jj * 2 * SEGS, 2 * SEGS), 2 * SEGS)
        for g in range(2):
            gates_ref[g, lines, :] = jnp.concatenate(held[g], axis=0).astype(BF16)
        return a, b

    carry = (jnp.ones((SEGS, width), F32), jnp.zeros((SEGS, width), F32))
    if chunk == 0:
        carry = pair(0, carry, True)
        begin = 1
    else:
        begin = 0
    a, b = lax.fori_loop(begin, seg // 2, lambda jj, c: pair(jj, c, False), carry)
    maps_ref[0] = a
    maps_ref[1] = b
    if last:
        total_ref = outs[2]
        ta, tb = jnp.ones((1, width), F32), jnp.zeros((1, width), F32)
        for maps in list(earlier) + [maps_ref]:
            ta, tb = compose_rows(maps, SEGS, ta, tb)
        for i in range(total_ref.shape[0]):
            total_ref[i, 0:1, :] = ta
            total_ref[i, 1:2, :] = tb


def gate_chunk(place, blocks, partial, weights, biases, gain, start, earlier, chunk, last, peers):
    half = len(blocks)
    rows, depth = blocks[0].shape
    gates, _, width = weights.shape
    tn = tile_of(width, 256)
    row_spec = pl.BlockSpec((1, tn), lambda n, p: (0, n))
    map_spec = pl.BlockSpec((2, SEGS, tn), lambda n, p: (0, 0, n))
    out_shape = [
        jax.ShapeDtypeStruct((2, rows, width), BF16),
        jax.ShapeDtypeStruct((2, SEGS, width), F32),
    ]
    out_specs = [pl.BlockSpec((2, rows, tn), lambda n, p: (0, 0, n)), map_spec]
    if last:
        out_shape.append(jax.ShapeDtypeStruct((peers, 2, width), F32))
        out_specs.append(pl.BlockSpec((peers, 2, tn), lambda n, p: (0, 0, n)))
    return pl.pallas_call(
        functools.partial(gate_kernel, half, chunk, len(earlier), last),
        out_shape=out_shape,
        grid_spec=pltpu.PrefetchScalarGridSpec(
            num_scalar_prefetch=1,
            grid=(width // tn,),
            in_specs=[pl.BlockSpec((rows, depth), lambda n, p: (0, 0))] * half
            + [
                pl.BlockSpec((2, rows, tn), lambda n, p: (0, chunk, n)),
                pl.BlockSpec((2, half * depth, tn), lambda n, p: (0, (p[0] // half) ^ 1, n)),
                pl.BlockSpec((2, tn), lambda n, p: (0, n)),
                row_spec,
                row_spec,
            ]
            + [map_spec] * len(earlier),
            out_specs=out_specs,
            scratch_shapes=[pltpu.VMEM((2, tn // LANES, rows, LANES), F32)],
        ),
        compiler_params=params(),
        cost_estimate=cost(
            2 * gates * rows * half * depth * width,
            gates * width * (half * depth * 2 + rows * 6) + half * rows * depth * 2,
            4 * rows * width,
        ),
    )(place, *blocks, partial, weights, biases, gain, start, *earlier)


def entering_state(place, peer_maps, start, peers):
    state = start
    for k in range(peers):
        moved = peer_maps[k, 0:1, :] * state + peer_maps[k, 1:2, :]
        state = jnp.where(place[1] > k, moved, state)
    return state


def enter_segments(maps_list, state, enter):
    for c, maps in enumerate(maps_list):
        for k in range(SEGS):
            enter[c * SEGS + k : c * SEGS + k + 1, :] = state
            state = maps[0, k : k + 1, :] * state + maps[1, k : k + 1, :]


def bend_kernel(chunks, peers, place, *refs):
    gates = refs[:chunks]
    maps = refs[chunks : 2 * chunks]
    peer_ref, gain_ref, start_ref, run_ref, maps_ref, total_ref, enter = refs[2 * chunks :]
    rows, width = gates[0].shape[1:]
    seg = rows // SEGS
    start = start_ref[...]
    enter_segments(maps, entering_state(place, peer_ref, start, peers), enter)
    gain = jnp.broadcast_to(gain_ref[...], (SEGS, width))

    def pair(jj, carry, first):
        lines = pl.ds(pl.multiple_of(jj * 2 * SEGS, 2 * SEGS), 2 * SEGS)
        out = []
        for c in range(chunks):
            state, a, b = carry[c]
            pre2 = gates[c][0, lines, :].astype(F32)
            cand2 = gates[c][1, lines, :].astype(F32)
            for k in range(2):
                pre = pre2[k * SEGS : (k + 1) * SEGS]
                cand = cand2[k * SEGS : (k + 1) * SEGS]
                update = jax.nn.sigmoid(pre)
                keep = 1.0 - update
                if first and k == 0 and c == 0:
                    lead = lax.broadcasted_iota(jnp.int32, (SEGS, width), 0) == 0
                    prev = jnp.where(lead & (place[1] == 0), start, 0.0)
                    squashed = jnp.tanh(cand + gain * prev)
                    bend = gain * (1.0 - squashed * squashed)
                    offset = update * (squashed - bend * prev)
                else:
                    squashed = jnp.tanh(cand)
                    bend = gain * (1.0 - squashed * squashed)
                    offset = update * squashed
                slope = keep + update * bend
                squashed = jnp.tanh(cand + gain * state)
                bend = gain * (1.0 - squashed * squashed)
                slope2 = keep + update * bend
                offset2 = update * (squashed - bend * state)
                state = slope * state + offset
                b = slope2 * b + offset2
                a = slope2 * a
                row = pl.ds(pl.multiple_of(c * rows + (2 * jj + k) * SEGS, SEGS), SEGS)
                run_ref[0, row, :] = a
                run_ref[1, row, :] = b
            out.append((state, a, b))
        return tuple(out)

    one, zero = jnp.ones((SEGS, width), F32), jnp.zeros((SEGS, width), F32)
    carry = tuple((enter[c * SEGS : (c + 1) * SEGS, :], one, zero) for c in range(chunks))
    carry = pair(0, carry, True)
    carry = lax.fori_loop(1, seg // 2, lambda jj, c: pair(jj, c, False), carry)
    for c in range(chunks):
        maps_ref[0, c * SEGS : (c + 1) * SEGS, :] = carry[c][1]
        maps_ref[1, c * SEGS : (c + 1) * SEGS, :] = carry[c][2]
    ta, tb = compose_rows(maps_ref, chunks * SEGS, jnp.ones((1, width), F32), jnp.zeros((1, width), F32))
    for i in range(peers):
        total_ref[i, 0:1, :] = ta
        total_ref[i, 1:2, :] = tb


def bend_all(place, gates, maps, peer_maps, gain, start):
    chunks = len(gates)
    peers = peer_maps.shape[0]
    _, rows, width = gates[0].shape
    tn = tile_of(width, 256)
    row_spec = pl.BlockSpec((1, tn), lambda n, p: (0, n))
    return pl.pallas_call(
        functools.partial(bend_kernel, chunks, peers),
        out_shape=[
            jax.ShapeDtypeStruct((2, chunks * rows, width), F32),
            jax.ShapeDtypeStruct((2, chunks * SEGS, width), F32),
            jax.ShapeDtypeStruct((peers, 2, width), F32),
        ],
        grid_spec=pltpu.PrefetchScalarGridSpec(
            num_scalar_prefetch=1,
            grid=(width // tn,),
            in_specs=[pl.BlockSpec((2, rows, tn), lambda n, p: (0, 0, n))] * chunks
            + [pl.BlockSpec((2, SEGS, tn), lambda n, p: (0, 0, n))] * chunks
            + [pl.BlockSpec((peers, 2, tn), lambda n, p: (0, 0, n)), row_spec, row_spec],
            out_specs=[
                pl.BlockSpec((2, chunks * rows, tn), lambda n, p: (0, 0, n)),
                pl.BlockSpec((2, chunks * SEGS, tn), lambda n, p: (0, 0, n)),
                pl.BlockSpec((peers, 2, tn), lambda n, p: (0, 0, n)),
            ],
            scratch_shapes=[pltpu.VMEM((chunks * SEGS, tn), F32)],
        ),
        compiler_params=params(),
        cost_estimate=cost(
            40 * chunks * rows * width, 12 * chunks * rows * width, 5 * chunks * rows * width
        ),
        name="bend",
    )(place, *gates, *maps, peer_maps, gain, start)


def state_kernel(chunk, peers, place, run_ref, maps_ref, peer_ref, start_ref, out_ref, enter, flat):
    rows, width = out_ref.shape
    seg = rows // SEGS
    state = entering_state(place, peer_ref, start_ref[...], peers)
    for k in range((chunk + 1) * SEGS):
        if k >= chunk * SEGS:
            enter[k - chunk * SEGS : k - chunk * SEGS + 1, :] = state
        state = maps_ref[0, k : k + 1, :] * state + maps_ref[1, k : k + 1, :]
    entered = enter[...]

    def step(j, carry):
        row = pl.ds(pl.multiple_of(j * SEGS, SEGS), SEGS)
        now = run_ref[0, row, :] * entered + run_ref[1, row, :]
        for l in range(width // LANES):
            flat[l, pl.ds(j, SEGS, stride=seg), :] = now[:, l * LANES : (l + 1) * LANES]
        return carry

    lax.fori_loop(0, seg, step, 0, unroll=4)
    for l in range(width // LANES):
        out_ref[:, l * LANES : (l + 1) * LANES] = flat[l].astype(BF16)


def state_chunk(place, run, maps, peer_maps, start, rows, chunk):
    width = run.shape[2]
    peers = peer_maps.shape[0]
    segs = maps.shape[1]
    tn = tile_of(width, 256)
    return pl.pallas_call(
        functools.partial(state_kernel, chunk, peers),
        out_shape=jax.ShapeDtypeStruct((rows, width), BF16),
        grid_spec=pltpu.PrefetchScalarGridSpec(
            num_scalar_prefetch=1,
            grid=(width // tn,),
            in_specs=[
                pl.BlockSpec((2, rows, tn), lambda n, p: (0, chunk, n)),
                pl.BlockSpec((2, segs, tn), lambda n, p: (0, 0, n)),
                pl.BlockSpec((peers, 2, tn), lambda n, p: (0, 0, n)),
                pl.BlockSpec((1, tn), lambda n, p: (0, n)),
            ],
            out_specs=pl.BlockSpec((rows, tn), lambda n, p: (0, n)),
            scratch_shapes=[pltpu.VMEM((SEGS, tn), F32), pltpu.VMEM((tn // LANES, rows, LANES), F32)],
        ),
        compiler_params=params(),
        cost_estimate=cost(2 * rows * width, 10 * rows * width),
    )(place, run, maps, peer_maps, start)


def mix_kernel(groups, group, pieces, peers, place, *refs):
    count = groups * group
    blocks = refs[:count]
    weights = refs[count : count + peers * pieces]
    out_ref, states = refs[-2:]
    rows, depth = blocks[0].shape
    lines_of = weights[0].shape[0]

    @pl.when(pl.program_id(0) == 0)
    def _():
        for c in range(groups):
            for d in range(group):
                deep = pl.ds(pl.multiple_of((place[0] ^ d) * depth, depth), depth)
                states[c * rows : (c + 1) * rows, deep] = blocks[c * group + d][...]

    outer = peers // 2
    total = None
    for s in range(outer):
        source = lax.rem(place[1] // 2 + outer - s, outer)
        for i in range(2):
            owner = source * 2 + (lax.rem(place[1], 2) ^ i)
            for p in range(pieces):
                deep = pl.ds(pl.multiple_of((owner * pieces + p) * lines_of, lines_of), lines_of)
                w_ref = weights[(s * 2 + i) * pieces + p]
                part = jnp.dot(states[:, deep], w_ref[...], preferred_element_type=F32)
                total = part if total is None else total + part
    out_ref[...] = total.astype(BF16)


def mix_rows(place, blocks, weights, whole, first, total_rows, pieces):
    groups, group = len(blocks), len(blocks[0])
    rows, depth = blocks[0][0].shape
    lines_of, width = weights[0].shape
    peers = len(weights) // pieces
    tn = tile_of(width, 256)
    here = groups * rows
    args = [place] + [b for g in blocks for b in g] + list(weights)
    in_specs = [pl.BlockSpec((rows, depth), lambda n, p: (0, 0))] * (groups * group)
    in_specs += [pl.BlockSpec((lines_of, tn), lambda n, p: (0, n))] * len(weights)
    aliases = {}
    if whole is not None:
        aliases = {len(args): 0}
        args.append(whole)
        in_specs.append(pl.BlockSpec(memory_space=pl.ANY))
    return pl.pallas_call(
        functools.partial(mix_kernel, groups, group, pieces, peers),
        out_shape=jax.ShapeDtypeStruct((total_rows, width), BF16),
        grid_spec=pltpu.PrefetchScalarGridSpec(
            num_scalar_prefetch=1,
            grid=(width // tn,),
            in_specs=in_specs,
            out_specs=pl.BlockSpec((here, tn), lambda n, p: (first // here, n)),
            scratch_shapes=[pltpu.VMEM((here, group * depth), BF16)],
        ),
        input_output_aliases=aliases,
        compiler_params=params(),
        cost_estimate=cost(
            2 * here * group * depth * width, 2 * group * depth * (width + here) + 2 * here * width
        ),
    )(*args)


EARLY = 5
CHUNKS = 4


def pieces_of(lines_of):
    return 2 if lines_of % (4 * LANES) == 0 else 1


class Ring:
    def __init__(self, w_output):
        self.peers = lax.axis_size("ctx")
        self.outer = self.peers // 2
        self.pieces = pieces_of(w_output.shape[0])
        lines_of = w_output.shape[0] // self.pieces
        self.held = {}
        for p in range(self.pieces):
            self.held[0, 0, p] = w_output[p * lines_of : (p + 1) * lines_of]

    def ring_step(self, n, gate=None):
        s, p = n // self.pieces + 1, n % self.pieces
        block = self.held[s - 1, 0, p]
        if gate is not None:
            block, _ = lax.optimization_barrier((block, gate))
        route = [(i, (i + 2) % self.peers) for i in range(self.peers)]
        self.held[s, 0, p] = lax.ppermute(block, "ctx", route)

    def swap_step(self, n, gate=None):
        s, p = n // self.pieces, n % self.pieces
        block = self.held[s, 0, p]
        if gate is not None:
            block, _ = lax.optimization_barrier((block, gate))
        self.held[s, 1, p] = swap(block, "ctx", 1)

    def run(self, gate):
        rings, swaps = (self.outer - 1) * self.pieces, self.outer * self.pieces
        for n in range(max(rings, swaps)):
            g = gate if n >= EARLY else None
            if n < rings:
                self.ring_step(n, g)
            if n < swaps:
                self.swap_step(n, g)

    def blocks(self):
        steps = [(s, i) for s in range(self.outer) for i in range(2)]
        return [self.held[s, i, p] for s, i in steps for p in range(self.pieces)]


def layer(tokens, w_input, w_output, bias_update, bias_cand, recur_gain, start_state):
    peers = lax.axis_size("ctx")
    group = lax.axis_size("ch")
    half = group // 2
    total_rows = tokens.shape[0]
    chunks = CHUNKS
    rows = total_rows // chunks
    place = jnp.stack([lax.axis_index("ch"), lax.axis_index("ctx")]).astype(jnp.int32)
    biases = jnp.stack([bias_update, bias_cand], axis=0)
    gain = recur_gain[None, :]
    start = start_state[None, :]

    far = []
    rest = tokens
    for c in range(chunks):
        piece = rest[c * rows : (c + 1) * rows]
        rest, piece = lax.optimization_barrier((rest, piece))
        far.append([swap(piece, "ch", half)])
    near = [tokens]
    for d in range(1, half):
        near.append(swap(tokens, "ch", d))
    for c in range(chunks):
        for d in range(1, half):
            far[c].append(swap(far[c][0], "ch", d))

    partial = near_product(place, near, w_input)
    gates, maps = [], []
    for c in range(chunks):
        last = c == chunks - 1
        out = gate_chunk(
            place, far[c], partial, w_input, biases, gain, start, maps if last else [], c, last, peers
        )
        gates.append(out[0])
        maps.append(out[1])
    peer_maps = lax.all_to_all(out[2], "ctx", 0, 0, tiled=True)
    run, run_maps, totals = bend_all(place, gates, maps, peer_maps, gain, start)
    peer_maps = lax.all_to_all(totals, "ctx", 0, 0, tiled=True)
    ring = Ring(w_output)
    ring.run(peer_maps)

    blocks = []
    for c in range(chunks):
        own = state_chunk(place, run, run_maps, peer_maps, start, rows, c)
        across = swap(own, "ch", half)
        blocks.append([own, across])
    for c in range(chunks):
        own, across = blocks[c]
        lows, highs = [own], [across]
        for d in range(1, half):
            lows.append(swap(own, "ch", d))
            highs.append(swap(across, "ch", d))
        blocks[c] = lows + highs
    weights = ring.blocks()
    mixed = None
    split = chunks - 1 if chunks > 1 else chunks
    mixed = mix_rows(place, blocks[:split], weights, None, 0, total_rows, ring.pieces)
    if split < chunks:
        mixed = mix_rows(
            place, blocks[split:], weights, mixed, split * rows, total_rows, ring.pieces
        )
    return mixed


def solution(mesh):
    return jax.shard_map(
        layer,
        mesh=mesh,
        in_specs=(
            P("ctx", "ch"),
            P(None, None, "ch"),
            P("ctx", "ch"),
            P("ch"),
            P("ch"),
            P("ch"),
            P("ch"),
        ),
        out_specs=P("ctx", "ch"),
        check_vma=False,
    )
```

```python
import functools
import math

import jax
import jax.numpy as jnp
from jax import lax
from jax.experimental import pallas as pl
from jax.experimental.pallas import tpu as pltpu
from jax.sharding import PartitionSpec as P


SEGS = 8
LANES = 128
F32 = jnp.float32
BF16 = jnp.bfloat16
MIB = 1024 * 1024


def swap(block, axis, bits):
    return lax.ppermute(block, axis, [(i, i ^ bits) for i in range(lax.axis_size(axis))])


def tile_of(width, most):
    return math.gcd(width, most)


def params(mib):
    return pltpu.CompilerParams(vmem_limit_bytes=mib * MIB)


def cost(flops, nbytes, trans=0):
    return pl.CostEstimate(flops=int(flops), bytes_accessed=int(nbytes), transcendentals=int(trans))


def near_kernel(half, place, *refs):
    blocks = refs[:half]
    w_ref, out_ref = refs[half:]
    depth = blocks[0].shape[1]
    slot = lax.rem(place[0], half)
    total = None
    for d in range(half):
        deep = pl.ds(pl.multiple_of((slot ^ d) * depth, depth), depth)
        part = jnp.dot(blocks[d][...], w_ref[0, deep, :], preferred_element_type=F32)
        total = part if total is None else total + part
    out_ref[0] = total


def near_product(place, blocks, weights):
    half = len(blocks)
    rows, depth = blocks[0].shape
    gates, _, width = weights.shape
    tn = tile_of(width, 512)
    spec = pl.BlockSpec((rows, depth), lambda g, n, p: (0, 0))
    return pl.pallas_call(
        functools.partial(near_kernel, half),
        out_shape=jax.ShapeDtypeStruct((gates, rows, width), F32),
        grid_spec=pltpu.PrefetchScalarGridSpec(
            num_scalar_prefetch=1,
            grid=(gates, width // tn),
            in_specs=[spec] * half
            + [pl.BlockSpec((1, half * depth, tn), lambda g, n, p: (g, p[0] // half, n))],
            out_specs=pl.BlockSpec((1, rows, tn), lambda g, n, p: (g, 0, n)),
        ),
        compiler_params=params(24),
        cost_estimate=cost(
            2 * gates * rows * half * depth * width,
            gates * width * (half * depth * 2 + rows * 4) + half * rows * depth * 2,
        ),
    )(place, *blocks, weights)


def compose_rows(maps, count, a, b):
    for k in range(count):
        slope = maps[0, k : k + 1, :]
        shift = maps[1, k : k + 1, :]
        b = slope * b + shift
        a = slope * a
    return a, b


def spread_rows(flat, g, lane, tiles, j, seg):
    parts = [flat[g, lane + l, pl.ds(j, SEGS, stride=seg), :] for l in range(tiles)]
    return jnp.concatenate(parts, axis=1)


def first_slopes(pre, cand, gain):
    update = jax.nn.sigmoid(pre)
    keep = 1.0 - update
    scaled = update * gain
    squashed = jnp.tanh(cand)
    slope = keep + (scaled - scaled * squashed * squashed)
    return update, keep, scaled, slope, update * squashed


def lead_row(place, start, shape):
    lead = lax.broadcasted_iota(jnp.int32, shape, 0) == 0
    return jnp.where(lead & (place[1] == 0), start, 0.0)


def around(update, keep, scaled, cand, gain, prev):
    squashed = jnp.tanh(cand + gain * prev)
    bend = scaled - scaled * squashed * squashed
    return keep + bend, update * squashed - bend * prev


def gate_kernel(half, chunk, rows, before, last, place, *refs):
    blocks = refs[:half]
    part_ref, w_ref, bias_ref, gain_ref, start_ref = refs[half : half + 5]
    earlier = refs[half + 5 : half + 5 + before]
    rest = refs[half + 5 + before :]
    if last:
        gates_ref, maps_ref, total_ref = rest[:3]
    else:
        gates_ref, maps_ref = rest[:2]
    lhs, wbuf, pbuf, acc, flat, lsem, wsem, psem = rest[-8:]
    depth = blocks[0].shape[1]
    width = gain_ref.shape[1]
    seg = rows // SEGS
    steps, lines_of = wbuf.shape[0], wbuf.shape[2]
    slot = lax.rem(place[0], half)
    base = ((place[0] // half) ^ 1) * (half * depth)

    def w_copy(k):
        lines = pl.ds(pl.multiple_of(base + k * lines_of, lines_of), lines_of)
        return pltpu.make_async_copy(w_ref.at[:, lines, :], wbuf.at[k], wsem.at[k])

    def l_copy(d):
        deep = pl.ds(pl.multiple_of((slot ^ d) * depth, depth), depth)
        return pltpu.make_async_copy(blocks[d], lhs.at[:, deep], lsem.at[d])

    p_copy = pltpu.make_async_copy(part_ref.at[:, chunk * rows : (chunk + 1) * rows, :], pbuf, psem)
    for d in range(half):
        l_copy(d).start()
    for k in range(steps):
        w_copy(k).start()
    p_copy.start()
    for d in range(half):
        l_copy(d).wait()

    def product(k, g):
        deep = pl.ds(pl.multiple_of(k * lines_of, lines_of), lines_of)
        return jnp.dot(lhs[:, deep], wbuf[k, g], preferred_element_type=F32)

    w_copy(0).wait()
    for g in range(2):
        acc[g] = product(0, g)

    def more(k, carry):
        w_copy(k).wait()
        for g in range(2):
            acc[g] += product(k, g)
        return carry

    lax.fori_loop(1, steps, more, 0)
    p_copy.wait()
    for g in range(2):
        for l in range(width // LANES):
            lanes = slice(l * LANES, (l + 1) * LANES)
            total = acc[g, :, lanes] + pbuf[g, :, lanes] + bias_ref[g : g + 1, lanes]
            flat[g, l] = total.astype(BF16).astype(F32)

    tiles = tile_of(width // LANES, 2)
    span = tiles * LANES

    def columns(n, carry_out):
        wide = pl.ds(pl.multiple_of(n * span, span), span)
        gain = jnp.broadcast_to(gain_ref[:, wide], (SEGS, span))

        def pair(jj, carry, first):
            a, b = carry
            held = ([], [])
            for k in range(2):
                j = 2 * jj + k
                pre = spread_rows(flat, 0, n * tiles, tiles, j, seg)
                cand = spread_rows(flat, 1, n * tiles, tiles, j, seg)
                held[0].append(pre)
                held[1].append(cand)
                update, keep, scaled, slope, offset = first_slopes(pre, cand, gain)
                if first and k == 0:
                    prev = lead_row(place, start_ref[:, wide], (SEGS, span))
                    slope, offset = around(update, keep, scaled, cand, gain, prev)
                b = slope * b + offset
                a = slope * a
            lines = pl.ds(pl.multiple_of(jj * 2 * SEGS, 2 * SEGS), 2 * SEGS)
            for g in range(2):
                gates_ref[g, lines, wide] = jnp.concatenate(held[g], axis=0).astype(BF16)
            return a, b

        carry = (jnp.ones((SEGS, span), F32), jnp.zeros((SEGS, span), F32))
        begin = 0
        if chunk == 0:
            carry = pair(0, carry, True)
            begin = 1
        a, b = lax.fori_loop(begin, seg // 2, lambda jj, c: pair(jj, c, False), carry)
        maps_ref[0, :, wide] = a
        maps_ref[1, :, wide] = b
        return carry_out

    lax.fori_loop(0, width // span, columns, 0)
    if last:
        ta, tb = jnp.ones((1, width), F32), jnp.zeros((1, width), F32)
        for maps in list(earlier) + [maps_ref]:
            ta, tb = compose_rows(maps, SEGS, ta, tb)
        for i in range(total_ref.shape[0]):
            total_ref[i, 0:1, :] = ta
            total_ref[i, 1:2, :] = tb


def gate_chunk(place, blocks, partial, weights, biases, gain, start, earlier, chunk, last, peers):
    half = len(blocks)
    rows, depth = blocks[0].shape
    gates, _, width = weights.shape
    lines_of = tile_of(half * depth, 512)
    steps = half * depth // lines_of
    anywhere = pl.BlockSpec(memory_space=pl.ANY)
    vmem = pl.BlockSpec(memory_space=pltpu.VMEM)
    out_shape = [
        jax.ShapeDtypeStruct((2, rows, width), BF16),
        jax.ShapeDtypeStruct((2, SEGS, width), F32),
    ]
    if last:
        out_shape.append(jax.ShapeDtypeStruct((peers, 2, width), F32))
    return pl.pallas_call(
        functools.partial(gate_kernel, half, chunk, rows, len(earlier), last),
        out_shape=out_shape,
        in_specs=[pl.BlockSpec(memory_space=pltpu.SMEM)]
        + [anywhere] * (half + 2)
        + [vmem] * (3 + len(earlier)),
        out_specs=[vmem] * len(out_shape),
        scratch_shapes=[
            pltpu.VMEM((rows, half * depth), BF16),
            pltpu.VMEM((steps, gates, lines_of, width), BF16),
            pltpu.VMEM((gates, rows, width), F32),
            pltpu.VMEM((gates, rows, width), F32),
            pltpu.VMEM((gates, width // LANES, rows, LANES), F32),
            pltpu.SemaphoreType.DMA((half,)),
            pltpu.SemaphoreType.DMA((steps,)),
            pltpu.SemaphoreType.DMA,
        ],
        compiler_params=params(24),
        cost_estimate=cost(
            2 * gates * rows * half * depth * width,
            gates * width * (half * depth * 2 + rows * 6) + half * rows * depth * 2,
            4 * rows * width,
        ),
    )(place, *blocks, partial, weights, biases, gain, start, *earlier)


def entering_state(place, peer_maps, start, peers):
    state = start
    for k in range(peers):
        moved = peer_maps[k, 0:1, :] * state + peer_maps[k, 1:2, :]
        state = jnp.where(place[1] > k, moved, state)
    return state


def enter_segments(maps_list, state, enter):
    for c, maps in enumerate(maps_list):
        for k in range(SEGS):
            enter[c * SEGS + k : c * SEGS + k + 1, :] = state
            state = maps[0, k : k + 1, :] * state + maps[1, k : k + 1, :]


def bend_kernel(chunks, peers, place, *refs):
    gates = refs[:chunks]
    maps = refs[chunks : 2 * chunks]
    peer_ref, gain_ref, start_ref, run_ref, maps_ref, total_ref, enter = refs[2 * chunks :]
    rows, span = gates[0].shape[1:]
    width = gain_ref.shape[1]
    seg = rows // SEGS
    n = pl.program_id(0)

    @pl.when(n == 0)
    def _():
        enter_segments(maps, entering_state(place, peer_ref, start_ref[...], peers), enter)

    wide = pl.ds(pl.multiple_of(n * span, span), span)
    gain = jnp.broadcast_to(gain_ref[:, wide], (SEGS, span))

    def pair(jj, carry, first):
        lines = pl.ds(pl.multiple_of(jj * 2 * SEGS, 2 * SEGS), 2 * SEGS)
        out = []
        for c in range(chunks):
            state, a, b = carry[c]
            pre2 = gates[c][0, lines, :].astype(F32)
            cand2 = gates[c][1, lines, :].astype(F32)
            for k in range(2):
                pre = pre2[k * SEGS : (k + 1) * SEGS]
                cand = cand2[k * SEGS : (k + 1) * SEGS]
                update, keep, scaled, slope, offset = first_slopes(pre, cand, gain)
                if first and k == 0 and c == 0:
                    prev = lead_row(place, start_ref[:, wide], (SEGS, span))
                    slope, offset = around(update, keep, scaled, cand, gain, prev)
                slope2, offset2 = around(update, keep, scaled, cand, gain, state)
                state = slope * state + offset
                b = slope2 * b + offset2
                a = slope2 * a
                row = pl.ds(pl.multiple_of(c * rows + (2 * jj + k) * SEGS, SEGS), SEGS)
                run_ref[0, row, :] = a
                run_ref[1, row, :] = b
            out.append((state, a, b))
        return tuple(out)

    one, zero = jnp.ones((SEGS, span), F32), jnp.zeros((SEGS, span), F32)
    carry = tuple((enter[c * SEGS : (c + 1) * SEGS, wide], one, zero) for c in range(chunks))
    carry = pair(0, carry, True)
    carry = lax.fori_loop(1, seg // 2, lambda jj, c: pair(jj, c, False), carry)
    for c in range(chunks):
        maps_ref[0, c * SEGS : (c + 1) * SEGS, wide] = carry[c][1]
        maps_ref[1, c * SEGS : (c + 1) * SEGS, wide] = carry[c][2]

    @pl.when(n == pl.num_programs(0) - 1)
    def _():
        ta, tb = jnp.ones((1, width), F32), jnp.zeros((1, width), F32)
        ta, tb = compose_rows(maps_ref, chunks * SEGS, ta, tb)
        for i in range(peers):
            total_ref[i, 0:1, :] = ta
            total_ref[i, 1:2, :] = tb


def bend_all(place, gates, maps, peer_maps, gain, start):
    chunks = len(gates)
    peers = peer_maps.shape[0]
    _, rows, width = gates[0].shape
    tn = tile_of(width, 256)
    row_spec = pl.BlockSpec((1, width), lambda n, p: (0, 0))
    total_spec = pl.BlockSpec((peers, 2, width), lambda n, p: (0, 0, 0))
    return pl.pallas_call(
        functools.partial(bend_kernel, chunks, peers),
        out_shape=[
            jax.ShapeDtypeStruct((2, chunks * rows, width), F32),
            jax.ShapeDtypeStruct((2, chunks * SEGS, width), F32),
            jax.ShapeDtypeStruct((peers, 2, width), F32),
        ],
        grid_spec=pltpu.PrefetchScalarGridSpec(
            num_scalar_prefetch=1,
            grid=(width // tn,),
            in_specs=[pl.BlockSpec((2, rows, tn), lambda n, p: (0, 0, n))] * chunks
            + [pl.BlockSpec((2, SEGS, width), lambda n, p: (0, 0, 0))] * chunks
            + [total_spec, row_spec, row_spec],
            out_specs=[
                pl.BlockSpec((2, chunks * rows, tn), lambda n, p: (0, 0, n)),
                pl.BlockSpec((2, chunks * SEGS, width), lambda n, p: (0, 0, 0)),
                total_spec,
            ],
            scratch_shapes=[pltpu.VMEM((chunks * SEGS, width), F32)],
        ),
        compiler_params=params(16),
        cost_estimate=cost(
            40 * chunks * rows * width, 12 * chunks * rows * width, 5 * chunks * rows * width
        ),
        name="bend",
    )(place, *gates, *maps, peer_maps, gain, start)


def state_kernel(chunk, peers, place, run_ref, maps_ref, peer_ref, start_ref, out_ref, enter, flat):
    rows, width = out_ref.shape
    seg = rows // SEGS
    state = entering_state(place, peer_ref, start_ref[...], peers)
    for k in range((chunk + 1) * SEGS):
        if k >= chunk * SEGS:
            enter[k - chunk * SEGS : k - chunk * SEGS + 1, :] = state
        state = maps_ref[0, k : k + 1, :] * state + maps_ref[1, k : k + 1, :]
    entered = enter[...]

    def step(j, carry):
        row = pl.ds(pl.multiple_of(j * SEGS, SEGS), SEGS)
        now = run_ref[0, row, :] * entered + run_ref[1, row, :]
        for l in range(width // LANES):
            flat[l, pl.ds(j, SEGS, stride=seg), :] = now[:, l * LANES : (l + 1) * LANES]
        return carry

    lax.fori_loop(0, seg, step, 0, unroll=4)
    for l in range(width // LANES):
        out_ref[:, l * LANES : (l + 1) * LANES] = flat[l].astype(BF16)


def state_chunk(place, run, maps, peer_maps, start, rows, chunk):
    width = run.shape[2]
    peers = peer_maps.shape[0]
    segs = maps.shape[1]
    tn = tile_of(width, 1024)
    return pl.pallas_call(
        functools.partial(state_kernel, chunk, peers),
        out_shape=jax.ShapeDtypeStruct((rows, width), BF16),
        grid_spec=pltpu.PrefetchScalarGridSpec(
            num_scalar_prefetch=1,
            grid=(width // tn,),
            in_specs=[
                pl.BlockSpec((2, rows, tn), lambda n, p: (0, chunk, n)),
                pl.BlockSpec((2, segs, tn), lambda n, p: (0, 0, n)),
                pl.BlockSpec((peers, 2, tn), lambda n, p: (0, 0, n)),
                pl.BlockSpec((1, tn), lambda n, p: (0, n)),
            ],
            out_specs=pl.BlockSpec((rows, tn), lambda n, p: (0, n)),
            scratch_shapes=[pltpu.VMEM((SEGS, tn), F32), pltpu.VMEM((tn // LANES, rows, LANES), F32)],
        ),
        compiler_params=params(12),
        cost_estimate=cost(2 * rows * width, 10 * rows * width),
    )(place, run, maps, peer_maps, start)


def mix_kernel(groups, group, pieces, peers, place, *refs):
    count = groups * group
    blocks = refs[:count]
    weights = refs[count : count + peers * pieces]
    out_ref, lhs, wbuf, acc, lsem, wsem = refs[-6:]
    rows, depth = blocks[0].shape
    lines_of = weights[0].shape[0]
    outer = peers // 2

    def w_copy(n, p):
        w_ref = weights[n * pieces + p]
        dst = wbuf.at[n, p * lines_of : (p + 1) * lines_of, :]
        return pltpu.make_async_copy(w_ref, dst, wsem.at[n, p])

    def l_copy(c, d):
        deep = pl.ds(pl.multiple_of((place[0] ^ d) * depth, depth), depth)
        dst = lhs.at[c * rows : (c + 1) * rows, deep]
        return pltpu.make_async_copy(blocks[c * group + d], dst, lsem.at[c, d])

    for c in range(groups):
        for d in range(group):
            l_copy(c, d).start()
    for n in range(peers):
        for p in range(pieces):
            w_copy(n, p).start()
    for c in range(groups):
        for d in range(group):
            l_copy(c, d).wait()
    span = lines_of * pieces
    for n in range(peers):
        source = lax.rem(place[1] // 2 + outer - n // 2, outer)
        owner = source * 2 + (lax.rem(place[1], 2) ^ (n % 2))
        deep = pl.ds(pl.multiple_of(owner * span, span), span)
        for p in range(pieces):
            w_copy(n, p).wait()
        part = jnp.dot(lhs[:, deep], wbuf[n], preferred_element_type=F32)
        if n == 0:
            acc[...] = part
        elif n < peers - 1:
            acc[...] += part
        else:
            out_ref[...] = (acc[...] + part).astype(BF16)


def mix_rows(place, blocks, weights, whole, first, total_rows, pieces):
    groups, group = len(blocks), len(blocks[0])
    rows, depth = blocks[0][0].shape
    lines_of, width = weights[0].shape
    peers = len(weights) // pieces
    here = groups * rows
    anywhere = pl.BlockSpec(memory_space=pl.ANY)
    args = [place] + [b for g in blocks for b in g] + list(weights)
    in_specs = [anywhere] * (groups * group + len(weights))
    aliases = {}
    if whole is not None:
        aliases = {len(args): 0}
        args.append(whole)
        in_specs.append(anywhere)
    return pl.pallas_call(
        functools.partial(mix_kernel, groups, group, pieces, peers),
        out_shape=jax.ShapeDtypeStruct((total_rows, width), BF16),
        grid_spec=pltpu.PrefetchScalarGridSpec(
            num_scalar_prefetch=1,
            grid=(1,),
            in_specs=in_specs,
            out_specs=pl.BlockSpec((here, width), lambda n, p: (first // here, 0)),
            scratch_shapes=[
                pltpu.VMEM((here, group * depth), BF16),
                pltpu.VMEM((peers, lines_of * pieces, width), BF16),
                pltpu.VMEM((here, width), F32),
                pltpu.SemaphoreType.DMA((groups, group)),
                pltpu.SemaphoreType.DMA((peers, pieces)),
            ],
        ),
        input_output_aliases=aliases,
        compiler_params=params(40 if peers <= 8 else 62),
        cost_estimate=cost(
            2 * here * group * depth * width, 2 * group * depth * (width + here) + 2 * here * width
        ),
    )(*args)


EARLY = 5
CHUNKS = 4


def pieces_of(lines_of):
    return 2 if lines_of % (4 * LANES) == 0 else 1


class Ring:
    def __init__(self, w_output):
        self.peers = lax.axis_size("ctx")
        self.outer = self.peers // 2
        self.pieces = pieces_of(w_output.shape[0])
        lines_of = w_output.shape[0] // self.pieces
        self.held = {}
        for p in range(self.pieces):
            self.held[0, 0, p] = w_output[p * lines_of : (p + 1) * lines_of]

    def ring_step(self, n, gate=None):
        s, p = n // self.pieces + 1, n % self.pieces
        block = self.held[s - 1, 0, p]
        if gate is not None:
            block, _ = lax.optimization_barrier((block, gate))
        route = [(i, (i + 2) % self.peers) for i in range(self.peers)]
        self.held[s, 0, p] = lax.ppermute(block, "ctx", route)

    def swap_step(self, n, gate=None):
        s, p = n // self.pieces, n % self.pieces
        block = self.held[s, 0, p]
        if gate is not None:
            block, _ = lax.optimization_barrier((block, gate))
        self.held[s, 1, p] = swap(block, "ctx", 1)

    def run(self, gate):
        rings, swaps = (self.outer - 1) * self.pieces, self.outer * self.pieces
        for n in range(max(rings, swaps)):
            g = gate if n >= EARLY else None
            if n < rings:
                self.ring_step(n, g)
            if n < swaps:
                self.swap_step(n, g)

    def blocks(self):
        steps = [(s, i) for s in range(self.outer) for i in range(2)]
        return [self.held[s, i, p] for s, i in steps for p in range(self.pieces)]


def layer(tokens, w_input, w_output, bias_update, bias_cand, recur_gain, start_state):
    peers = lax.axis_size("ctx")
    group = lax.axis_size("ch")
    half = group // 2
    total_rows = tokens.shape[0]
    chunks = CHUNKS
    rows = total_rows // chunks
    place = jnp.stack([lax.axis_index("ch"), lax.axis_index("ctx")]).astype(jnp.int32)
    biases = jnp.stack([bias_update, bias_cand], axis=0)
    gain = recur_gain[None, :]
    start = start_state[None, :]

    far = []
    rest = tokens
    for c in range(chunks):
        piece = rest[c * rows : (c + 1) * rows]
        rest, piece = lax.optimization_barrier((rest, piece))
        far.append([swap(piece, "ch", half)])
    near = [tokens]
    for d in range(1, half):
        near.append(swap(tokens, "ch", d))
    for c in range(chunks):
        for d in range(1, half):
            far[c].append(swap(far[c][0], "ch", d))

    partial = near_product(place, near, w_input)
    gates, maps = [], []
    for c in range(chunks):
        last = c == chunks - 1
        out = gate_chunk(
            place, far[c], partial, w_input, biases, gain, start, maps if last else [], c, last, peers
        )
        gates.append(out[0])
        maps.append(out[1])
    peer_maps = lax.all_to_all(out[2], "ctx", 0, 0, tiled=True)
    run, run_maps, totals = bend_all(place, gates, maps, peer_maps, gain, start)
    peer_maps = lax.all_to_all(totals, "ctx", 0, 0, tiled=True)
    ring = Ring(w_output)
    ring.run(peer_maps)

    blocks = []
    for c in range(chunks):
        own = state_chunk(place, run, run_maps, peer_maps, start, rows, c)
        across = swap(own, "ch", half)
        blocks.append([own, across])
    for c in range(chunks):
        own, across = blocks[c]
        lows, highs = [own], [across]
        for d in range(1, half):
            lows.append(swap(own, "ch", d))
            highs.append(swap(across, "ch", d))
        blocks[c] = lows + highs
    weights = ring.blocks()
    mixed = None
    split = chunks - 1 if chunks > 1 else chunks
    mixed = mix_rows(place, blocks[:split], weights, None, 0, total_rows, ring.pieces)
    if split < chunks:
        mixed = mix_rows(
            place, blocks[split:], weights, mixed, split * rows, total_rows, ring.pieces
        )
    return mixed


def solution(mesh):
    return jax.shard_map(
        layer,
        mesh=mesh,
        in_specs=(
            P("ctx", "ch"),
            P(None, None, "ch"),
            P("ctx", "ch"),
            P("ch"),
            P("ch"),
            P("ch"),
            P("ch"),
        ),
        out_specs=P("ctx", "ch"),
        check_vma=False,
    )
```

```python
import functools
import math

import jax
import jax.numpy as jnp
from jax import lax
from jax.experimental import pallas as pl
from jax.experimental.pallas import tpu as pltpu
from jax.sharding import PartitionSpec as P


SEGS = 8
LANES = 128
F32 = jnp.float32
BF16 = jnp.bfloat16
MIB = 1024 * 1024


def swap(block, axis, bits):
    return lax.ppermute(block, axis, [(i, i ^ bits) for i in range(lax.axis_size(axis))])


def tile_of(width, most):
    return math.gcd(width, most)


def params(mib):
    return pltpu.CompilerParams(vmem_limit_bytes=mib * MIB)


def cost(flops, nbytes, trans=0):
    return pl.CostEstimate(flops=int(flops), bytes_accessed=int(nbytes), transcendentals=int(trans))


def near_kernel(half, tiles, place, *refs):
    blocks = refs[:half]
    w_ref, out_ref, lhs, wbuf, lsem, wsem = refs[half:]
    depth = blocks[0].shape[1]
    span = wbuf.shape[2]
    slot = lax.rem(place[0], half)
    base = (place[0] // half) * (half * depth)

    def w_copy(n):
        lines = pl.ds(pl.multiple_of(base, half * depth), half * depth)
        wide = pl.ds(pl.multiple_of(lax.rem(n, tiles) * span, span), span)
        return pltpu.make_async_copy(w_ref.at[n // tiles, lines, wide], wbuf.at[n], wsem.at[n])

    def l_copy(d):
        deep = pl.ds(pl.multiple_of((slot ^ d) * depth, depth), depth)
        return pltpu.make_async_copy(blocks[d], lhs.at[:, deep], lsem.at[d])

    count = wbuf.shape[0]
    w_copy(0).start()
    for d in range(half):
        l_copy(d).start()
    for n in range(1, count):
        w_copy(n).start()
    for d in range(half):
        l_copy(d).wait()

    def body(n, carry):
        w_copy(n).wait()
        wide = pl.ds(pl.multiple_of(lax.rem(n, tiles) * span, span), span)
        total = None
        for d in range(half):
            deep = slice(d * depth, (d + 1) * depth)
            part = jnp.dot(lhs[:, deep], wbuf[n, deep, :], preferred_element_type=F32)
            total = part if total is None else total + part
        out_ref[n // tiles, :, wide] = total
        return carry

    lax.fori_loop(0, count, body, 0)


def near_product(place, blocks, weights):
    half = len(blocks)
    rows, depth = blocks[0].shape
    gates, _, width = weights.shape
    span = tile_of(width, 512)
    tiles = width // span
    anywhere = pl.BlockSpec(memory_space=pl.ANY)
    return pl.pallas_call(
        functools.partial(near_kernel, half, tiles),
        out_shape=jax.ShapeDtypeStruct((gates, rows, width), F32),
        in_specs=[pl.BlockSpec(memory_space=pltpu.SMEM)]
        + [anywhere] * half
        + [pl.BlockSpec(memory_space=pltpu.HBM)],
        out_specs=pl.BlockSpec(memory_space=pltpu.VMEM),
        scratch_shapes=[
            pltpu.VMEM((rows, half * depth), BF16),
            pltpu.VMEM((gates * tiles, half * depth, span), BF16),
            pltpu.SemaphoreType.DMA((half,)),
            pltpu.SemaphoreType.DMA((gates * tiles,)),
        ],
        compiler_params=params(28),
        cost_estimate=cost(
            2 * gates * rows * half * depth * width,
            gates * width * (half * depth * 2 + rows * 4) + half * rows * depth * 2,
        ),
    )(place, *blocks, weights)


def split_kernel(sizes, src, *refs):
    outs, sem = refs[:-1], refs[-1]
    copies, first = [], 0
    for k, rows in enumerate(sizes):
        copies.append(pltpu.make_async_copy(src.at[first : first + rows, :], outs[k], sem.at[k]))
        first += rows
    for copy in copies:
        copy.start()
    for copy in copies:
        copy.wait()


def split_rows(array, sizes):
    vmem = pl.BlockSpec(memory_space=pltpu.VMEM)
    return pl.pallas_call(
        functools.partial(split_kernel, sizes),
        out_shape=[jax.ShapeDtypeStruct((rows, array.shape[1]), array.dtype) for rows in sizes],
        in_specs=[pl.BlockSpec(memory_space=pltpu.HBM)],
        out_specs=[vmem] * len(sizes),
        scratch_shapes=[pltpu.SemaphoreType.DMA((len(sizes),))],
        compiler_params=params(12),
        cost_estimate=cost(0, 4 * array.shape[0] * array.shape[1]),
        name="split",
    )(array)


def compose_rows(maps, count, a, b):
    for k in range(count):
        slope = maps[0, k : k + 1, :]
        shift = maps[1, k : k + 1, :]
        b = slope * b + shift
        a = slope * a
    return a, b


def spread_rows(flat, g, lane, tiles, j, seg):
    parts = [flat[g, lane + l, pl.ds(j, SEGS, stride=seg), :] for l in range(tiles)]
    return jnp.concatenate(parts, axis=1)


def first_slopes(pre, cand, gain):
    update = jax.nn.sigmoid(pre)
    keep = 1.0 - update
    scaled = update * gain
    squashed = jnp.tanh(cand)
    slope = keep + (scaled - scaled * squashed * squashed)
    return update, keep, scaled, slope, update * squashed


def lead_row(place, start, shape):
    lead = lax.broadcasted_iota(jnp.int32, shape, 0) == 0
    return jnp.where(lead & (place[1] == 0), start, 0.0)


def around(update, keep, scaled, cand, gain, prev):
    squashed = jnp.tanh(cand + gain * prev)
    bend = scaled - scaled * squashed * squashed
    return keep + bend, update * squashed - bend * prev


def gate_kernel(half, chunk, first_row, rows, before, last, place, *refs):
    blocks = refs[:half]
    part_ref, w_ref, bias_ref, gain_ref, start_ref = refs[half : half + 5]
    earlier = refs[half + 5 : half + 5 + before]
    rest = refs[half + 5 + before :]
    if last:
        gates_ref, maps_ref, total_ref = rest[:3]
    else:
        gates_ref, maps_ref = rest[:2]
    lhs, wbuf, pbuf, acc, flat, lsem, wsem, psem = rest[-8:]
    depth = blocks[0].shape[1]
    width = gain_ref.shape[1]
    seg = rows // SEGS
    steps, lines_of = wbuf.shape[0], wbuf.shape[2]
    slot = lax.rem(place[0], half)
    base = ((place[0] // half) ^ 1) * (half * depth)

    def w_copy(k):
        lines = pl.ds(pl.multiple_of(base + k * lines_of, lines_of), lines_of)
        return pltpu.make_async_copy(w_ref.at[:, lines, :], wbuf.at[k], wsem.at[k])

    def l_copy(d):
        deep = pl.ds(pl.multiple_of((slot ^ d) * depth, depth), depth)
        return pltpu.make_async_copy(blocks[d], lhs.at[:, deep], lsem.at[d])

    p_copy = pltpu.make_async_copy(part_ref.at[:, first_row : first_row + rows, :], pbuf, psem)
    for d in range(half):
        l_copy(d).start()
    for k in range(steps):
        w_copy(k).start()
    p_copy.start()
    for d in range(half):
        l_copy(d).wait()

    def product(k, g):
        deep = pl.ds(pl.multiple_of(k * lines_of, lines_of), lines_of)
        return jnp.dot(lhs[:, deep], wbuf[k, g], preferred_element_type=F32)

    w_copy(0).wait()
    for g in range(2):
        acc[g] = product(0, g)

    def more(k, carry):
        w_copy(k).wait()
        for g in range(2):
            acc[g] += product(k, g)
        return carry

    lax.fori_loop(1, steps, more, 0)
    p_copy.wait()
    for g in range(2):
        for l in range(width // LANES):
            lanes = slice(l * LANES, (l + 1) * LANES)
            total = acc[g, :, lanes] + pbuf[g, :, lanes] + bias_ref[g : g + 1, lanes]
            flat[g, l] = total.astype(BF16).astype(F32)

    tiles = tile_of(width // LANES, 2)
    span = tiles * LANES

    def columns(n, carry_out):
        wide = pl.ds(pl.multiple_of(n * span, span), span)
        gain = jnp.broadcast_to(gain_ref[:, wide], (SEGS, span))

        def pair(jj, carry, first):
            a, b = carry
            held = ([], [])
            for k in range(2):
                j = 2 * jj + k
                pre = spread_rows(flat, 0, n * tiles, tiles, j, seg)
                cand = spread_rows(flat, 1, n * tiles, tiles, j, seg)
                held[0].append(pre)
                held[1].append(cand)
                update, keep, scaled, slope, offset = first_slopes(pre, cand, gain)
                if first and k == 0:
                    prev = lead_row(place, start_ref[:, wide], (SEGS, span))
                    slope, offset = around(update, keep, scaled, cand, gain, prev)
                b = slope * b + offset
                a = slope * a
            lines = pl.ds(pl.multiple_of(jj * 2 * SEGS, 2 * SEGS), 2 * SEGS)
            for g in range(2):
                gates_ref[g, lines, wide] = jnp.concatenate(held[g], axis=0).astype(BF16)
            return a, b

        carry = (jnp.ones((SEGS, span), F32), jnp.zeros((SEGS, span), F32))
        begin = 0
        if chunk == 0:
            carry = pair(0, carry, True)
            begin = 1
        a, b = lax.fori_loop(begin, seg // 2, lambda jj, c: pair(jj, c, False), carry)
        maps_ref[0, :, wide] = a
        maps_ref[1, :, wide] = b
        return carry_out

    lax.fori_loop(0, width // span, columns, 0)
    if last:
        ta, tb = jnp.ones((1, width), F32), jnp.zeros((1, width), F32)
        for maps in list(earlier) + [maps_ref]:
            ta, tb = compose_rows(maps, SEGS, ta, tb)
        for i in range(total_ref.shape[0]):
            total_ref[i, 0:1, :] = ta
            total_ref[i, 1:2, :] = tb


def gate_chunk(
    place, blocks, partial, weights, biases, gain, start, earlier, chunk, first_row, last, peers
):
    half = len(blocks)
    rows, depth = blocks[0].shape
    gates, _, width = weights.shape
    lines_of = tile_of(half * depth, 512)
    steps = half * depth // lines_of
    anywhere = pl.BlockSpec(memory_space=pl.ANY)
    vmem = pl.BlockSpec(memory_space=pltpu.VMEM)
    out_shape = [
        jax.ShapeDtypeStruct((2, rows, width), BF16),
        jax.ShapeDtypeStruct((2, SEGS, width), F32),
    ]
    if last:
        out_shape.append(jax.ShapeDtypeStruct((peers, 2, width), F32))
    return pl.pallas_call(
        functools.partial(gate_kernel, half, chunk, first_row, rows, len(earlier), last),
        out_shape=out_shape,
        in_specs=[pl.BlockSpec(memory_space=pltpu.SMEM)]
        + [anywhere] * (half + 1)
        + [pl.BlockSpec(memory_space=pltpu.HBM)]
        + [vmem] * (3 + len(earlier)),
        out_specs=[vmem] * len(out_shape),
        scratch_shapes=[
            pltpu.VMEM((rows, half * depth), BF16),
            pltpu.VMEM((steps, gates, lines_of, width), BF16),
            pltpu.VMEM((gates, rows, width), F32),
            pltpu.VMEM((gates, rows, width), F32),
            pltpu.VMEM((gates, width // LANES, rows, LANES), F32),
            pltpu.SemaphoreType.DMA((half,)),
            pltpu.SemaphoreType.DMA((steps,)),
            pltpu.SemaphoreType.DMA,
        ],
        compiler_params=params(32),
        cost_estimate=cost(
            2 * gates * rows * half * depth * width,
            gates * width * (half * depth * 2 + rows * 6) + half * rows * depth * 2,
            4 * rows * width,
        ),
    )(place, *blocks, partial, weights, biases, gain, start, *earlier)


def entering_state(place, peer_maps, start, peers):
    state = start
    for k in range(peers):
        moved = peer_maps[k, 0:1, :] * state + peer_maps[k, 1:2, :]
        state = jnp.where(place[1] > k, moved, state)
    return state


def enter_segments(maps_list, state, enter):
    for c, maps in enumerate(maps_list):
        for k in range(SEGS):
            enter[c * SEGS + k : c * SEGS + k + 1, :] = state
            state = maps[0, k : k + 1, :] * state + maps[1, k : k + 1, :]


def bend_kernel(chunks, peers, place, *refs):
    gates = refs[:chunks]
    maps = refs[chunks : 2 * chunks]
    peer_ref, gain_ref, start_ref, run_ref, maps_ref, total_ref, enter = refs[2 * chunks :]
    span = gates[0].shape[2]
    width = gain_ref.shape[1]
    heights = [g.shape[1] for g in gates]
    firsts = [sum(heights[:c]) for c in range(chunks)]
    least = min(heights)
    turns = least // SEGS // 2
    n = pl.program_id(0)

    @pl.when(n == 0)
    def _():
        enter_segments(maps, entering_state(place, peer_ref, start_ref[...], peers), enter)

    wide = pl.ds(pl.multiple_of(n * span, span), span)
    gain = jnp.broadcast_to(gain_ref[:, wide], (SEGS, span))

    def advance(c, jj, held, first):
        state, a, b = held
        lines = pl.ds(pl.multiple_of(jj * 2 * SEGS, 2 * SEGS), 2 * SEGS)
        pre2 = gates[c][0, lines, :].astype(F32)
        cand2 = gates[c][1, lines, :].astype(F32)
        for k in range(2):
            pre = pre2[k * SEGS : (k + 1) * SEGS]
            cand = cand2[k * SEGS : (k + 1) * SEGS]
            update, keep, scaled, slope, offset = first_slopes(pre, cand, gain)
            if first and k == 0:
                prev = lead_row(place, start_ref[:, wide], (SEGS, span))
                slope, offset = around(update, keep, scaled, cand, gain, prev)
            slope2, offset2 = around(update, keep, scaled, cand, gain, state)
            state = slope * state + offset
            b = slope2 * b + offset2
            a = slope2 * a
            row = pl.ds(pl.multiple_of(firsts[c] + (2 * jj + k) * SEGS, SEGS), SEGS)
            run_ref[0, row, :] = a
            run_ref[1, row, :] = b
        return state, a, b

    def pair(turn, carry, first):
        out = []
        for c in range(chunks):
            held = carry[c]
            times = heights[c] // least
            for r in range(times):
                held = advance(c, turn * times + r, held, first and c == 0 and r == 0)
            out.append(held)
        return tuple(out)

    one, zero = jnp.ones((SEGS, span), F32), jnp.zeros((SEGS, span), F32)
    carry = tuple((enter[c * SEGS : (c + 1) * SEGS, wide], one, zero) for c in range(chunks))
    carry = pair(0, carry, True)
    carry = lax.fori_loop(1, turns, lambda turn, c: pair(turn, c, False), carry)
    for c in range(chunks):
        maps_ref[0, c * SEGS : (c + 1) * SEGS, wide] = carry[c][1]
        maps_ref[1, c * SEGS : (c + 1) * SEGS, wide] = carry[c][2]

    @pl.when(n == pl.num_programs(0) - 1)
    def _():
        ta, tb = jnp.ones((1, width), F32), jnp.zeros((1, width), F32)
        ta, tb = compose_rows(maps_ref, chunks * SEGS, ta, tb)
        for i in range(peers):
            total_ref[i, 0:1, :] = ta
            total_ref[i, 1:2, :] = tb


def bend_all(place, gates, maps, peer_maps, gain, start):
    chunks = len(gates)
    peers = peer_maps.shape[0]
    width = gates[0].shape[2]
    total_rows = sum(g.shape[1] for g in gates)
    tn = tile_of(width, 256)
    row_spec = pl.BlockSpec((1, width), lambda n, p: (0, 0))
    total_spec = pl.BlockSpec((peers, 2, width), lambda n, p: (0, 0, 0))
    return pl.pallas_call(
        functools.partial(bend_kernel, chunks, peers),
        out_shape=[
            jax.ShapeDtypeStruct((2, total_rows, width), F32),
            jax.ShapeDtypeStruct((2, chunks * SEGS, width), F32),
            jax.ShapeDtypeStruct((peers, 2, width), F32),
        ],
        grid_spec=pltpu.PrefetchScalarGridSpec(
            num_scalar_prefetch=1,
            grid=(width // tn,),
            in_specs=[pl.BlockSpec((2, g.shape[1], tn), lambda n, p: (0, 0, n)) for g in gates]
            + [pl.BlockSpec((2, SEGS, width), lambda n, p: (0, 0, 0))] * chunks
            + [total_spec, row_spec, row_spec],
            out_specs=[
                pl.BlockSpec((2, total_rows, tn), lambda n, p: (0, 0, n)),
                pl.BlockSpec((2, chunks * SEGS, width), lambda n, p: (0, 0, 0)),
                total_spec,
            ],
            scratch_shapes=[pltpu.VMEM((chunks * SEGS, width), F32)],
        ),
        compiler_params=params(16),
        cost_estimate=cost(
            40 * total_rows * width, 12 * total_rows * width, 5 * total_rows * width
        ),
        name="bend",
    )(place, *gates, *maps, peer_maps, gain, start)


def state_kernel(chunk, peers, place, run_ref, maps_ref, peer_ref, start_ref, out_ref, enter, flat):
    rows, width = out_ref.shape
    seg = rows // SEGS
    state = entering_state(place, peer_ref, start_ref[...], peers)
    for k in range((chunk + 1) * SEGS):
        if k >= chunk * SEGS:
            enter[k - chunk * SEGS : k - chunk * SEGS + 1, :] = state
        state = maps_ref[0, k : k + 1, :] * state + maps_ref[1, k : k + 1, :]
    entered = enter[...]

    def step(j, carry):
        row = pl.ds(pl.multiple_of(j * SEGS, SEGS), SEGS)
        now = run_ref[0, row, :] * entered + run_ref[1, row, :]
        for l in range(width // LANES):
            flat[l, pl.ds(j, SEGS, stride=seg), :] = now[:, l * LANES : (l + 1) * LANES]
        return carry

    lax.fori_loop(0, seg, step, 0, unroll=4)
    for l in range(width // LANES):
        out_ref[:, l * LANES : (l + 1) * LANES] = flat[l].astype(BF16)


def state_chunk(place, run, maps, peer_maps, start, first_row, rows, chunk):
    width = run.shape[2]
    peers = peer_maps.shape[0]
    segs = maps.shape[1]
    tn = tile_of(width, 1024)
    return pl.pallas_call(
        functools.partial(state_kernel, chunk, peers),
        out_shape=jax.ShapeDtypeStruct((rows, width), BF16),
        grid_spec=pltpu.PrefetchScalarGridSpec(
            num_scalar_prefetch=1,
            grid=(width // tn,),
            in_specs=[
                pl.BlockSpec((2, rows, tn), lambda n, p: (0, first_row // rows, n)),
                pl.BlockSpec((2, segs, tn), lambda n, p: (0, 0, n)),
                pl.BlockSpec((peers, 2, tn), lambda n, p: (0, 0, n)),
                pl.BlockSpec((1, tn), lambda n, p: (0, n)),
            ],
            out_specs=pl.BlockSpec((rows, tn), lambda n, p: (0, n)),
            scratch_shapes=[pltpu.VMEM((SEGS, tn), F32), pltpu.VMEM((tn // LANES, rows, LANES), F32)],
        ),
        compiler_params=params(12),
        cost_estimate=cost(2 * rows * width, 10 * rows * width),
    )(place, run, maps, peer_maps, start)


def mix_kernel(groups, group, pieces, peers, place, *refs):
    count = groups * group
    blocks = refs[:count]
    weights = refs[count : count + peers * pieces]
    out_ref, lhs, wbuf, acc, lsem, wsem = refs[-6:]
    depth = blocks[0].shape[1]
    heights = [blocks[c * group].shape[0] for c in range(groups)]
    lines_of = weights[0].shape[0]
    outer = peers // 2

    def w_copy(n, p):
        w_ref = weights[n * pieces + p]
        dst = wbuf.at[n, p * lines_of : (p + 1) * lines_of, :]
        return pltpu.make_async_copy(w_ref, dst, wsem.at[n, p])

    def l_copy(c, d):
        deep = pl.ds(pl.multiple_of((place[0] ^ d) * depth, depth), depth)
        top = sum(heights[:c])
        dst = lhs.at[top : top + heights[c], deep]
        return pltpu.make_async_copy(blocks[c * group + d], dst, lsem.at[c, d])

    for c in range(groups):
        for d in range(group):
            l_copy(c, d).start()
    for n in range(peers):
        for p in range(pieces):
            w_copy(n, p).start()
    for c in range(groups):
        for d in range(group):
            l_copy(c, d).wait()
    span = lines_of * pieces
    for n in range(peers):
        source = lax.rem(place[1] // 2 + outer - n // 2, outer)
        owner = source * 2 + (lax.rem(place[1], 2) ^ (n % 2))
        deep = pl.ds(pl.multiple_of(owner * span, span), span)
        for p in range(pieces):
            w_copy(n, p).wait()
        part = jnp.dot(lhs[:, deep], wbuf[n], preferred_element_type=F32)
        if n == 0:
            acc[...] = part
        elif n < peers - 1:
            acc[...] += part
        else:
            out_ref[...] = (acc[...] + part).astype(BF16)


def mix_rows(place, blocks, weights, whole, first, total_rows, pieces):
    groups, group = len(blocks), len(blocks[0])
    depth = blocks[0][0].shape[1]
    lines_of, width = weights[0].shape
    peers = len(weights) // pieces
    here = sum(g[0].shape[0] for g in blocks)
    anywhere = pl.BlockSpec(memory_space=pl.ANY)
    args = [place] + [b for g in blocks for b in g] + list(weights)
    in_specs = [anywhere] * (groups * group + len(weights))
    aliases = {}
    if whole is not None:
        aliases = {len(args): 0}
        args.append(whole)
        in_specs.append(anywhere)
    return pl.pallas_call(
        functools.partial(mix_kernel, groups, group, pieces, peers),
        out_shape=jax.ShapeDtypeStruct((total_rows, width), BF16),
        grid_spec=pltpu.PrefetchScalarGridSpec(
            num_scalar_prefetch=1,
            grid=(1,),
            in_specs=in_specs,
            out_specs=pl.BlockSpec((here, width), lambda n, p: (first // here, 0)),
            scratch_shapes=[
                pltpu.VMEM((here, group * depth), BF16),
                pltpu.VMEM((peers, lines_of * pieces, width), BF16),
                pltpu.VMEM((here, width), F32),
                pltpu.SemaphoreType.DMA((groups, group)),
                pltpu.SemaphoreType.DMA((peers, pieces)),
            ],
        ),
        input_output_aliases=aliases,
        compiler_params=params(40 if peers <= 8 else 62),
        cost_estimate=cost(
            2 * here * group * depth * width, 2 * group * depth * (width + here) + 2 * here * width
        ),
    )(*args)


EARLY = 5
SHARES = (2, 1, 1)


def pieces_of(lines_of):
    return 2 if lines_of % (4 * LANES) == 0 else 1


class Ring:
    def __init__(self, w_output):
        self.peers = lax.axis_size("ctx")
        self.outer = self.peers // 2
        self.pieces = pieces_of(w_output.shape[0])
        lines_of = w_output.shape[0] // self.pieces
        self.held = {}
        for p in range(self.pieces):
            self.held[0, 0, p] = w_output[p * lines_of : (p + 1) * lines_of]

    def ring_step(self, n, gate=None):
        s, p = n // self.pieces + 1, n % self.pieces
        block = self.held[s - 1, 0, p]
        if gate is not None:
            block, _ = lax.optimization_barrier((block, gate))
        route = [(i, (i + 2) % self.peers) for i in range(self.peers)]
        self.held[s, 0, p] = lax.ppermute(block, "ctx", route)

    def swap_step(self, n, gate=None):
        s, p = n // self.pieces, n % self.pieces
        block = self.held[s, 0, p]
        if gate is not None:
            block, _ = lax.optimization_barrier((block, gate))
        self.held[s, 1, p] = swap(block, "ctx", 1)

    def run(self, gate):
        rings, swaps = (self.outer - 1) * self.pieces, self.outer * self.pieces
        for n in range(max(rings, swaps)):
            g = gate if n >= EARLY else None
            if n < rings:
                self.ring_step(n, g)
            if n < swaps:
                self.swap_step(n, g)

    def blocks(self):
        steps = [(s, i) for s in range(self.outer) for i in range(2)]
        return [self.held[s, i, p] for s, i in steps for p in range(self.pieces)]


def layer(tokens, w_input, w_output, bias_update, bias_cand, recur_gain, start_state):
    peers = lax.axis_size("ctx")
    group = lax.axis_size("ch")
    half = group // 2
    total_rows = tokens.shape[0]
    chunks = len(SHARES)
    sizes = [total_rows * share // sum(SHARES) for share in SHARES]
    firsts = [sum(sizes[:c]) for c in range(chunks)]
    place = jnp.stack([lax.axis_index("ch"), lax.axis_index("ctx")]).astype(jnp.int32)
    biases = jnp.stack([bias_update, bias_cand], axis=0)
    gain = recur_gain[None, :]
    start = start_state[None, :]

    far = []
    for piece in split_rows(tokens, sizes):
        far.append([swap(piece, "ch", half)])
    near = [tokens]
    for d in range(1, half):
        near.append(swap(tokens, "ch", d))
    for c in range(chunks):
        for d in range(1, half):
            far[c].append(swap(far[c][0], "ch", d))

    partial = near_product(place, near, w_input)
    gates, maps = [], []
    for c in range(chunks):
        last = c == chunks - 1
        out = gate_chunk(
            place,
            far[c],
            partial,
            w_input,
            biases,
            gain,
            start,
            maps if last else [],
            c,
            firsts[c],
            last,
            peers,
        )
        gates.append(out[0])
        maps.append(out[1])
    peer_maps = lax.all_to_all(out[2], "ctx", 0, 0, tiled=True)
    run, run_maps, totals = bend_all(place, gates, maps, peer_maps, gain, start)
    peer_maps = lax.all_to_all(totals, "ctx", 0, 0, tiled=True)
    ring = Ring(w_output)
    ring.run(peer_maps)

    blocks = []
    for c in range(chunks):
        own = state_chunk(place, run, run_maps, peer_maps, start, firsts[c], sizes[c], c)
        across = swap(own, "ch", half)
        blocks.append([own, across])
    for c in range(chunks):
        own, across = blocks[c]
        lows, highs = [own], [across]
        for d in range(1, half):
            lows.append(swap(own, "ch", d))
            highs.append(swap(across, "ch", d))
        blocks[c] = lows + highs
    weights = ring.blocks()
    mixed = None
    split = chunks - 1 if chunks > 1 else chunks
    mixed = mix_rows(place, blocks[:split], weights, None, 0, total_rows, ring.pieces)
    if split < chunks:
        mixed = mix_rows(
            place, blocks[split:], weights, mixed, firsts[split], total_rows, ring.pieces
        )
    return mixed


def solution(mesh):
    return jax.shard_map(
        layer,
        mesh=mesh,
        in_specs=(
            P("ctx", "ch"),
            P(None, None, "ch"),
            P("ctx", "ch"),
            P("ch"),
            P("ch"),
            P("ch"),
            P("ch"),
        ),
        out_specs=P("ctx", "ch"),
        check_vma=False,
    )
```

```python
import functools
import math

import jax
import jax.numpy as jnp
from jax import lax
from jax.experimental import pallas as pl
from jax.experimental.pallas import tpu as pltpu
from jax.sharding import PartitionSpec as P


SEGS = 8
LANES = 128
F32 = jnp.float32
BF16 = jnp.bfloat16
MIB = 1024 * 1024


def swap(block, axis, bits):
    return lax.ppermute(block, axis, [(i, i ^ bits) for i in range(lax.axis_size(axis))])


def tile_of(width, most):
    return math.gcd(width, most)


def params(mib):
    return pltpu.CompilerParams(vmem_limit_bytes=mib * MIB)


def cost(flops, nbytes, trans=0):
    return pl.CostEstimate(flops=int(flops), bytes_accessed=int(nbytes), transcendentals=int(trans))


def near_kernel(half, tiles, place, *refs):
    blocks = refs[:half]
    w_ref, out_ref, lhs, wbuf, lsem, wsem = refs[half:]
    depth = blocks[0].shape[1]
    span = wbuf.shape[2]
    slot = lax.rem(place[0], half)
    base = (place[0] // half) * (half * depth)

    def w_copy(n):
        lines = pl.ds(pl.multiple_of(base, half * depth), half * depth)
        wide = pl.ds(pl.multiple_of(lax.rem(n, tiles) * span, span), span)
        return pltpu.make_async_copy(w_ref.at[n // tiles, lines, wide], wbuf.at[n], wsem.at[n])

    def l_copy(d):
        deep = pl.ds(pl.multiple_of((slot ^ d) * depth, depth), depth)
        return pltpu.make_async_copy(blocks[d], lhs.at[:, deep], lsem.at[d])

    count = wbuf.shape[0]
    w_copy(0).start()
    for d in range(half):
        l_copy(d).start()
    for n in range(1, count):
        w_copy(n).start()
    for d in range(half):
        l_copy(d).wait()

    def body(n, carry):
        w_copy(n).wait()
        wide = pl.ds(pl.multiple_of(lax.rem(n, tiles) * span, span), span)
        total = None
        for d in range(half):
            deep = slice(d * depth, (d + 1) * depth)
            part = jnp.dot(lhs[:, deep], wbuf[n, deep, :], preferred_element_type=F32)
            total = part if total is None else total + part
        out_ref[n // tiles, :, wide] = total
        return carry

    lax.fori_loop(0, count, body, 0)


def near_product(place, blocks, weights):
    half = len(blocks)
    rows, depth = blocks[0].shape
    gates, _, width = weights.shape
    span = tile_of(width, 512)
    tiles = width // span
    anywhere = pl.BlockSpec(memory_space=pl.ANY)
    return pl.pallas_call(
        functools.partial(near_kernel, half, tiles),
        out_shape=jax.ShapeDtypeStruct((gates, rows, width), F32),
        in_specs=[pl.BlockSpec(memory_space=pltpu.SMEM)]
        + [anywhere] * half
        + [pl.BlockSpec(memory_space=pltpu.HBM)],
        out_specs=pl.BlockSpec(memory_space=pltpu.VMEM),
        scratch_shapes=[
            pltpu.VMEM((rows, half * depth), BF16),
            pltpu.VMEM((gates * tiles, half * depth, span), BF16),
            pltpu.SemaphoreType.DMA((half,)),
            pltpu.SemaphoreType.DMA((gates * tiles,)),
        ],
        compiler_params=params(28),
        cost_estimate=cost(
            2 * gates * rows * half * depth * width,
            gates * width * (half * depth * 2 + rows * 4) + half * rows * depth * 2,
        ),
    )(place, *blocks, weights)


def split_kernel(sizes, src, *refs):
    outs, sem = refs[:-1], refs[-1]
    copies, first = [], 0
    for k, rows in enumerate(sizes):
        copies.append(pltpu.make_async_copy(src.at[first : first + rows, :], outs[k], sem.at[k]))
        first += rows
    for copy in copies:
        copy.start()
    for copy in copies:
        copy.wait()


def split_rows(array, sizes):
    vmem = pl.BlockSpec(memory_space=pltpu.VMEM)
    return pl.pallas_call(
        functools.partial(split_kernel, sizes),
        out_shape=[jax.ShapeDtypeStruct((rows, array.shape[1]), array.dtype) for rows in sizes],
        in_specs=[pl.BlockSpec(memory_space=pltpu.HBM)],
        out_specs=[vmem] * len(sizes),
        scratch_shapes=[pltpu.SemaphoreType.DMA((len(sizes),))],
        compiler_params=params(12),
        cost_estimate=cost(0, 4 * array.shape[0] * array.shape[1]),
        name="split",
    )(array)


def compose_rows(maps, count, a, b):
    for k in range(count):
        slope = maps[0, k : k + 1, :]
        shift = maps[1, k : k + 1, :]
        b = slope * b + shift
        a = slope * a
    return a, b


def spread_rows(flat, g, lane, tiles, j, seg):
    parts = [flat[g, lane + l, pl.ds(j, SEGS, stride=seg), :] for l in range(tiles)]
    return jnp.concatenate(parts, axis=1)


def first_slopes(pre, cand, gain):
    update = jax.nn.sigmoid(pre)
    keep = 1.0 - update
    scaled = update * gain
    squashed = jnp.tanh(cand)
    slope = keep + (scaled - scaled * squashed * squashed)
    return update, keep, scaled, slope, update * squashed


def lead_row(place, start, shape):
    lead = lax.broadcasted_iota(jnp.int32, shape, 0) == 0
    return jnp.where(lead & (place[1] == 0), start, 0.0)


def around(update, keep, scaled, cand, gain, prev):
    squashed = jnp.tanh(cand + gain * prev)
    bend = scaled - scaled * squashed * squashed
    return keep + bend, update * squashed - bend * prev


def gate_kernel(half, chunk, first_row, rows, before, last, place, *refs):
    blocks = refs[:half]
    part_ref, w_ref, bias_ref, gain_ref, start_ref = refs[half : half + 5]
    earlier = refs[half + 5 : half + 5 + before]
    rest = refs[half + 5 + before :]
    if last:
        gates_ref, maps_ref, total_ref = rest[:3]
    else:
        gates_ref, maps_ref = rest[:2]
    lhs, wbuf, pbuf, acc, flat, lsem, wsem, psem = rest[-8:]
    depth = blocks[0].shape[1]
    width = gain_ref.shape[1]
    seg = rows // SEGS
    steps, lines_of = wbuf.shape[0], wbuf.shape[2]
    slot = lax.rem(place[0], half)
    base = ((place[0] // half) ^ 1) * (half * depth)

    def w_copy(k):
        lines = pl.ds(pl.multiple_of(base + k * lines_of, lines_of), lines_of)
        return pltpu.make_async_copy(w_ref.at[:, lines, :], wbuf.at[k], wsem.at[k])

    def l_copy(d):
        deep = pl.ds(pl.multiple_of((slot ^ d) * depth, depth), depth)
        return pltpu.make_async_copy(blocks[d], lhs.at[:, deep], lsem.at[d])

    p_copy = pltpu.make_async_copy(part_ref.at[:, first_row : first_row + rows, :], pbuf, psem)
    for d in range(half):
        l_copy(d).start()
    for k in range(steps):
        w_copy(k).start()
    p_copy.start()
    for d in range(half):
        l_copy(d).wait()

    def product(k, g):
        deep = pl.ds(pl.multiple_of(k * lines_of, lines_of), lines_of)
        return jnp.dot(lhs[:, deep], wbuf[k, g], preferred_element_type=F32)

    w_copy(0).wait()
    for g in range(2):
        acc[g] = product(0, g)

    def more(k, carry):
        w_copy(k).wait()
        for g in range(2):
            acc[g] += product(k, g)
        return carry

    lax.fori_loop(1, steps, more, 0)
    p_copy.wait()
    for g in range(2):
        for l in range(width // LANES):
            lanes = slice(l * LANES, (l + 1) * LANES)
            flat[g, l] = acc[g, :, lanes] + pbuf[g, :, lanes] + bias_ref[g : g + 1, lanes]

    tiles = tile_of(width // LANES, 8)
    span = tiles * LANES

    def columns(n, carry_out):
        wide = pl.ds(pl.multiple_of(n * span, span), span)
        gain = jnp.broadcast_to(gain_ref[:, wide], (SEGS, span))

        def pair(jj, carry, first):
            a, b = carry
            lines = pl.ds(pl.multiple_of(jj * 2 * SEGS, 2 * SEGS), 2 * SEGS)
            held = []
            for g in range(2):
                rows2 = [spread_rows(flat, g, n * tiles, tiles, 2 * jj + k, seg) for k in range(2)]
                rounded = jnp.concatenate(rows2, axis=0).astype(BF16)
                gates_ref[g, lines, wide] = rounded
                held.append(rounded.astype(F32))
            for k in range(2):
                pre = held[0][k * SEGS : (k + 1) * SEGS]
                cand = held[1][k * SEGS : (k + 1) * SEGS]
                update, keep, scaled, slope, offset = first_slopes(pre, cand, gain)
                if first and k == 0:
                    prev = lead_row(place, start_ref[:, wide], (SEGS, span))
                    slope, offset = around(update, keep, scaled, cand, gain, prev)
                b = slope * b + offset
                a = slope * a
            return a, b

        carry = (jnp.ones((SEGS, span), F32), jnp.zeros((SEGS, span), F32))
        begin = 0
        if chunk == 0:
            carry = pair(0, carry, True)
            begin = 1
        a, b = lax.fori_loop(begin, seg // 2, lambda jj, c: pair(jj, c, False), carry)
        maps_ref[0, :, wide] = a
        maps_ref[1, :, wide] = b
        return carry_out

    lax.fori_loop(0, width // span, columns, 0)
    if last:
        ta, tb = jnp.ones((1, width), F32), jnp.zeros((1, width), F32)
        for maps in list(earlier) + [maps_ref]:
            ta, tb = compose_rows(maps, SEGS, ta, tb)
        for i in range(total_ref.shape[0]):
            total_ref[i, 0:1, :] = ta
            total_ref[i, 1:2, :] = tb


def gate_chunk(
    place, blocks, partial, weights, biases, gain, start, earlier, chunk, first_row, last, peers
):
    half = len(blocks)
    rows, depth = blocks[0].shape
    gates, _, width = weights.shape
    lines_of = tile_of(half * depth, 512)
    steps = half * depth // lines_of
    anywhere = pl.BlockSpec(memory_space=pl.ANY)
    vmem = pl.BlockSpec(memory_space=pltpu.VMEM)
    out_shape = [
        jax.ShapeDtypeStruct((2, rows, width), BF16),
        jax.ShapeDtypeStruct((2, SEGS, width), F32),
    ]
    if last:
        out_shape.append(jax.ShapeDtypeStruct((peers, 2, width), F32))
    return pl.pallas_call(
        functools.partial(gate_kernel, half, chunk, first_row, rows, len(earlier), last),
        out_shape=out_shape,
        in_specs=[pl.BlockSpec(memory_space=pltpu.SMEM)]
        + [anywhere] * (half + 1)
        + [pl.BlockSpec(memory_space=pltpu.HBM)]
        + [vmem] * (3 + len(earlier)),
        out_specs=[vmem] * len(out_shape),
        scratch_shapes=[
            pltpu.VMEM((rows, half * depth), BF16),
            pltpu.VMEM((steps, gates, lines_of, width), BF16),
            pltpu.VMEM((gates, rows, width), F32),
            pltpu.VMEM((gates, rows, width), F32),
            pltpu.VMEM((gates, width // LANES, rows, LANES), F32),
            pltpu.SemaphoreType.DMA((half,)),
            pltpu.SemaphoreType.DMA((steps,)),
            pltpu.SemaphoreType.DMA,
        ],
        compiler_params=params(32),
        cost_estimate=cost(
            2 * gates * rows * half * depth * width,
            gates * width * (half * depth * 2 + rows * 6) + half * rows * depth * 2,
            4 * rows * width,
        ),
    )(place, *blocks, partial, weights, biases, gain, start, *earlier)


def entering_state(place, peer_maps, start, peers):
    state = start
    for k in range(peers):
        moved = peer_maps[k, 0:1, :] * state + peer_maps[k, 1:2, :]
        state = jnp.where(place[1] > k, moved, state)
    return state


def enter_segments(maps_list, state, enter):
    for c, maps in enumerate(maps_list):
        for k in range(SEGS):
            enter[c * SEGS + k : c * SEGS + k + 1, :] = state
            state = maps[0, k : k + 1, :] * state + maps[1, k : k + 1, :]


def bend_kernel(chunks, peers, place, *refs):
    gates = refs[:chunks]
    maps = refs[chunks : 2 * chunks]
    peer_ref, gain_ref, start_ref, run_ref, maps_ref, total_ref, enter = refs[2 * chunks :]
    span = gates[0].shape[2]
    width = gain_ref.shape[1]
    heights = [g.shape[1] for g in gates]
    firsts = [sum(heights[:c]) for c in range(chunks)]
    least = min(heights)
    turns = least // SEGS // 2
    n = pl.program_id(0)

    @pl.when(n == 0)
    def _():
        enter_segments(maps, entering_state(place, peer_ref, start_ref[...], peers), enter)

    wide = pl.ds(pl.multiple_of(n * span, span), span)
    gain = jnp.broadcast_to(gain_ref[:, wide], (SEGS, span))

    def advance(c, jj, held, first):
        state, a, b = held
        lines = pl.ds(pl.multiple_of(jj * 2 * SEGS, 2 * SEGS), 2 * SEGS)
        pre2 = gates[c][0, lines, :].astype(F32)
        cand2 = gates[c][1, lines, :].astype(F32)
        for k in range(2):
            pre = pre2[k * SEGS : (k + 1) * SEGS]
            cand = cand2[k * SEGS : (k + 1) * SEGS]
            update, keep, scaled, slope, offset = first_slopes(pre, cand, gain)
            if first and k == 0:
                prev = lead_row(place, start_ref[:, wide], (SEGS, span))
                slope, offset = around(update, keep, scaled, cand, gain, prev)
            slope2, offset2 = around(update, keep, scaled, cand, gain, state)
            state = slope * state + offset
            b = slope2 * b + offset2
            a = slope2 * a
            row = pl.ds(pl.multiple_of(firsts[c] + (2 * jj + k) * SEGS, SEGS), SEGS)
            run_ref[0, row, :] = a
            run_ref[1, row, :] = b
        return state, a, b

    def pair(turn, carry, first):
        out = []
        for c in range(chunks):
            held = carry[c]
            times = heights[c] // least
            for r in range(times):
                held = advance(c, turn * times + r, held, first and c == 0 and r == 0)
            out.append(held)
        return tuple(out)

    one, zero = jnp.ones((SEGS, span), F32), jnp.zeros((SEGS, span), F32)
    carry = tuple((enter[c * SEGS : (c + 1) * SEGS, wide], one, zero) for c in range(chunks))
    carry = pair(0, carry, True)
    carry = lax.fori_loop(1, turns, lambda turn, c: pair(turn, c, False), carry)
    for c in range(chunks):
        maps_ref[0, c * SEGS : (c + 1) * SEGS, wide] = carry[c][1]
        maps_ref[1, c * SEGS : (c + 1) * SEGS, wide] = carry[c][2]

    @pl.when(n == pl.num_programs(0) - 1)
    def _():
        ta, tb = jnp.ones((1, width), F32), jnp.zeros((1, width), F32)
        ta, tb = compose_rows(maps_ref, chunks * SEGS, ta, tb)
        for i in range(peers):
            total_ref[i, 0:1, :] = ta
            total_ref[i, 1:2, :] = tb


def bend_all(place, gates, maps, peer_maps, gain, start):
    chunks = len(gates)
    peers = peer_maps.shape[0]
    width = gates[0].shape[2]
    total_rows = sum(g.shape[1] for g in gates)
    tn = tile_of(width, 256)
    row_spec = pl.BlockSpec((1, width), lambda n, p: (0, 0))
    total_spec = pl.BlockSpec((peers, 2, width), lambda n, p: (0, 0, 0))
    return pl.pallas_call(
        functools.partial(bend_kernel, chunks, peers),
        out_shape=[
            jax.ShapeDtypeStruct((2, total_rows, width), F32),
            jax.ShapeDtypeStruct((2, chunks * SEGS, width), F32),
            jax.ShapeDtypeStruct((peers, 2, width), F32),
        ],
        grid_spec=pltpu.PrefetchScalarGridSpec(
            num_scalar_prefetch=1,
            grid=(width // tn,),
            in_specs=[pl.BlockSpec((2, g.shape[1], tn), lambda n, p: (0, 0, n)) for g in gates]
            + [pl.BlockSpec((2, SEGS, width), lambda n, p: (0, 0, 0))] * chunks
            + [total_spec, row_spec, row_spec],
            out_specs=[
                pl.BlockSpec((2, total_rows, tn), lambda n, p: (0, 0, n)),
                pl.BlockSpec((2, chunks * SEGS, width), lambda n, p: (0, 0, 0)),
                total_spec,
            ],
            scratch_shapes=[pltpu.VMEM((chunks * SEGS, width), F32)],
        ),
        compiler_params=params(16),
        cost_estimate=cost(
            40 * total_rows * width, 12 * total_rows * width, 5 * total_rows * width
        ),
        name="bend",
    )(place, *gates, *maps, peer_maps, gain, start)


def state_kernel(chunk, peers, place, run_ref, maps_ref, peer_ref, start_ref, out_ref, enter, flat):
    rows, width = out_ref.shape
    seg = rows // SEGS
    state = entering_state(place, peer_ref, start_ref[...], peers)
    for k in range((chunk + 1) * SEGS):
        if k >= chunk * SEGS:
            enter[k - chunk * SEGS : k - chunk * SEGS + 1, :] = state
        state = maps_ref[0, k : k + 1, :] * state + maps_ref[1, k : k + 1, :]
    entered = enter[...]

    def step(j, carry):
        row = pl.ds(pl.multiple_of(j * SEGS, SEGS), SEGS)
        now = run_ref[0, row, :] * entered + run_ref[1, row, :]
        for l in range(width // LANES):
            flat[l, pl.ds(j, SEGS, stride=seg), :] = now[:, l * LANES : (l + 1) * LANES]
        return carry

    lax.fori_loop(0, seg, step, 0, unroll=4)
    for l in range(width // LANES):
        out_ref[:, l * LANES : (l + 1) * LANES] = flat[l].astype(BF16)


def state_chunk(place, run, maps, peer_maps, start, first_row, rows, chunk):
    width = run.shape[2]
    peers = peer_maps.shape[0]
    segs = maps.shape[1]
    tn = tile_of(width, 1024)
    return pl.pallas_call(
        functools.partial(state_kernel, chunk, peers),
        out_shape=jax.ShapeDtypeStruct((rows, width), BF16),
        grid_spec=pltpu.PrefetchScalarGridSpec(
            num_scalar_prefetch=1,
            grid=(width // tn,),
            in_specs=[
                pl.BlockSpec((2, rows, tn), lambda n, p: (0, first_row // rows, n)),
                pl.BlockSpec((2, segs, tn), lambda n, p: (0, 0, n)),
                pl.BlockSpec((peers, 2, tn), lambda n, p: (0, 0, n)),
                pl.BlockSpec((1, tn), lambda n, p: (0, n)),
            ],
            out_specs=pl.BlockSpec((rows, tn), lambda n, p: (0, n)),
            scratch_shapes=[pltpu.VMEM((SEGS, tn), F32), pltpu.VMEM((tn // LANES, rows, LANES), F32)],
        ),
        compiler_params=params(12),
        cost_estimate=cost(2 * rows * width, 10 * rows * width),
    )(place, run, maps, peer_maps, start)


def mix_kernel(groups, group, pieces, peers, slots, before, place, *refs):
    count = groups * group
    blocks = refs[:count]
    weights = refs[count : count + len(slots) * 2 * pieces]
    out_ref, lhs, wbuf, acc, lsem, wsem = refs[-6:]
    prev_ref = refs[count + len(weights)] if before else None
    depth = blocks[0].shape[1]
    heights = [blocks[c * group].shape[0] for c in range(groups)]
    lines_of = weights[0].shape[0]
    outer = peers // 2
    here = len(slots) * 2

    def w_copy(n, p):
        w_ref = weights[n * pieces + p]
        dst = wbuf.at[n, p * lines_of : (p + 1) * lines_of, :]
        return pltpu.make_async_copy(w_ref, dst, wsem.at[n, p])

    def l_copy(c, d):
        deep = pl.ds(pl.multiple_of((place[0] ^ d) * depth, depth), depth)
        top = sum(heights[:c])
        dst = lhs.at[top : top + heights[c], deep]
        return pltpu.make_async_copy(blocks[c * group + d], dst, lsem.at[c, d])

    for n in range(here):
        for p in range(pieces):
            w_copy(n, p).start()
    for c in range(groups):
        for d in range(group):
            l_copy(c, d).start()
    for c in range(groups):
        for d in range(group):
            l_copy(c, d).wait()
    span = lines_of * pieces
    for n in range(here):
        source = lax.rem(place[1] // 2 + outer - slots[n // 2], outer)
        owner = source * 2 + (lax.rem(place[1], 2) ^ (n % 2))
        deep = pl.ds(pl.multiple_of(owner * span, span), span)
        for p in range(pieces):
            w_copy(n, p).wait()
        part = jnp.dot(lhs[:, deep], wbuf[n], preferred_element_type=F32)
        if n == 0 and before:
            part = part + prev_ref[...]
        if n > 0:
            part = acc[...] + part
        if n < here - 1:
            acc[...] = part
        else:
            out_ref[...] = part.astype(out_ref.dtype)


def mix_rows(place, blocks, weights, slots, prev, final, whole, first, total_rows, pieces):
    groups, group = len(blocks), len(blocks[0])
    depth = blocks[0][0].shape[1]
    lines_of, width = weights[0].shape
    peers = len(weights) // pieces
    rows = sum(g[0].shape[0] for g in blocks)
    used = [weights[(s * 2 + i) * pieces + p] for s in slots for i in range(2) for p in range(pieces)]
    args = [place] + [b for g in blocks for b in g] + used
    in_specs = [pl.BlockSpec(memory_space=pl.ANY)] * (groups * group)
    in_specs += [pl.BlockSpec(memory_space=pltpu.HBM)] * len(used)
    if prev is not None:
        args.append(prev)
        in_specs.append(pl.BlockSpec((rows, width), lambda n, p: (0, 0)))
    aliases = {}
    if whole is not None:
        aliases = {len(args): 0}
        args.append(whole)
        in_specs.append(pl.BlockSpec(memory_space=pl.ANY))
    deep = len(slots) * 2 * pieces * lines_of
    if final:
        out_shape = jax.ShapeDtypeStruct((total_rows, width), BF16)
        out_spec = pl.BlockSpec((rows, width), lambda n, p: (first // rows, 0))
    else:
        out_shape = jax.ShapeDtypeStruct((rows, width), F32)
        out_spec = pl.BlockSpec((rows, width), lambda n, p: (0, 0))
    return pl.pallas_call(
        functools.partial(mix_kernel, groups, group, pieces, peers, tuple(slots), prev is not None),
        out_shape=out_shape,
        grid_spec=pltpu.PrefetchScalarGridSpec(
            num_scalar_prefetch=1,
            grid=(1,),
            in_specs=in_specs,
            out_specs=out_spec,
            scratch_shapes=[
                pltpu.VMEM((rows, group * depth), BF16),
                pltpu.VMEM((len(slots) * 2, lines_of * pieces, width), BF16),
                pltpu.VMEM((rows, width), F32),
                pltpu.SemaphoreType.DMA((groups, group)),
                pltpu.SemaphoreType.DMA((len(slots) * 2, pieces)),
            ],
        ),
        input_output_aliases=aliases,
        compiler_params=params(40 if peers <= 8 else 62),
        cost_estimate=cost(2 * rows * deep * width, 2 * deep * (width + rows) + 4 * rows * width),
    )(*args)


EARLY = 5
SHARES = (2, 1, 1)


def pieces_of(lines_of):
    return 2 if lines_of % (4 * LANES) == 0 else 1


class Ring:
    def __init__(self, w_output):
        self.peers = lax.axis_size("ctx")
        self.outer = self.peers // 2
        self.pieces = pieces_of(w_output.shape[0])
        lines_of = w_output.shape[0] // self.pieces
        self.held = {}
        for p in range(self.pieces):
            self.held[0, 0, p] = w_output[p * lines_of : (p + 1) * lines_of]

    def ring_step(self, n, gate=None):
        s, p = n // self.pieces + 1, n % self.pieces
        block = self.held[s - 1, 0, p]
        if gate is not None:
            block, _ = lax.optimization_barrier((block, gate))
        route = [(i, (i + 2) % self.peers) for i in range(self.peers)]
        self.held[s, 0, p] = lax.ppermute(block, "ctx", route)

    def swap_step(self, n, gate=None):
        s, p = n // self.pieces, n % self.pieces
        block = self.held[s, 0, p]
        if gate is not None:
            block, _ = lax.optimization_barrier((block, gate))
        self.held[s, 1, p] = swap(block, "ctx", 1)

    def run(self, gate):
        rings, swaps = (self.outer - 1) * self.pieces, self.outer * self.pieces
        for n in range(max(rings, swaps)):
            g = gate if n >= EARLY else None
            if n < rings:
                self.ring_step(n, g)
            if n < swaps:
                self.swap_step(n, g)

    def blocks(self):
        steps = [(s, i) for s in range(self.outer) for i in range(2)]
        return [self.held[s, i, p] for s, i in steps for p in range(self.pieces)]


def layer(tokens, w_input, w_output, bias_update, bias_cand, recur_gain, start_state):
    peers = lax.axis_size("ctx")
    group = lax.axis_size("ch")
    half = group // 2
    total_rows = tokens.shape[0]
    chunks = len(SHARES)
    sizes = [total_rows * share // sum(SHARES) for share in SHARES]
    firsts = [sum(sizes[:c]) for c in range(chunks)]
    place = jnp.stack([lax.axis_index("ch"), lax.axis_index("ctx")]).astype(jnp.int32)
    biases = jnp.stack([bias_update, bias_cand], axis=0)
    gain = recur_gain[None, :]
    start = start_state[None, :]

    far = []
    for piece in split_rows(tokens, sizes):
        far.append([swap(piece, "ch", half)])
    near = [tokens]
    for d in range(1, half):
        near.append(swap(tokens, "ch", d))
    for c in range(chunks):
        for d in range(1, half):
            far[c].append(swap(far[c][0], "ch", d))

    partial = near_product(place, near, w_input)
    gates, maps = [], []
    for c in range(chunks):
        last = c == chunks - 1
        out = gate_chunk(
            place,
            far[c],
            partial,
            w_input,
            biases,
            gain,
            start,
            maps if last else [],
            c,
            firsts[c],
            last,
            peers,
        )
        gates.append(out[0])
        maps.append(out[1])
    peer_maps = lax.all_to_all(out[2], "ctx", 0, 0, tiled=True)
    run, run_maps, totals = bend_all(place, gates, maps, peer_maps, gain, start)
    peer_maps = lax.all_to_all(totals, "ctx", 0, 0, tiled=True)
    ring = Ring(w_output)
    ring.run(peer_maps)

    blocks = []
    for c in range(chunks):
        own = state_chunk(place, run, run_maps, peer_maps, start, firsts[c], sizes[c], c)
        across = swap(own, "ch", half)
        blocks.append([own, across])
    for c in range(chunks):
        own, across = blocks[c]
        lows, highs = [own], [across]
        for d in range(1, half):
            lows.append(swap(own, "ch", d))
            highs.append(swap(across, "ch", d))
        blocks[c] = lows + highs
    weights = ring.blocks()
    split = chunks - 1
    late = max(1, ring.outer // 4)
    slots = list(range(ring.outer))
    partial = mix_rows(
        place, blocks[:split], weights, slots[:-late], None, False, None, 0, total_rows, ring.pieces
    )
    mixed = mix_rows(
        place, blocks[:split], weights, slots[-late:], partial, True, None, 0, total_rows, ring.pieces
    )
    return mix_rows(
        place,
        blocks[split:],
        weights,
        slots,
        None,
        True,
        mixed,
        firsts[split],
        total_rows,
        ring.pieces,
    )


def solution(mesh):
    return jax.shard_map(
        layer,
        mesh=mesh,
        in_specs=(
            P("ctx", "ch"),
            P(None, None, "ch"),
            P("ctx", "ch"),
            P("ch"),
            P("ch"),
            P("ch"),
            P("ch"),
        ),
        out_specs=P("ctx", "ch"),
        check_vma=False,
    )
```

```python
import functools
import math

import jax
import jax.numpy as jnp
from jax import lax
from jax.experimental import pallas as pl
from jax.experimental.pallas import tpu as pltpu
from jax.sharding import PartitionSpec as P


SEGS = 8
LANES = 128
BLOCK = 256
F32 = jnp.float32
BF16 = jnp.bfloat16
MIB = 1024 * 1024


def swap(block, axis, bits):
    return lax.ppermute(block, axis, [(i, i ^ bits) for i in range(lax.axis_size(axis))])


def tile_of(width, most):
    return math.gcd(width, most)


def params(mib):
    return pltpu.CompilerParams(vmem_limit_bytes=mib * MIB)


def cost(flops, nbytes, trans=0):
    return pl.CostEstimate(flops=int(flops), bytes_accessed=int(nbytes), transcendentals=int(trans))


def near_kernel(half, tiles, heights, place, *refs):
    count = len(heights)
    blocks = refs[: half * count]
    w_ref, out_ref, lhs, wbuf, lsem, wsem = refs[half * count :]
    depth = blocks[0].shape[1]
    span = wbuf.shape[2]
    slot = lax.rem(place[0], half)
    base = (place[0] // half) * (half * depth)

    def w_copy(n):
        lines = pl.ds(pl.multiple_of(base, half * depth), half * depth)
        wide = pl.ds(pl.multiple_of(lax.rem(n, tiles) * span, span), span)
        return pltpu.make_async_copy(w_ref.at[n // tiles, lines, wide], wbuf.at[n], wsem.at[n])

    def l_copy(d, k):
        deep = pl.ds(pl.multiple_of((slot ^ d) * depth, depth), depth)
        top = sum(heights[:k])
        dst = lhs.at[top : top + heights[k], deep]
        return pltpu.make_async_copy(blocks[d * count + k], dst, lsem.at[d, k])

    steps = wbuf.shape[0]
    for n in range(steps):
        w_copy(n).start()
    for d in range(half):
        for k in range(count):
            l_copy(d, k).start()
    for d in range(half):
        for k in range(count):
            l_copy(d, k).wait()

    def body(n, carry):
        w_copy(n).wait()
        wide = pl.ds(pl.multiple_of(lax.rem(n, tiles) * span, span), span)
        total = None
        for d in range(half):
            deep = slice(d * depth, (d + 1) * depth)
            part = jnp.dot(lhs[:, deep], wbuf[n, deep, :], preferred_element_type=F32)
            total = part if total is None else total + part
        out_ref[n // tiles, :, wide] = total
        return carry

    lax.fori_loop(0, steps, body, 0)


def near_product(place, blocks, weights):
    half = len(blocks)
    heights = tuple(b.shape[0] for b in blocks[0])
    rows, depth = sum(heights), blocks[0][0].shape[1]
    gates, _, width = weights.shape
    span = tile_of(width, 512)
    tiles = width // span
    return pl.pallas_call(
        functools.partial(near_kernel, half, tiles, heights),
        out_shape=jax.ShapeDtypeStruct((gates, rows, width), F32),
        in_specs=[pl.BlockSpec(memory_space=pltpu.SMEM)]
        + [pl.BlockSpec(memory_space=pl.ANY)] * (half * len(heights))
        + [pl.BlockSpec(memory_space=pltpu.HBM)],
        out_specs=pl.BlockSpec(memory_space=pltpu.VMEM),
        scratch_shapes=[
            pltpu.VMEM((rows, half * depth), BF16),
            pltpu.VMEM((gates * tiles, half * depth, span), BF16),
            pltpu.SemaphoreType.DMA((half, len(heights))),
            pltpu.SemaphoreType.DMA((gates * tiles,)),
        ],
        compiler_params=params(28),
        cost_estimate=cost(
            2 * gates * rows * half * depth * width,
            gates * width * (half * depth * 2 + rows * 4) + half * rows * depth * 2,
        ),
    )(place, *[piece for block in blocks for piece in block], weights)


def row_order(transposed):
    shape = (BLOCK, BLOCK)
    row = lax.broadcasted_iota(jnp.int32, shape, 1 if transposed else 0)
    token = lax.broadcasted_iota(jnp.int32, shape, 0 if transposed else 1)
    chosen = lax.rem(row, SEGS) * (BLOCK // SEGS) + row // SEGS == token
    return jnp.where(chosen, 1.0, 0.0).astype(BF16)


def split_kernel(first, sizes, joined, src, *refs):
    count = len(sizes)
    outs = refs[:count]
    buf, sem = refs[-2:]
    blocks = sum(sizes) // BLOCK
    copies = []
    for k in range(blocks):
        lines = pl.ds(first + k * BLOCK, BLOCK)
        copies.append(pltpu.make_async_copy(src.at[lines, :], buf.at[k], sem.at[k]))
    for copy in copies:
        copy.start()
    order = row_order(False)
    k = 0
    for c in range(count):
        for r in range(sizes[c] // BLOCK):
            copies[k].wait()
            moved = jnp.dot(order, buf[k], preferred_element_type=F32).astype(BF16)
            outs[c][r * BLOCK : (r + 1) * BLOCK, :] = moved
            if joined:
                refs[count][k * BLOCK : (k + 1) * BLOCK, :] = moved
            k += 1


def split_rows(array, first, sizes, joined):
    vmem = pl.BlockSpec(memory_space=pltpu.VMEM)
    rows, width = sum(sizes), array.shape[1]
    shapes = list(sizes) + ([rows] if joined else [])
    return pl.pallas_call(
        functools.partial(split_kernel, first, tuple(sizes), joined),
        out_shape=[jax.ShapeDtypeStruct((r, width), array.dtype) for r in shapes],
        in_specs=[pl.BlockSpec(memory_space=pltpu.HBM)],
        out_specs=[vmem] * len(shapes),
        scratch_shapes=[
            pltpu.VMEM((rows // BLOCK, BLOCK, width), BF16),
            pltpu.SemaphoreType.DMA((rows // BLOCK,)),
        ],
        compiler_params=params(12),
        cost_estimate=cost(2 * rows * BLOCK * width, 4 * rows * width),
    )(array)


def compose_rows(maps, count, a, b):
    for k in range(count):
        slope = maps[0, k : k + 1, :]
        shift = maps[1, k : k + 1, :]
        b = slope * b + shift
        a = slope * a
    return a, b


def first_slopes(pre, cand, gain):
    update = jax.nn.sigmoid(pre)
    keep = 1.0 - update
    scaled = update * gain
    squashed = jnp.tanh(cand)
    slope = keep + (scaled - scaled * squashed * squashed)
    return update, keep, scaled, slope, update * squashed


def lead_row(place, start, shape):
    lead = lax.broadcasted_iota(jnp.int32, shape, 0) == 0
    return jnp.where(lead & (place[1] == 0), start, 0.0)


def around(update, keep, scaled, cand, gain, prev):
    squashed = jnp.tanh(cand + gain * prev)
    bend = scaled - scaled * squashed * squashed
    return keep + bend, update * squashed - bend * prev


def gate_kernel(half, first_row, rows, before, last, place, *refs):
    blocks = refs[:half]
    part_ref, w_ref, bias_ref, gain_ref, start_ref = refs[half : half + 5]
    earlier = refs[half + 5 : half + 5 + before]
    rest = refs[half + 5 + before :]
    if last:
        gates_ref, maps_ref, total_ref = rest[:3]
    else:
        gates_ref, maps_ref = rest[:2]
    wbuf, acc, wsem = rest[-3:]
    depth = blocks[0].shape[1]
    width = gain_ref.shape[1]
    seg = BLOCK // SEGS
    count = rows // BLOCK
    lines_of = wbuf.shape[3]
    parts = depth // lines_of
    slot = lax.rem(place[0], half)
    base = ((place[0] // half) ^ 1) * (half * depth)

    def w_copy(g, d, q):
        top = base + (slot ^ d) * depth + q * lines_of
        lines = pl.ds(pl.multiple_of(top, lines_of), lines_of)
        return pltpu.make_async_copy(w_ref.at[g, lines, :], wbuf.at[g, d, q], wsem.at[g, d, q])

    every = [(d, q) for d in range(half) for q in range(parts)]
    for g in range(2):
        for d, q in every:
            w_copy(g, d, q).start()
    for g in range(2):
        for d, q in every:
            w_copy(g, d, q).wait()
            deep = slice(q * lines_of, (q + 1) * lines_of)
            part = jnp.dot(blocks[d][:, deep], wbuf[g, d, q], preferred_element_type=F32)
            if (d, q) == (0, 0):
                acc[g] = part
            else:
                acc[g] += part

    span = tile_of(width, 512)

    def columns(n, carry_out):
        wide = pl.ds(pl.multiple_of(n * span, span), span)
        gain = jnp.broadcast_to(gain_ref[:, wide], (SEGS, span))
        bias = [jnp.broadcast_to(bias_ref[g : g + 1, wide], (2 * SEGS, span)) for g in range(2)]

        def pair(jj, carry, first):
            out = []
            for c in range(count):
                a, b = carry[c]
                lines = pl.ds(pl.multiple_of(c * BLOCK + jj * 2 * SEGS, 2 * SEGS), 2 * SEGS)
                deep = pl.ds(
                    pl.multiple_of(first_row + c * BLOCK + jj * 2 * SEGS, 2 * SEGS), 2 * SEGS
                )
                held = []
                for g in range(2):
                    total = acc[g, lines, wide] + part_ref[g, deep, wide] + bias[g]
                    rounded = total.astype(BF16)
                    gates_ref[g, lines, wide] = rounded
                    held.append(rounded.astype(F32))
                for k in range(2):
                    pre = held[0][k * SEGS : (k + 1) * SEGS]
                    cand = held[1][k * SEGS : (k + 1) * SEGS]
                    update, keep, scaled, slope, offset = first_slopes(pre, cand, gain)
                    if first and k == 0 and c == 0:
                        prev = lead_row(place, start_ref[:, wide], (SEGS, span))
                        slope, offset = around(update, keep, scaled, cand, gain, prev)
                    b = slope * b + offset
                    a = slope * a
                out.append((a, b))
            return tuple(out)

        carry = ((jnp.ones((SEGS, span), F32), jnp.zeros((SEGS, span), F32)),) * count
        begin = 0
        if first_row == 0:
            carry = pair(0, carry, True)
            begin = 1
        carry = lax.fori_loop(begin, seg // 2, lambda jj, c: pair(jj, c, False), carry)
        for c in range(count):
            maps_ref[0, c * SEGS : (c + 1) * SEGS, wide] = carry[c][0]
            maps_ref[1, c * SEGS : (c + 1) * SEGS, wide] = carry[c][1]
        return carry_out

    lax.fori_loop(0, width // span, columns, 0)
    if last:
        ta, tb = jnp.ones((1, width), F32), jnp.zeros((1, width), F32)
        for maps in list(earlier) + [maps_ref]:
            ta, tb = compose_rows(maps, maps.shape[1], ta, tb)
        for i in range(total_ref.shape[0]):
            total_ref[i, 0:1, :] = ta
            total_ref[i, 1:2, :] = tb


def gate_chunk(place, blocks, partial, weights, biases, gain, start, earlier, first_row, last, peers):
    half = len(blocks)
    rows, depth = blocks[0].shape
    gates, _, width = weights.shape
    lines_of = tile_of(depth, 512)
    vmem = pl.BlockSpec(memory_space=pltpu.VMEM)
    out_shape = [
        jax.ShapeDtypeStruct((2, rows, width), BF16),
        jax.ShapeDtypeStruct((2, rows // BLOCK * SEGS, width), F32),
    ]
    if last:
        out_shape.append(jax.ShapeDtypeStruct((peers, 2, width), F32))
    return pl.pallas_call(
        functools.partial(gate_kernel, half, first_row, rows, len(earlier), last),
        out_shape=out_shape,
        in_specs=[pl.BlockSpec(memory_space=pltpu.SMEM)]
        + [vmem] * (half + 1)
        + [pl.BlockSpec(memory_space=pltpu.HBM)]
        + [vmem] * (3 + len(earlier)),
        out_specs=[vmem] * len(out_shape),
        scratch_shapes=[
            pltpu.VMEM((gates, half, depth // lines_of, lines_of, width), BF16),
            pltpu.VMEM((gates, rows, width), F32),
            pltpu.SemaphoreType.DMA((gates, half, depth // lines_of)),
        ],
        compiler_params=params(32),
        cost_estimate=cost(
            2 * gates * rows * half * depth * width,
            gates * width * (half * depth * 2 + rows * 6) + half * rows * depth * 2,
            4 * rows * width,
        ),
    )(place, *blocks, partial, weights, biases, gain, start, *earlier)


def entering_state(place, peer_maps, start, peers):
    state = start
    for k in range(peers):
        moved = peer_maps[k, 0:1, :] * state + peer_maps[k, 1:2, :]
        state = jnp.where(place[1] > k, moved, state)
    return state


def enter_segments(maps_list, state, enter):
    row = 0
    for maps in maps_list:
        for k in range(maps.shape[1]):
            enter[row : row + 1, :] = state
            state = maps[0, k : k + 1, :] * state + maps[1, k : k + 1, :]
            row += 1


def bend_kernel(chunks, peers, place, *refs):
    gates = refs[:chunks]
    maps = refs[chunks : 2 * chunks]
    peer_ref, gain_ref, start_ref, run_ref, maps_ref, total_ref, enter = refs[2 * chunks :]
    span = gates[0].shape[2]
    width = gain_ref.shape[1]
    where = [(c, r * BLOCK) for c in range(chunks) for r in range(gates[c].shape[1] // BLOCK)]
    n = pl.program_id(0)

    @pl.when(n == 0)
    def _():
        enter_segments(maps, entering_state(place, peer_ref, start_ref[...], peers), enter)

    wide = pl.ds(pl.multiple_of(n * span, span), span)
    gain = jnp.broadcast_to(gain_ref[:, wide], (SEGS, span))

    def advance(block, jj, held, first):
        state, a, b = held
        c, top = where[block]
        lines = pl.ds(pl.multiple_of(top + jj * 2 * SEGS, 2 * SEGS), 2 * SEGS)
        pre2 = gates[c][0, lines, :].astype(F32)
        cand2 = gates[c][1, lines, :].astype(F32)
        for k in range(2):
            pre = pre2[k * SEGS : (k + 1) * SEGS]
            cand = cand2[k * SEGS : (k + 1) * SEGS]
            update, keep, scaled, slope, offset = first_slopes(pre, cand, gain)
            if first and k == 0 and block == 0:
                prev = lead_row(place, start_ref[:, wide], (SEGS, span))
                slope, offset = around(update, keep, scaled, cand, gain, prev)
            slope2, offset2 = around(update, keep, scaled, cand, gain, state)
            state = slope * state + offset
            b = slope2 * b + offset2
            a = slope2 * a
            row = pl.ds(pl.multiple_of(block * BLOCK + (2 * jj + k) * SEGS, SEGS), SEGS)
            run_ref[0, row, :] = a
            run_ref[1, row, :] = b
        return state, a, b

    def pair(jj, carry, first):
        return tuple(advance(m, jj, carry[m], first) for m in range(len(where)))

    one, zero = jnp.ones((SEGS, span), F32), jnp.zeros((SEGS, span), F32)
    carry = tuple((enter[m * SEGS : (m + 1) * SEGS, wide], one, zero) for m in range(len(where)))
    carry = pair(0, carry, True)
    carry = lax.fori_loop(1, BLOCK // SEGS // 2, lambda jj, c: pair(jj, c, False), carry)
    for m in range(len(where)):
        maps_ref[0, m * SEGS : (m + 1) * SEGS, wide] = carry[m][1]
        maps_ref[1, m * SEGS : (m + 1) * SEGS, wide] = carry[m][2]

    @pl.when(n == pl.num_programs(0) - 1)
    def _():
        ta, tb = jnp.ones((1, width), F32), jnp.zeros((1, width), F32)
        ta, tb = compose_rows(maps_ref, maps_ref.shape[1], ta, tb)
        for i in range(peers):
            total_ref[i, 0:1, :] = ta
            total_ref[i, 1:2, :] = tb


def bend_all(place, gates, maps, peer_maps, gain, start):
    chunks = len(gates)
    peers = peer_maps.shape[0]
    width = gates[0].shape[2]
    total_rows = sum(g.shape[1] for g in gates)
    segs = total_rows // BLOCK * SEGS
    tn = tile_of(width, 256)
    row_spec = pl.BlockSpec((1, width), lambda n, p: (0, 0))
    total_spec = pl.BlockSpec((peers, 2, width), lambda n, p: (0, 0, 0))
    return pl.pallas_call(
        functools.partial(bend_kernel, chunks, peers),
        out_shape=[
            jax.ShapeDtypeStruct((2, total_rows, width), F32),
            jax.ShapeDtypeStruct((2, segs, width), F32),
            jax.ShapeDtypeStruct((peers, 2, width), F32),
        ],
        grid_spec=pltpu.PrefetchScalarGridSpec(
            num_scalar_prefetch=1,
            grid=(width // tn,),
            in_specs=[pl.BlockSpec((2, g.shape[1], tn), lambda n, p: (0, 0, n)) for g in gates]
            + [pl.BlockSpec((2, m.shape[1], width), lambda n, p: (0, 0, 0)) for m in maps]
            + [total_spec, row_spec, row_spec],
            out_specs=[
                pl.BlockSpec((2, total_rows, tn), lambda n, p: (0, 0, n)),
                pl.BlockSpec((2, segs, width), lambda n, p: (0, 0, 0)),
                total_spec,
            ],
            scratch_shapes=[pltpu.VMEM((segs, width), F32)],
        ),
        compiler_params=params(16),
        cost_estimate=cost(
            40 * total_rows * width, 12 * total_rows * width, 5 * total_rows * width
        ),
        name="bend",
    )(place, *gates, *maps, peer_maps, gain, start)


def state_kernel(first_row, peers, place, run_ref, maps_ref, peer_ref, start_ref, out_ref, enter):
    rows = out_ref.shape[0]
    begin = first_row // BLOCK * SEGS
    state = entering_state(place, peer_ref, start_ref[...], peers)
    for k in range(begin + rows // BLOCK * SEGS):
        if k >= begin:
            enter[k - begin : k - begin + 1, :] = state
        state = maps_ref[0, k : k + 1, :] * state + maps_ref[1, k : k + 1, :]
    for c in range(rows // BLOCK):
        once = enter[c * SEGS : (c + 1) * SEGS, :]
        entered = jnp.concatenate([once, once], axis=0)

        def step(jj, carry):
            at = pl.multiple_of(c * BLOCK + jj * 2 * SEGS, 2 * SEGS)
            lines = pl.ds(at, 2 * SEGS)
            deep = pl.ds(pl.multiple_of(first_row + at, 2 * SEGS), 2 * SEGS)
            out_ref[lines, :] = (run_ref[0, deep, :] * entered + run_ref[1, deep, :]).astype(BF16)
            return carry

        lax.fori_loop(0, BLOCK // SEGS // 2, step, 0)


def state_chunk(place, run, maps, peer_maps, start, first_row, rows):
    width = run.shape[2]
    peers = peer_maps.shape[0]
    vmem = pl.BlockSpec(memory_space=pltpu.VMEM)
    return pl.pallas_call(
        functools.partial(state_kernel, first_row, peers),
        out_shape=jax.ShapeDtypeStruct((rows, width), BF16),
        in_specs=[pl.BlockSpec(memory_space=pltpu.SMEM)] + [vmem] * 4,
        out_specs=vmem,
        scratch_shapes=[pltpu.VMEM((rows // BLOCK * SEGS, width), F32)],
        compiler_params=params(16),
        cost_estimate=cost(2 * rows * width, 10 * rows * width),
    )(place, run, maps, peer_maps, start)


def mix_kernel(groups, group, pieces, peers, slots, final, before, place, *refs):
    count = groups * group
    blocks = refs[:count]
    weights = refs[count : count + len(slots) * 2 * pieces]
    out_ref, lhs, wbuf, acc, lsem, wsem = refs[-6:]
    prev_ref = refs[count + len(weights)] if before else None
    depth = blocks[0].shape[1]
    heights = [blocks[c * group].shape[0] for c in range(groups)]
    lines_of = weights[0].shape[0]
    outer = peers // 2
    here = len(slots) * 2

    def w_copy(n, p):
        w_ref = weights[n * pieces + p]
        dst = wbuf.at[n, p * lines_of : (p + 1) * lines_of, :]
        return pltpu.make_async_copy(w_ref, dst, wsem.at[n, p])

    def l_copy(c, d):
        deep = pl.ds(pl.multiple_of((place[0] ^ d) * depth, depth), depth)
        top = sum(heights[:c])
        dst = lhs.at[top : top + heights[c], deep]
        return pltpu.make_async_copy(blocks[c * group + d], dst, lsem.at[c, d])

    for n in range(here):
        for p in range(pieces):
            w_copy(n, p).start()
    for c in range(groups):
        for d in range(group):
            l_copy(c, d).start()
    for c in range(groups):
        for d in range(group):
            l_copy(c, d).wait()
    span = lines_of * pieces
    for n in range(here):
        source = lax.rem(place[1] // 2 + outer - slots[n // 2], outer)
        owner = source * 2 + (lax.rem(place[1], 2) ^ (n % 2))
        deep = pl.ds(pl.multiple_of(owner * span, span), span)
        for p in range(pieces):
            w_copy(n, p).wait()
        part = jnp.dot(lhs[:, deep], wbuf[n], preferred_element_type=F32)
        if n == 0 and before:
            part = part + prev_ref[...]
        if n > 0:
            part = acc[...] + part
        if n < here - 1:
            acc[...] = part
        elif not final:
            out_ref[...] = part
        else:
            acc[...] = part
            order = row_order(True)
            for m in range(acc.shape[0] // BLOCK):
                lines = slice(m * BLOCK, (m + 1) * BLOCK)
                rounded = acc[lines, :].astype(BF16)
                moved = jnp.dot(order, rounded, preferred_element_type=F32)
                out_ref[lines, :] = moved.astype(BF16)


def mix_rows(place, blocks, weights, slots, prev, final, whole, first, total_rows, pieces):
    groups, group = len(blocks), len(blocks[0])
    depth = blocks[0][0].shape[1]
    lines_of, width = weights[0].shape
    peers = len(weights) // pieces
    rows = sum(g[0].shape[0] for g in blocks)
    used = [weights[(s * 2 + i) * pieces + p] for s in slots for i in range(2) for p in range(pieces)]
    args = [place] + [b for g in blocks for b in g] + used
    in_specs = [pl.BlockSpec(memory_space=pl.ANY)] * (groups * group)
    in_specs += [pl.BlockSpec(memory_space=pltpu.HBM)] * len(used)
    if prev is not None:
        args.append(prev)
        in_specs.append(pl.BlockSpec((rows, width), lambda n, p: (0, 0)))
    aliases = {}
    if whole is not None:
        aliases = {len(args): 0}
        args.append(whole)
        in_specs.append(pl.BlockSpec(memory_space=pl.ANY))
    deep = len(slots) * 2 * pieces * lines_of
    if final:
        out_shape = jax.ShapeDtypeStruct((total_rows, width), BF16)
        out_spec = pl.BlockSpec((rows, width), lambda n, p: (first // rows, 0))
    else:
        out_shape = jax.ShapeDtypeStruct((rows, width), F32)
        out_spec = pl.BlockSpec((rows, width), lambda n, p: (0, 0))
    return pl.pallas_call(
        functools.partial(
            mix_kernel, groups, group, pieces, peers, tuple(slots), final, prev is not None
        ),
        out_shape=out_shape,
        grid_spec=pltpu.PrefetchScalarGridSpec(
            num_scalar_prefetch=1,
            grid=(1,),
            in_specs=in_specs,
            out_specs=out_spec,
            scratch_shapes=[
                pltpu.VMEM((rows, group * depth), BF16),
                pltpu.VMEM((len(slots) * 2, lines_of * pieces, width), BF16),
                pltpu.VMEM((rows, width), F32),
                pltpu.SemaphoreType.DMA((groups, group)),
                pltpu.SemaphoreType.DMA((len(slots) * 2, pieces)),
            ],
        ),
        input_output_aliases=aliases,
        compiler_params=params(40 if peers <= 8 else 62),
        cost_estimate=cost(2 * rows * deep * width, 2 * deep * (width + rows) + 4 * rows * width),
    )(*args)


EARLY = 5
SHARES = (2, 1, 1)


def pieces_of(lines_of):
    return 2 if lines_of % (4 * LANES) == 0 else 1


class Ring:
    def __init__(self, w_output):
        self.peers = lax.axis_size("ctx")
        self.outer = self.peers // 2
        self.pieces = pieces_of(w_output.shape[0])
        lines_of = w_output.shape[0] // self.pieces
        self.held = {}
        for p in range(self.pieces):
            self.held[0, 0, p] = w_output[p * lines_of : (p + 1) * lines_of]

    def ring_step(self, n, gate=None):
        s, p = n // self.pieces + 1, n % self.pieces
        block = self.held[s - 1, 0, p]
        if gate is not None:
            block, _ = lax.optimization_barrier((block, gate))
        route = [(i, (i + 2) % self.peers) for i in range(self.peers)]
        self.held[s, 0, p] = lax.ppermute(block, "ctx", route)

    def swap_step(self, n, gate=None):
        s, p = n // self.pieces, n % self.pieces
        block = self.held[s, 0, p]
        if gate is not None:
            block, _ = lax.optimization_barrier((block, gate))
        self.held[s, 1, p] = swap(block, "ctx", 1)

    def run(self, gate):
        rings, swaps = (self.outer - 1) * self.pieces, self.outer * self.pieces
        for n in range(max(rings, swaps)):
            g = gate if n >= EARLY else None
            if n < rings:
                self.ring_step(n, g)
            if n < swaps:
                self.swap_step(n, g)

    def blocks(self):
        steps = [(s, i) for s in range(self.outer) for i in range(2)]
        return [self.held[s, i, p] for s, i in steps for p in range(self.pieces)]


def layer(tokens, w_input, w_output, bias_update, bias_cand, recur_gain, start_state):
    peers = lax.axis_size("ctx")
    group = lax.axis_size("ch")
    half = group // 2
    total_rows = tokens.shape[0]
    chunks = len(SHARES)
    sizes = [total_rows * share // sum(SHARES) for share in SHARES]
    firsts = [sum(sizes[:c]) for c in range(chunks)]
    place = jnp.stack([lax.axis_index("ch"), lax.axis_index("ctx")]).astype(jnp.int32)
    biases = jnp.stack([bias_update, bias_cand], axis=0)
    gain = recur_gain[None, :]
    start = start_state[None, :]

    (head,) = split_rows(tokens, 0, sizes[:1], False)
    *others, tail = split_rows(tokens, sizes[0], sizes[1:], True)
    far = []
    for piece in [head, *others]:
        far.append([swap(piece, "ch", half)])
    near = [[head, tail]]
    for d in range(1, half):
        near.append([swap(head, "ch", d)])
        near[d].append(swap(tail, "ch", d))
    for c in range(chunks):
        for d in range(1, half):
            far[c].append(swap(far[c][0], "ch", d))

    partial = near_product(place, near, w_input)
    gates, maps = [], []
    for c in range(chunks):
        last = c == chunks - 1
        out = gate_chunk(
            place,
            far[c],
            partial,
            w_input,
            biases,
            gain,
            start,
            maps if last else [],
            firsts[c],
            last,
            peers,
        )
        gates.append(out[0])
        maps.append(out[1])
    peer_maps = lax.all_to_all(out[2], "ctx", 0, 0, tiled=True)
    run, run_maps, totals = bend_all(place, gates, maps, peer_maps, gain, start)
    peer_maps = lax.all_to_all(totals, "ctx", 0, 0, tiled=True)
    ring = Ring(w_output)
    ring.run(peer_maps)

    blocks = []
    for c in range(chunks):
        own = state_chunk(place, run, run_maps, peer_maps, start, firsts[c], sizes[c])
        across = swap(own, "ch", half)
        blocks.append([own, across])
    for c in range(chunks):
        own, across = blocks[c]
        lows, highs = [own], [across]
        for d in range(1, half):
            lows.append(swap(own, "ch", d))
            highs.append(swap(across, "ch", d))
        blocks[c] = lows + highs
    weights = ring.blocks()
    late = max(1, ring.outer // 4)
    slots = list(range(ring.outer))

    def mix(c, used, prev, final, whole):
        return mix_rows(
            place,
            blocks[c : c + 1],
            weights,
            used,
            prev,
            final,
            whole,
            firsts[c],
            total_rows,
            ring.pieces,
        )

    partial = mix(0, slots[:-late], None, False, None)
    mixed = mix(0, slots[-late:], partial, True, None)
    for c in range(1, chunks):
        mixed = mix(c, slots, None, True, mixed)
    return mixed


def solution(mesh):
    return jax.shard_map(
        layer,
        mesh=mesh,
        in_specs=(
            P("ctx", "ch"),
            P(None, None, "ch"),
            P("ctx", "ch"),
            P("ch"),
            P("ch"),
            P("ch"),
            P("ch"),
        ),
        out_specs=P("ctx", "ch"),
        check_vma=False,
    )
```

```python
import functools
import math

import jax
import jax.numpy as jnp
from jax import lax
from jax.experimental import pallas as pl
from jax.experimental.pallas import tpu as pltpu
from jax.sharding import PartitionSpec as P


SEGS = 8
LANES = 128
BLOCK = 256
F32 = jnp.float32
BF16 = jnp.bfloat16
MIB = 1024 * 1024


def swap(block, axis, bits):
    return lax.ppermute(block, axis, [(i, i ^ bits) for i in range(lax.axis_size(axis))])


def tile_of(width, most):
    return math.gcd(width, most)


def params(mib):
    return pltpu.CompilerParams(vmem_limit_bytes=mib * MIB)


def cost(flops, nbytes, trans=0):
    return pl.CostEstimate(flops=int(flops), bytes_accessed=int(nbytes), transcendentals=int(trans))


def near_kernel(half, tiles, heights, place, *refs):
    count = len(heights)
    blocks = refs[: half * count]
    w_ref, out_ref, lhs, wbuf, lsem, wsem = refs[half * count :]
    depth = blocks[0].shape[1]
    span = wbuf.shape[2]
    slot = lax.rem(place[0], half)
    base = (place[0] // half) * (half * depth)

    def w_copy(n):
        lines = pl.ds(pl.multiple_of(base, half * depth), half * depth)
        wide = pl.ds(pl.multiple_of(lax.rem(n, tiles) * span, span), span)
        return pltpu.make_async_copy(w_ref.at[n // tiles, lines, wide], wbuf.at[n], wsem.at[n])

    def l_copy(d, k):
        deep = pl.ds(pl.multiple_of((slot ^ d) * depth, depth), depth)
        top = sum(heights[:k])
        dst = lhs.at[top : top + heights[k], deep]
        return pltpu.make_async_copy(blocks[d * count + k], dst, lsem.at[d, k])

    steps = wbuf.shape[0]
    for n in range(steps):
        w_copy(n).start()
    for d in range(half):
        for k in range(count):
            l_copy(d, k).start()
    for d in range(half):
        for k in range(count):
            l_copy(d, k).wait()

    def body(n, carry):
        w_copy(n).wait()
        wide = pl.ds(pl.multiple_of(lax.rem(n, tiles) * span, span), span)
        total = None
        for d in range(half):
            deep = slice(d * depth, (d + 1) * depth)
            part = jnp.dot(lhs[:, deep], wbuf[n, deep, :], preferred_element_type=F32)
            total = part if total is None else total + part
        out_ref[n // tiles, :, wide] = total
        return carry

    lax.fori_loop(0, steps, body, 0)


def near_product(place, blocks, weights):
    half = len(blocks)
    heights = tuple(b.shape[0] for b in blocks[0])
    rows, depth = sum(heights), blocks[0][0].shape[1]
    gates, _, width = weights.shape
    span = tile_of(width, 512)
    tiles = width // span
    return pl.pallas_call(
        functools.partial(near_kernel, half, tiles, heights),
        out_shape=jax.ShapeDtypeStruct((gates, rows, width), F32),
        in_specs=[pl.BlockSpec(memory_space=pltpu.SMEM)]
        + [pl.BlockSpec(memory_space=pl.ANY)] * (half * len(heights))
        + [pl.BlockSpec(memory_space=pltpu.HBM)],
        out_specs=pl.BlockSpec(memory_space=pltpu.VMEM),
        scratch_shapes=[
            pltpu.VMEM((rows, half * depth), BF16),
            pltpu.VMEM((gates * tiles, half * depth, span), BF16),
            pltpu.SemaphoreType.DMA((half, len(heights))),
            pltpu.SemaphoreType.DMA((gates * tiles,)),
        ],
        compiler_params=params(28),
        cost_estimate=cost(
            2 * gates * rows * half * depth * width,
            gates * width * (half * depth * 2 + rows * 4) + half * rows * depth * 2,
        ),
    )(place, *[piece for block in blocks for piece in block], weights)


def row_order(transposed):
    shape = (BLOCK, BLOCK)
    row = lax.broadcasted_iota(jnp.int32, shape, 1 if transposed else 0)
    token = lax.broadcasted_iota(jnp.int32, shape, 0 if transposed else 1)
    chosen = lax.rem(row, SEGS) * (BLOCK // SEGS) + row // SEGS == token
    return jnp.where(chosen, 1.0, 0.0).astype(BF16)


def split_kernel(first, sizes, joined, src, *refs):
    count = len(sizes)
    outs = refs[:count]
    buf, sem = refs[-2:]
    blocks = sum(sizes) // BLOCK
    copies = []
    for k in range(blocks):
        lines = pl.ds(first + k * BLOCK, BLOCK)
        copies.append(pltpu.make_async_copy(src.at[lines, :], buf.at[k], sem.at[k]))
    for copy in copies:
        copy.start()
    order = row_order(False)
    k = 0
    for c in range(count):
        for r in range(sizes[c] // BLOCK):
            copies[k].wait()
            moved = jnp.dot(order, buf[k], preferred_element_type=F32).astype(BF16)
            outs[c][r * BLOCK : (r + 1) * BLOCK, :] = moved
            if joined:
                refs[count][k * BLOCK : (k + 1) * BLOCK, :] = moved
            k += 1


def split_rows(array, first, sizes, joined):
    vmem = pl.BlockSpec(memory_space=pltpu.VMEM)
    rows, width = sum(sizes), array.shape[1]
    shapes = list(sizes) + ([rows] if joined else [])
    return pl.pallas_call(
        functools.partial(split_kernel, first, tuple(sizes), joined),
        out_shape=[jax.ShapeDtypeStruct((r, width), array.dtype) for r in shapes],
        in_specs=[pl.BlockSpec(memory_space=pltpu.HBM)],
        out_specs=[vmem] * len(shapes),
        scratch_shapes=[
            pltpu.VMEM((rows // BLOCK, BLOCK, width), BF16),
            pltpu.SemaphoreType.DMA((rows // BLOCK,)),
        ],
        compiler_params=params(12),
        cost_estimate=cost(2 * rows * BLOCK * width, 4 * rows * width),
    )(array)


def compose_rows(maps, cols, a, b):
    for k in range(maps.shape[1]):
        slope = maps[0, k : k + 1, cols]
        shift = maps[1, k : k + 1, cols]
        b = slope * b + shift
        a = slope * a
    return a, b


def first_slopes(pre, cand, gain):
    update = jax.nn.sigmoid(pre)
    keep = 1.0 - update
    scaled = update * gain
    squashed = jnp.tanh(cand)
    slope = keep + (scaled - scaled * squashed * squashed)
    return update, keep, scaled, slope, update * squashed


def lead_row(place, start, shape):
    lead = lax.broadcasted_iota(jnp.int32, shape, 0) == 0
    return jnp.where(lead & (place[1] == 0), start, 0.0)


def around(update, keep, scaled, cand, gain, prev):
    squashed = jnp.tanh(cand + gain * prev)
    bend = scaled - scaled * squashed * squashed
    return keep + bend, update * squashed - bend * prev


def gate_kernel(half, first_row, rows, first_col, before, last, place, *refs):
    blocks = refs[:half]
    part_ref, w_ref, bias_ref, gain_ref, start_ref = refs[half : half + 5]
    earlier = refs[half + 5 : half + 5 + before]
    rest = refs[half + 5 + before :]
    if last:
        gates_ref, maps_ref, total_ref = rest[:3]
    else:
        gates_ref, maps_ref = rest[:2]
    wbuf, acc, wsem = rest[-3:]
    depth = blocks[0].shape[1]
    width = acc.shape[2]
    cols = slice(first_col, first_col + width)
    seg = BLOCK // SEGS
    count = rows // BLOCK
    lines_of = wbuf.shape[3]
    parts = depth // lines_of
    slot = lax.rem(place[0], half)
    base = ((place[0] // half) ^ 1) * (half * depth)

    def w_copy(g, d, q):
        top = base + (slot ^ d) * depth + q * lines_of
        lines = pl.ds(pl.multiple_of(top, lines_of), lines_of)
        return pltpu.make_async_copy(w_ref.at[g, lines, cols], wbuf.at[g, d, q], wsem.at[g, d, q])

    every = [(d, q) for d in range(half) for q in range(parts)]
    for g in range(2):
        for d, q in every:
            w_copy(g, d, q).start()
    for g in range(2):
        for d, q in every:
            w_copy(g, d, q).wait()
            deep = slice(q * lines_of, (q + 1) * lines_of)
            part = jnp.dot(blocks[d][:, deep], wbuf[g, d, q], preferred_element_type=F32)
            if (d, q) == (0, 0):
                acc[g] = part
            else:
                acc[g] += part

    span = tile_of(width, 512)

    def columns(n, carry_out):
        wide = pl.ds(pl.multiple_of(n * span, span), span)
        there = pl.ds(pl.multiple_of(first_col + n * span, span), span)
        gain = jnp.broadcast_to(gain_ref[:, there], (SEGS, span))
        bias = [jnp.broadcast_to(bias_ref[g : g + 1, there], (2 * SEGS, span)) for g in range(2)]

        def pair(jj, carry, first):
            out = []
            for c in range(count):
                a, b = carry[c]
                lines = pl.ds(pl.multiple_of(c * BLOCK + jj * 2 * SEGS, 2 * SEGS), 2 * SEGS)
                deep = pl.ds(
                    pl.multiple_of(first_row + c * BLOCK + jj * 2 * SEGS, 2 * SEGS), 2 * SEGS
                )
                held = []
                for g in range(2):
                    total = acc[g, lines, wide] + part_ref[g, deep, there] + bias[g]
                    rounded = total.astype(BF16)
                    gates_ref[g, lines, wide] = rounded
                    held.append(rounded.astype(F32))
                for k in range(2):
                    pre = held[0][k * SEGS : (k + 1) * SEGS]
                    cand = held[1][k * SEGS : (k + 1) * SEGS]
                    update, keep, scaled, slope, offset = first_slopes(pre, cand, gain)
                    if first and k == 0 and c == 0:
                        prev = lead_row(place, start_ref[:, there], (SEGS, span))
                        slope, offset = around(update, keep, scaled, cand, gain, prev)
                    b = slope * b + offset
                    a = slope * a
                out.append((a, b))
            return tuple(out)

        carry = ((jnp.ones((SEGS, span), F32), jnp.zeros((SEGS, span), F32)),) * count
        begin = 0
        if first_row == 0:
            carry = pair(0, carry, True)
            begin = 1
        carry = lax.fori_loop(begin, seg // 2, lambda jj, c: pair(jj, c, False), carry)
        for c in range(count):
            maps_ref[0, c * SEGS : (c + 1) * SEGS, wide] = carry[c][0]
            maps_ref[1, c * SEGS : (c + 1) * SEGS, wide] = carry[c][1]
        return carry_out

    lax.fori_loop(0, width // span, columns, 0)
    if last:
        ta, tb = jnp.ones((1, width), F32), jnp.zeros((1, width), F32)
        for maps in earlier:
            ta, tb = compose_rows(maps, cols, ta, tb)
        ta, tb = compose_rows(maps_ref, slice(0, width), ta, tb)
        for i in range(total_ref.shape[0]):
            total_ref[i, 0:1, :] = ta
            total_ref[i, 1:2, :] = tb


def gate_chunk(
    place, blocks, partial, weights, biases, gain, start, earlier, first_row, window, last, peers
):
    half = len(blocks)
    rows, depth = blocks[0].shape
    gates = weights.shape[0]
    first_col, width = window
    lines_of = tile_of(depth, 512)
    vmem = pl.BlockSpec(memory_space=pltpu.VMEM)
    out_shape = [
        jax.ShapeDtypeStruct((2, rows, width), BF16),
        jax.ShapeDtypeStruct((2, rows // BLOCK * SEGS, width), F32),
    ]
    if last:
        out_shape.append(jax.ShapeDtypeStruct((peers, 2, width), F32))
    return pl.pallas_call(
        functools.partial(gate_kernel, half, first_row, rows, first_col, len(earlier), last),
        out_shape=out_shape,
        in_specs=[pl.BlockSpec(memory_space=pltpu.SMEM)]
        + [vmem] * (half + 1)
        + [pl.BlockSpec(memory_space=pltpu.HBM)]
        + [vmem] * (3 + len(earlier)),
        out_specs=[vmem] * len(out_shape),
        scratch_shapes=[
            pltpu.VMEM((gates, half, depth // lines_of, lines_of, width), BF16),
            pltpu.VMEM((gates, rows, width), F32),
            pltpu.SemaphoreType.DMA((gates, half, depth // lines_of)),
        ],
        compiler_params=params(32),
        cost_estimate=cost(
            2 * gates * rows * half * depth * width,
            gates * width * (half * depth * 2 + rows * 6) + half * rows * depth * 2,
            4 * rows * width,
        ),
    )(place, *blocks, partial, weights, biases, gain, start, *earlier)


def entering_state(place, peer_maps, start, peers):
    state = start
    for k in range(peers):
        moved = peer_maps[k, 0:1, :] * state + peer_maps[k, 1:2, :]
        state = jnp.where(place[1] > k, moved, state)
    return state


def enter_segments(maps_list, state, enter):
    row = 0
    for maps in maps_list:
        for k in range(maps.shape[1]):
            enter[row : row + 1, :] = state
            state = maps[0, k : k + 1, :] * state + maps[1, k : k + 1, :]
            row += 1


def bend_kernel(chunks, peers, place, *refs):
    gates = refs[:chunks]
    maps = refs[chunks : 2 * chunks]
    peer_ref, gain_ref, start_ref, run_ref, maps_ref, total_ref, enter = refs[2 * chunks :]
    span = gates[0].shape[2]
    width = gain_ref.shape[1]
    where = [(c, r * BLOCK) for c in range(chunks) for r in range(gates[c].shape[1] // BLOCK)]
    n = pl.program_id(0)

    @pl.when(n == 0)
    def _():
        enter_segments(maps, entering_state(place, peer_ref, start_ref[...], peers), enter)

    wide = pl.ds(pl.multiple_of(n * span, span), span)
    gain = jnp.broadcast_to(gain_ref[:, wide], (SEGS, span))

    def advance(block, jj, held, first):
        state, a, b = held
        c, top = where[block]
        lines = pl.ds(pl.multiple_of(top + jj * 2 * SEGS, 2 * SEGS), 2 * SEGS)
        pre2 = gates[c][0, lines, :].astype(F32)
        cand2 = gates[c][1, lines, :].astype(F32)
        for k in range(2):
            pre = pre2[k * SEGS : (k + 1) * SEGS]
            cand = cand2[k * SEGS : (k + 1) * SEGS]
            update, keep, scaled, slope, offset = first_slopes(pre, cand, gain)
            if first and k == 0 and block == 0:
                prev = lead_row(place, start_ref[:, wide], (SEGS, span))
                slope, offset = around(update, keep, scaled, cand, gain, prev)
            slope2, offset2 = around(update, keep, scaled, cand, gain, state)
            state = slope * state + offset
            b = slope2 * b + offset2
            a = slope2 * a
            row = pl.ds(pl.multiple_of(block * BLOCK + (2 * jj + k) * SEGS, SEGS), SEGS)
            run_ref[0, row, :] = a
            run_ref[1, row, :] = b
        return state, a, b

    def pair(jj, carry, first):
        return tuple(advance(m, jj, carry[m], first) for m in range(len(where)))

    one, zero = jnp.ones((SEGS, span), F32), jnp.zeros((SEGS, span), F32)
    carry = tuple((enter[m * SEGS : (m + 1) * SEGS, wide], one, zero) for m in range(len(where)))
    carry = pair(0, carry, True)
    carry = lax.fori_loop(1, BLOCK // SEGS // 2, lambda jj, c: pair(jj, c, False), carry)
    for m in range(len(where)):
        maps_ref[0, m * SEGS : (m + 1) * SEGS, wide] = carry[m][1]
        maps_ref[1, m * SEGS : (m + 1) * SEGS, wide] = carry[m][2]

    @pl.when(n == pl.num_programs(0) - 1)
    def _():
        ta, tb = jnp.ones((1, width), F32), jnp.zeros((1, width), F32)
        ta, tb = compose_rows(maps_ref, slice(0, width), ta, tb)
        for i in range(peers):
            total_ref[i, 0:1, :] = ta
            total_ref[i, 1:2, :] = tb


def bend_all(place, gates, maps, peer_maps, gain, start, window):
    chunks = len(gates)
    peers = peer_maps.shape[0]
    first_col, width = window
    total_rows = sum(g.shape[1] for g in gates)
    segs = total_rows // BLOCK * SEGS
    tn = tile_of(width, 256)
    row_spec = pl.BlockSpec((1, width), lambda n, p: (0, first_col // width))

    def columns(array, shape, wide):
        offset = first_col // wide if array.shape[2] > width else 0
        if wide == width:
            return pl.BlockSpec(shape, lambda n, p: (0, 0, offset))
        return pl.BlockSpec(shape, lambda n, p: (0, 0, n + offset))

    total_spec = pl.BlockSpec((peers, 2, width), lambda n, p: (0, 0, 0))
    return pl.pallas_call(
        functools.partial(bend_kernel, chunks, peers),
        out_shape=[
            jax.ShapeDtypeStruct((2, total_rows, width), F32),
            jax.ShapeDtypeStruct((2, segs, width), F32),
            jax.ShapeDtypeStruct((peers, 2, width), F32),
        ],
        grid_spec=pltpu.PrefetchScalarGridSpec(
            num_scalar_prefetch=1,
            grid=(width // tn,),
            in_specs=[columns(g, (2, g.shape[1], tn), tn) for g in gates]
            + [columns(m, (2, m.shape[1], width), width) for m in maps]
            + [total_spec, row_spec, row_spec],
            out_specs=[
                pl.BlockSpec((2, total_rows, tn), lambda n, p: (0, 0, n)),
                pl.BlockSpec((2, segs, width), lambda n, p: (0, 0, 0)),
                total_spec,
            ],
            scratch_shapes=[pltpu.VMEM((segs, width), F32)],
        ),
        compiler_params=params(16),
        cost_estimate=cost(
            40 * total_rows * width, 12 * total_rows * width, 5 * total_rows * width
        ),
    )(place, *gates, *maps, peer_maps, gain, start)


def state_kernel(first_row, first_cols, peers, place, *refs):
    sides = len(first_cols)
    start_ref, out_ref, enter = refs[3 * sides :]
    rows = out_ref.shape[0]
    begin = first_row // BLOCK * SEGS
    for m in range(sides):
        run_ref, maps_ref, peer_ref = refs[3 * m : 3 * m + 3]
        width = run_ref.shape[2]
        cols = slice(m * width, (m + 1) * width)
        start = start_ref[:, first_cols[m] : first_cols[m] + width]
        state = entering_state(place, peer_ref, start, peers)
        for k in range(begin + rows // BLOCK * SEGS):
            if k >= begin:
                enter[k - begin : k - begin + 1, :] = state
            state = maps_ref[0, k : k + 1, :] * state + maps_ref[1, k : k + 1, :]
        for c in range(rows // BLOCK):
            once = enter[c * SEGS : (c + 1) * SEGS, :]
            entered = jnp.concatenate([once, once], axis=0)

            def step(jj, carry):
                at = pl.multiple_of(c * BLOCK + jj * 2 * SEGS, 2 * SEGS)
                lines = pl.ds(at, 2 * SEGS)
                deep = pl.ds(pl.multiple_of(first_row + at, 2 * SEGS), 2 * SEGS)
                now = run_ref[0, deep, :] * entered + run_ref[1, deep, :]
                out_ref[lines, cols] = now.astype(BF16)
                return carry

            lax.fori_loop(0, BLOCK // SEGS // 2, step, 0)


def state_chunk(place, sides, start, first_row, rows):
    peers = sides[0][3].shape[0]
    widths = [side[1].shape[2] for side in sides]
    vmem = pl.BlockSpec(memory_space=pltpu.VMEM)
    first_cols = tuple(side[0] for side in sides)
    return pl.pallas_call(
        functools.partial(state_kernel, first_row, first_cols, peers),
        out_shape=jax.ShapeDtypeStruct((rows, sum(widths)), BF16),
        in_specs=[pl.BlockSpec(memory_space=pltpu.SMEM)] + [vmem] * (3 * len(sides) + 1),
        out_specs=vmem,
        scratch_shapes=[pltpu.VMEM((rows // BLOCK * SEGS, widths[0]), F32)],
        compiler_params=params(16),
        cost_estimate=cost(2 * rows * sum(widths), 10 * rows * sum(widths)),
    )(place, *[part for side in sides for part in side[1:]], start)


def mix_kernel(sides, group, pieces, peers, slots, final, before, place, *refs):
    count = sides * group
    blocks = refs[:count]
    weights = refs[count : count + len(slots) * 2 * pieces]
    out_ref, lhs, wbuf, acc, lsem, wsem = refs[-6:]
    prev_ref = refs[count + len(weights)] if before else None
    part_of = blocks[0].shape[1]
    depth = part_of * sides
    lines_of = weights[0].shape[0]
    outer = peers // 2
    here = len(slots) * 2

    def w_copy(n, p):
        w_ref = weights[n * pieces + p]
        dst = wbuf.at[n, p * lines_of : (p + 1) * lines_of, :]
        return pltpu.make_async_copy(w_ref, dst, wsem.at[n, p])

    def l_copy(c, d):
        at = pl.multiple_of((place[0] ^ d) * depth + c * part_of, part_of)
        return pltpu.make_async_copy(
            blocks[c * group + d], lhs.at[:, pl.ds(at, part_of)], lsem.at[c, d]
        )

    for n in range(here):
        for p in range(pieces):
            w_copy(n, p).start()
    for c in range(sides):
        for d in range(group):
            l_copy(c, d).start()
    for c in range(sides):
        for d in range(group):
            l_copy(c, d).wait()
    span = lines_of * pieces
    for n in range(here):
        source = lax.rem(place[1] // 2 + outer - slots[n // 2], outer)
        owner = source * 2 + (lax.rem(place[1], 2) ^ (n % 2))
        deep = pl.ds(pl.multiple_of(owner * span, span), span)
        for p in range(pieces):
            w_copy(n, p).wait()
        part = jnp.dot(lhs[:, deep], wbuf[n], preferred_element_type=F32)
        if n == 0 and before:
            part = part + prev_ref[...]
        if n > 0:
            part = acc[...] + part
        if n < here - 1:
            acc[...] = part
        elif not final:
            out_ref[...] = part
        else:
            acc[...] = part
            order = row_order(True)
            for m in range(acc.shape[0] // BLOCK):
                lines = slice(m * BLOCK, (m + 1) * BLOCK)
                rounded = acc[lines, :].astype(BF16)
                moved = jnp.dot(order, rounded, preferred_element_type=F32)
                out_ref[lines, :] = moved.astype(BF16)


def mix_rows(place, blocks, weights, slots, prev, final, whole, first, total_rows, pieces):
    sides, group = len(blocks), len(blocks[0])
    depth = blocks[0][0].shape[1] * sides
    lines_of, width = weights[0].shape
    peers = len(weights) // pieces
    rows = blocks[0][0].shape[0]
    used = [weights[(s * 2 + i) * pieces + p] for s in slots for i in range(2) for p in range(pieces)]
    args = [place] + [b for g in blocks for b in g] + used
    in_specs = [pl.BlockSpec(memory_space=pl.ANY)] * (sides * group)
    in_specs += [pl.BlockSpec(memory_space=pltpu.HBM)] * len(used)
    if prev is not None:
        args.append(prev)
        in_specs.append(pl.BlockSpec((rows, width), lambda n, p: (0, 0)))
    aliases = {}
    if whole is not None:
        aliases = {len(args): 0}
        args.append(whole)
        in_specs.append(pl.BlockSpec(memory_space=pl.ANY))
    deep = len(slots) * 2 * pieces * lines_of
    if final:
        out_shape = jax.ShapeDtypeStruct((total_rows, width), BF16)
        out_spec = pl.BlockSpec((rows, width), lambda n, p: (first // rows, 0))
    else:
        out_shape = jax.ShapeDtypeStruct((rows, width), F32)
        out_spec = pl.BlockSpec((rows, width), lambda n, p: (0, 0))
    return pl.pallas_call(
        functools.partial(
            mix_kernel, sides, group, pieces, peers, tuple(slots), final, prev is not None
        ),
        out_shape=out_shape,
        grid_spec=pltpu.PrefetchScalarGridSpec(
            num_scalar_prefetch=1,
            grid=(1,),
            in_specs=in_specs,
            out_specs=out_spec,
            scratch_shapes=[
                pltpu.VMEM((rows, group * depth), BF16),
                pltpu.VMEM((len(slots) * 2, lines_of * pieces, width), BF16),
                pltpu.VMEM((rows, width), F32),
                pltpu.SemaphoreType.DMA((sides, group)),
                pltpu.SemaphoreType.DMA((len(slots) * 2, pieces)),
            ],
        ),
        input_output_aliases=aliases,
        compiler_params=params(40 if peers <= 8 else 62),
        cost_estimate=cost(2 * rows * deep * width, 2 * deep * (width + rows) + 4 * rows * width),
    )(*args)


EARLY = 5
SHARES = (2, 1, 1)


def pieces_of(lines_of):
    return 2 if lines_of % (4 * LANES) == 0 else 1


class Ring:
    def __init__(self, w_output):
        self.peers = lax.axis_size("ctx")
        self.outer = self.peers // 2
        self.pieces = pieces_of(w_output.shape[0])
        lines_of = w_output.shape[0] // self.pieces
        self.held = {}
        for p in range(self.pieces):
            self.held[0, 0, p] = w_output[p * lines_of : (p + 1) * lines_of]

    def ring_step(self, n, gate=None):
        s, p = n // self.pieces + 1, n % self.pieces
        block = self.held[s - 1, 0, p]
        if gate is not None:
            block, _ = lax.optimization_barrier((block, gate))
        route = [(i, (i + 2) % self.peers) for i in range(self.peers)]
        self.held[s, 0, p] = lax.ppermute(block, "ctx", route)

    def swap_step(self, n, gate=None):
        s, p = n // self.pieces, n % self.pieces
        block = self.held[s, 0, p]
        if gate is not None:
            block, _ = lax.optimization_barrier((block, gate))
        self.held[s, 1, p] = swap(block, "ctx", 1)

    def run(self, gate):
        rings, swaps = (self.outer - 1) * self.pieces, self.outer * self.pieces
        for n in range(max(rings, swaps)):
            g = gate if n >= EARLY else None
            if n < rings:
                self.ring_step(n, g)
            if n < swaps:
                self.swap_step(n, g)

    def blocks(self):
        steps = [(s, i) for s in range(self.outer) for i in range(2)]
        return [self.held[s, i, p] for s, i in steps for p in range(self.pieces)]


def layer(tokens, w_input, w_output, bias_update, bias_cand, recur_gain, start_state):
    peers = lax.axis_size("ctx")
    group = lax.axis_size("ch")
    half = group // 2
    total_rows = tokens.shape[0]
    chunks = len(SHARES)
    sizes = [total_rows * share // sum(SHARES) for share in SHARES]
    firsts = [sum(sizes[:c]) for c in range(chunks)]
    place = jnp.stack([lax.axis_index("ch"), lax.axis_index("ctx")]).astype(jnp.int32)
    biases = jnp.stack([bias_update, bias_cand], axis=0)
    gain = recur_gain[None, :]
    start = start_state[None, :]

    (head,) = split_rows(tokens, 0, sizes[:1], False)
    *others, tail = split_rows(tokens, sizes[0], sizes[1:], True)
    far = []
    for piece in [head, *others]:
        far.append([swap(piece, "ch", half)])
    near = [[head, tail]]
    for d in range(1, half):
        near.append([swap(head, "ch", d)])
        near[d].append(swap(tail, "ch", d))
    for c in range(chunks):
        for d in range(1, half):
            far[c].append(swap(far[c][0], "ch", d))

    partial = near_product(place, near, w_input)
    width = w_input.shape[2]
    gates, maps = [], []
    for c in range(chunks - 1):
        out = gate_chunk(
            place,
            far[c],
            partial,
            w_input,
            biases,
            gain,
            start,
            [],
            firsts[c],
            (0, width),
            False,
            peers,
        )
        gates.append(out[0])
        maps.append(out[1])
    windows = [(0, width // 2), (width // 2, width // 2)]
    sides = []
    for window in windows:
        out = gate_chunk(
            place,
            far[-1],
            partial,
            w_input,
            biases,
            gain,
            start,
            maps,
            firsts[-1],
            window,
            True,
            peers,
        )
        peer_maps = lax.all_to_all(out[2], "ctx", 0, 0, tiled=True)
        sides.append((out[0], out[1], peer_maps))
    for m, window in enumerate(windows):
        run, run_maps, totals = bend_all(
            place, gates + [sides[m][0]], maps + [sides[m][1]], sides[m][2], gain, start, window
        )
        peer_maps = lax.all_to_all(totals, "ctx", 0, 0, tiled=True)
        sides[m] = (window[0], run, run_maps, peer_maps)
    ring = Ring(w_output)
    ring.run(peer_maps)

    plan = [(f"0{m}", 0, [sides[m]]) for m in range(len(sides))]
    plan += [(f"{c}0", c, sides) for c in range(1, chunks)]
    sent = []
    for label, c, used in plan:
        own = state_chunk(place, used, start, firsts[c], sizes[c])
        sent.append((label, c, own, swap(own, "ch", half)))
    blocks = [[] for _ in range(chunks)]
    for label, c, own, across in sent:
        lows, highs = [own], [across]
        for d in range(1, half):
            lows.append(swap(own, "ch", d))
            highs.append(swap(across, "ch", d))
        blocks[c].append(lows + highs)
    weights = ring.blocks()
    late = max(1, ring.outer // 4)
    slots = list(range(ring.outer))

    def mix(c, used, prev, final, whole):
        return mix_rows(
            place,
            blocks[c],
            weights,
            used,
            prev,
            final,
            whole,
            firsts[c],
            total_rows,
            ring.pieces,
        )

    partial = mix(0, slots[:-late], None, False, None)
    mixed = mix(0, slots[-late:], partial, True, None)
    for c in range(1, chunks):
        mixed = mix(c, slots, None, True, mixed)
    return mixed


def solution(mesh):
    return jax.shard_map(
        layer,
        mesh=mesh,
        in_specs=(
            P("ctx", "ch"),
            P(None, None, "ch"),
            P("ctx", "ch"),
            P("ch"),
            P("ch"),
            P("ch"),
            P("ch"),
        ),
        out_specs=P("ctx", "ch"),
        check_vma=False,
    )
```

```python
import functools
import math

import jax
import jax.numpy as jnp
from jax import lax
from jax.experimental import pallas as pl
from jax.experimental.pallas import tpu as pltpu
from jax.sharding import PartitionSpec as P


SEGS = 8
LANES = 128
BLOCK = 256
F32 = jnp.float32
BF16 = jnp.bfloat16
MIB = 1024 * 1024


def swap(block, axis, bits):
    return lax.ppermute(block, axis, [(i, i ^ bits) for i in range(lax.axis_size(axis))])


def tile_of(width, most):
    return math.gcd(width, most)


def params(mib):
    return pltpu.CompilerParams(vmem_limit_bytes=mib * MIB)


def cost(flops, nbytes, trans=0):
    return pl.CostEstimate(flops=int(flops), bytes_accessed=int(nbytes), transcendentals=int(trans))


def near_kernel(half, tiles, heights, place, *refs):
    count = len(heights)
    blocks = refs[: half * count]
    w_ref, out_ref, lhs, wbuf, lsem, wsem = refs[half * count :]
    depth = blocks[0].shape[1]
    span = wbuf.shape[2]
    slot = lax.rem(place[0], half)
    base = (place[0] // half) * (half * depth)

    def w_copy(n):
        lines = pl.ds(pl.multiple_of(base, half * depth), half * depth)
        wide = pl.ds(pl.multiple_of(lax.rem(n, tiles) * span, span), span)
        return pltpu.make_async_copy(w_ref.at[n // tiles, lines, wide], wbuf.at[n], wsem.at[n])

    def l_copy(d, k):
        deep = pl.ds(pl.multiple_of((slot ^ d) * depth, depth), depth)
        top = sum(heights[:k])
        dst = lhs.at[top : top + heights[k], deep]
        return pltpu.make_async_copy(blocks[d * count + k], dst, lsem.at[d, k])

    steps = wbuf.shape[0]
    for n in range(steps):
        w_copy(n).start()
    for d in range(half):
        for k in range(count):
            l_copy(d, k).start()
    for d in range(half):
        for k in range(count):
            l_copy(d, k).wait()

    def body(n, carry):
        w_copy(n).wait()
        wide = pl.ds(pl.multiple_of(lax.rem(n, tiles) * span, span), span)
        total = None
        for d in range(half):
            deep = slice(d * depth, (d + 1) * depth)
            part = jnp.dot(lhs[:, deep], wbuf[n, deep, :], preferred_element_type=F32)
            total = part if total is None else total + part
        out_ref[n // tiles, :, wide] = total
        return carry

    lax.fori_loop(0, steps, body, 0)


def near_product(place, blocks, weights):
    half = len(blocks)
    heights = tuple(b.shape[0] for b in blocks[0])
    rows, depth = sum(heights), blocks[0][0].shape[1]
    gates, _, width = weights.shape
    span = tile_of(width, 512)
    tiles = width // span
    return pl.pallas_call(
        functools.partial(near_kernel, half, tiles, heights),
        out_shape=jax.ShapeDtypeStruct((gates, rows, width), F32),
        in_specs=[pl.BlockSpec(memory_space=pltpu.SMEM)]
        + [pl.BlockSpec(memory_space=pl.ANY)] * (half * len(heights))
        + [pl.BlockSpec(memory_space=pltpu.HBM)],
        out_specs=pl.BlockSpec(memory_space=pltpu.VMEM),
        scratch_shapes=[
            pltpu.VMEM((rows, half * depth), BF16),
            pltpu.VMEM((gates * tiles, half * depth, span), BF16),
            pltpu.SemaphoreType.DMA((half, len(heights))),
            pltpu.SemaphoreType.DMA((gates * tiles,)),
        ],
        compiler_params=params(28),
        cost_estimate=cost(
            2 * gates * rows * half * depth * width,
            gates * width * (half * depth * 2 + rows * 4) + half * rows * depth * 2,
        ),
    )(place, *[piece for block in blocks for piece in block], weights)


def row_order(transposed):
    shape = (BLOCK, BLOCK)
    row = lax.broadcasted_iota(jnp.int32, shape, 1 if transposed else 0)
    token = lax.broadcasted_iota(jnp.int32, shape, 0 if transposed else 1)
    chosen = lax.rem(row, SEGS) * (BLOCK // SEGS) + row // SEGS == token
    return jnp.where(chosen, 1.0, 0.0).astype(BF16)


def split_kernel(first, sizes, joined, src, *refs):
    count = len(sizes)
    outs = refs[:count]
    buf, sem = refs[-2:]
    blocks = sum(sizes) // BLOCK
    copies = []
    for k in range(blocks):
        lines = pl.ds(first + k * BLOCK, BLOCK)
        copies.append(pltpu.make_async_copy(src.at[lines, :], buf.at[k], sem.at[k]))
    for copy in copies:
        copy.start()
    order = row_order(False)
    k = 0
    for c in range(count):
        for r in range(sizes[c] // BLOCK):
            copies[k].wait()
            moved = jnp.dot(order, buf[k], preferred_element_type=F32).astype(BF16)
            outs[c][r * BLOCK : (r + 1) * BLOCK, :] = moved
            if joined:
                refs[count][k * BLOCK : (k + 1) * BLOCK, :] = moved
            k += 1


def split_rows(array, first, sizes, joined):
    vmem = pl.BlockSpec(memory_space=pltpu.VMEM)
    rows, width = sum(sizes), array.shape[1]
    shapes = list(sizes) + ([rows] if joined else [])
    return pl.pallas_call(
        functools.partial(split_kernel, first, tuple(sizes), joined),
        out_shape=[jax.ShapeDtypeStruct((r, width), array.dtype) for r in shapes],
        in_specs=[pl.BlockSpec(memory_space=pltpu.HBM)],
        out_specs=[vmem] * len(shapes),
        scratch_shapes=[
            pltpu.VMEM((rows // BLOCK, BLOCK, width), BF16),
            pltpu.SemaphoreType.DMA((rows // BLOCK,)),
        ],
        compiler_params=params(60),
        cost_estimate=cost(2 * rows * BLOCK * width, 4 * rows * width),
    )(array)


def compose_rows(maps, count, a, b):
    for k in range(count):
        slope = maps[0, k : k + 1, :]
        shift = maps[1, k : k + 1, :]
        b = slope * b + shift
        a = slope * a
    return a, b


def first_slopes(pre, cand, gain):
    update = jax.nn.sigmoid(pre)
    keep = 1.0 - update
    scaled = update * gain
    squashed = jnp.tanh(cand)
    slope = keep + (scaled - scaled * squashed * squashed)
    return update, keep, scaled, slope, update * squashed


def lead_row(place, start, shape):
    lead = lax.broadcasted_iota(jnp.int32, shape, 0) == 0
    return jnp.where(lead & (place[1] == 0), start, 0.0)


def around(update, keep, scaled, cand, gain, prev):
    squashed = jnp.tanh(cand + gain * prev)
    bend = scaled - scaled * squashed * squashed
    return keep + bend, update * squashed - bend * prev


def gate_kernel(half, first_row, rows, before, last, place, *refs):
    blocks = refs[:half]
    part_ref, w_ref, bias_ref, gain_ref, start_ref = refs[half : half + 5]
    earlier = refs[half + 5 : half + 5 + before]
    rest = refs[half + 5 + before :]
    if last:
        gates_ref, maps_ref, total_ref = rest[:3]
    else:
        gates_ref, maps_ref = rest[:2]
    wbuf, acc, wsem = rest[-3:]
    depth = blocks[0].shape[1]
    width = gain_ref.shape[1]
    seg = BLOCK // SEGS
    count = rows // BLOCK
    lines_of = wbuf.shape[3]
    parts = depth // lines_of
    slot = lax.rem(place[0], half)
    base = ((place[0] // half) ^ 1) * (half * depth)

    def w_copy(g, d, q):
        top = base + (slot ^ d) * depth + q * lines_of
        lines = pl.ds(pl.multiple_of(top, lines_of), lines_of)
        return pltpu.make_async_copy(w_ref.at[g, lines, :], wbuf.at[g, d, q], wsem.at[g, d, q])

    every = [(d, q) for d in range(half) for q in range(parts)]
    for g in range(2):
        for d, q in every:
            w_copy(g, d, q).start()
    for g in range(2):
        for d, q in every:
            w_copy(g, d, q).wait()
            deep = slice(q * lines_of, (q + 1) * lines_of)
            part = jnp.dot(blocks[d][:, deep], wbuf[g, d, q], preferred_element_type=F32)
            if (d, q) == (0, 0):
                acc[g] = part
            else:
                acc[g] += part

    span = tile_of(width, 512)

    def columns(n, carry_out):
        wide = pl.ds(pl.multiple_of(n * span, span), span)
        gain = jnp.broadcast_to(gain_ref[:, wide], (SEGS, span))
        bias = [jnp.broadcast_to(bias_ref[g : g + 1, wide], (2 * SEGS, span)) for g in range(2)]

        def pair(jj, carry, first):
            out = []
            for c in range(count):
                a, b = carry[c]
                lines = pl.ds(pl.multiple_of(c * BLOCK + jj * 2 * SEGS, 2 * SEGS), 2 * SEGS)
                deep = pl.ds(
                    pl.multiple_of(first_row + c * BLOCK + jj * 2 * SEGS, 2 * SEGS), 2 * SEGS
                )
                held = []
                for g in range(2):
                    total = acc[g, lines, wide] + part_ref[g, deep, wide] + bias[g]
                    rounded = total.astype(BF16)
                    gates_ref[g, lines, wide] = rounded
                    held.append(rounded.astype(F32))
                for k in range(2):
                    pre = held[0][k * SEGS : (k + 1) * SEGS]
                    cand = held[1][k * SEGS : (k + 1) * SEGS]
                    update, keep, scaled, slope, offset = first_slopes(pre, cand, gain)
                    if first and k == 0 and c == 0:
                        prev = lead_row(place, start_ref[:, wide], (SEGS, span))
                        slope, offset = around(update, keep, scaled, cand, gain, prev)
                    b = slope * b + offset
                    a = slope * a
                out.append((a, b))
            return tuple(out)

        carry = ((jnp.ones((SEGS, span), F32), jnp.zeros((SEGS, span), F32)),) * count
        begin = 0
        if first_row == 0:
            carry = pair(0, carry, True)
            begin = 1
        carry = lax.fori_loop(begin, seg // 2, lambda jj, c: pair(jj, c, False), carry)
        for c in range(count):
            maps_ref[0, c * SEGS : (c + 1) * SEGS, wide] = carry[c][0]
            maps_ref[1, c * SEGS : (c + 1) * SEGS, wide] = carry[c][1]
        return carry_out

    lax.fori_loop(0, width // span, columns, 0)
    if last:
        ta, tb = jnp.ones((1, width), F32), jnp.zeros((1, width), F32)
        for maps in list(earlier) + [maps_ref]:
            ta, tb = compose_rows(maps, maps.shape[1], ta, tb)
        for i in range(total_ref.shape[0]):
            total_ref[i, 0:1, :] = ta
            total_ref[i, 1:2, :] = tb


def gate_chunk(place, blocks, partial, weights, biases, gain, start, earlier, first_row, last, peers):
    half = len(blocks)
    rows, depth = blocks[0].shape
    gates, _, width = weights.shape
    lines_of = tile_of(depth, 512)
    vmem = pl.BlockSpec(memory_space=pltpu.VMEM)
    out_shape = [
        jax.ShapeDtypeStruct((2, rows, width), BF16),
        jax.ShapeDtypeStruct((2, rows // BLOCK * SEGS, width), F32),
    ]
    if last:
        out_shape.append(jax.ShapeDtypeStruct((peers, 2, width), F32))
    return pl.pallas_call(
        functools.partial(gate_kernel, half, first_row, rows, len(earlier), last),
        out_shape=out_shape,
        in_specs=[pl.BlockSpec(memory_space=pltpu.SMEM)]
        + [vmem] * (half + 1)
        + [pl.BlockSpec(memory_space=pltpu.HBM)]
        + [vmem] * (3 + len(earlier)),
        out_specs=[vmem] * len(out_shape),
        scratch_shapes=[
            pltpu.VMEM((gates, half, depth // lines_of, lines_of, width), BF16),
            pltpu.VMEM((gates, rows, width), F32),
            pltpu.SemaphoreType.DMA((gates, half, depth // lines_of)),
        ],
        compiler_params=params(32),
        cost_estimate=cost(
            2 * gates * rows * half * depth * width,
            gates * width * (half * depth * 2 + rows * 6) + half * rows * depth * 2,
            4 * rows * width,
        ),
    )(place, *blocks, partial, weights, biases, gain, start, *earlier)


def entering_state(place, peer_maps, start, peers):
    state = start
    for k in range(peers):
        moved = peer_maps[k, 0:1, :] * state + peer_maps[k, 1:2, :]
        state = jnp.where(place[1] > k, moved, state)
    return state


def enter_segments(maps_list, state, enter):
    row = 0
    for maps in maps_list:
        for k in range(maps.shape[1]):
            enter[row : row + 1, :] = state
            state = maps[0, k : k + 1, :] * state + maps[1, k : k + 1, :]
            row += 1


def bend_kernel(chunks, peers, place, *refs):
    gates = refs[:chunks]
    maps = refs[chunks : 2 * chunks]
    peer_ref, gain_ref, start_ref, run_ref, maps_ref, total_ref, enter = refs[2 * chunks :]
    span = gates[0].shape[2]
    width = gain_ref.shape[1]
    where = [(c, r * BLOCK) for c in range(chunks) for r in range(gates[c].shape[1] // BLOCK)]
    n = pl.program_id(0)

    @pl.when(n == 0)
    def _():
        enter_segments(maps, entering_state(place, peer_ref, start_ref[...], peers), enter)

    wide = pl.ds(pl.multiple_of(n * span, span), span)
    gain = jnp.broadcast_to(gain_ref[:, wide], (SEGS, span))

    def advance(block, jj, held, first):
        state, a, b = held
        c, top = where[block]
        lines = pl.ds(pl.multiple_of(top + jj * 2 * SEGS, 2 * SEGS), 2 * SEGS)
        pre2 = gates[c][0, lines, :].astype(F32)
        cand2 = gates[c][1, lines, :].astype(F32)
        for k in range(2):
            pre = pre2[k * SEGS : (k + 1) * SEGS]
            cand = cand2[k * SEGS : (k + 1) * SEGS]
            update, keep, scaled, slope, offset = first_slopes(pre, cand, gain)
            if first and k == 0 and block == 0:
                prev = lead_row(place, start_ref[:, wide], (SEGS, span))
                slope, offset = around(update, keep, scaled, cand, gain, prev)
            slope2, offset2 = around(update, keep, scaled, cand, gain, state)
            state = slope * state + offset
            b = slope2 * b + offset2
            a = slope2 * a
            row = pl.ds(pl.multiple_of(block * BLOCK + (2 * jj + k) * SEGS, SEGS), SEGS)
            run_ref[0, row, :] = a
            run_ref[1, row, :] = b
        return state, a, b

    def pair(jj, carry, first):
        return tuple(advance(m, jj, carry[m], first) for m in range(len(where)))

    one, zero = jnp.ones((SEGS, span), F32), jnp.zeros((SEGS, span), F32)
    carry = tuple((enter[m * SEGS : (m + 1) * SEGS, wide], one, zero) for m in range(len(where)))
    carry = pair(0, carry, True)
    carry = lax.fori_loop(1, BLOCK // SEGS // 2, lambda jj, c: pair(jj, c, False), carry)
    for m in range(len(where)):
        maps_ref[0, m * SEGS : (m + 1) * SEGS, wide] = carry[m][1]
        maps_ref[1, m * SEGS : (m + 1) * SEGS, wide] = carry[m][2]

    @pl.when(n == pl.num_programs(0) - 1)
    def _():
        ta, tb = jnp.ones((1, width), F32), jnp.zeros((1, width), F32)
        ta, tb = compose_rows(maps_ref, maps_ref.shape[1], ta, tb)
        for i in range(peers):
            total_ref[i, 0:1, :] = ta
            total_ref[i, 1:2, :] = tb


def bend_all(place, gates, maps, peer_maps, gain, start):
    chunks = len(gates)
    peers = peer_maps.shape[0]
    width = gates[0].shape[2]
    total_rows = sum(g.shape[1] for g in gates)
    segs = total_rows // BLOCK * SEGS
    tn = tile_of(width, 256)
    row_spec = pl.BlockSpec((1, width), lambda n, p: (0, 0))
    total_spec = pl.BlockSpec((peers, 2, width), lambda n, p: (0, 0, 0))
    return pl.pallas_call(
        functools.partial(bend_kernel, chunks, peers),
        out_shape=[
            jax.ShapeDtypeStruct((2, total_rows, width), F32),
            jax.ShapeDtypeStruct((2, segs, width), F32),
            jax.ShapeDtypeStruct((peers, 2, width), F32),
        ],
        grid_spec=pltpu.PrefetchScalarGridSpec(
            num_scalar_prefetch=1,
            grid=(width // tn,),
            in_specs=[pl.BlockSpec((2, g.shape[1], tn), lambda n, p: (0, 0, n)) for g in gates]
            + [pl.BlockSpec((2, m.shape[1], width), lambda n, p: (0, 0, 0)) for m in maps]
            + [total_spec, row_spec, row_spec],
            out_specs=[
                pl.BlockSpec((2, total_rows, tn), lambda n, p: (0, 0, n)),
                pl.BlockSpec((2, segs, width), lambda n, p: (0, 0, 0)),
                total_spec,
            ],
            scratch_shapes=[pltpu.VMEM((segs, width), F32)],
        ),
        compiler_params=params(16),
        cost_estimate=cost(
            40 * total_rows * width, 12 * total_rows * width, 5 * total_rows * width
        ),
        name="bend",
    )(place, *gates, *maps, peer_maps, gain, start)


def state_kernel(first_row, peers, place, run_ref, maps_ref, peer_ref, start_ref, out_ref, enter):
    rows = out_ref.shape[0]
    begin = first_row // BLOCK * SEGS
    state = entering_state(place, peer_ref, start_ref[...], peers)
    for k in range(begin + rows // BLOCK * SEGS):
        if k >= begin:
            enter[k - begin : k - begin + 1, :] = state
        state = maps_ref[0, k : k + 1, :] * state + maps_ref[1, k : k + 1, :]
    for c in range(rows // BLOCK):
        once = enter[c * SEGS : (c + 1) * SEGS, :]
        entered = jnp.concatenate([once, once], axis=0)

        def step(jj, carry):
            at = pl.multiple_of(c * BLOCK + jj * 2 * SEGS, 2 * SEGS)
            lines = pl.ds(at, 2 * SEGS)
            deep = pl.ds(pl.multiple_of(first_row + at, 2 * SEGS), 2 * SEGS)
            out_ref[lines, :] = (run_ref[0, deep, :] * entered + run_ref[1, deep, :]).astype(BF16)
            return carry

        lax.fori_loop(0, BLOCK // SEGS // 2, step, 0)


def state_chunk(place, run, maps, peer_maps, start, first_row, rows):
    width = run.shape[2]
    peers = peer_maps.shape[0]
    vmem = pl.BlockSpec(memory_space=pltpu.VMEM)
    return pl.pallas_call(
        functools.partial(state_kernel, first_row, peers),
        out_shape=jax.ShapeDtypeStruct((rows, width), BF16),
        in_specs=[pl.BlockSpec(memory_space=pltpu.SMEM)] + [vmem] * 4,
        out_specs=vmem,
        scratch_shapes=[pltpu.VMEM((rows // BLOCK * SEGS, width), F32)],
        compiler_params=params(16),
        cost_estimate=cost(2 * rows * width, 10 * rows * width),
    )(place, run, maps, peer_maps, start)


def mix_kernel(groups, group, pieces, peers, slots, final, before, place, *refs):
    count = groups * group
    blocks = refs[:count]
    weights = refs[count : count + len(slots) * 2 * pieces]
    out_ref, lhs, wbuf, acc, lsem, wsem = refs[-6:]
    prev_refs = refs[count + len(weights) : count + len(weights) + before]
    depth = blocks[0].shape[1]
    heights = [blocks[c * group].shape[0] for c in range(groups)]
    lines_of = weights[0].shape[0]
    outer = peers // 2
    here = len(slots) * 2

    def w_copy(n, p):
        w_ref = weights[n * pieces + p]
        dst = wbuf.at[n, p * lines_of : (p + 1) * lines_of, :]
        return pltpu.make_async_copy(w_ref, dst, wsem.at[n, p])

    def l_copy(c, d):
        deep = pl.ds(pl.multiple_of((place[0] ^ d) * depth, depth), depth)
        top = sum(heights[:c])
        dst = lhs.at[top : top + heights[c], deep]
        return pltpu.make_async_copy(blocks[c * group + d], dst, lsem.at[c, d])

    for n in range(here):
        for p in range(pieces):
            w_copy(n, p).start()
    for c in range(groups):
        for d in range(group):
            l_copy(c, d).start()
    for c in range(groups):
        for d in range(group):
            l_copy(c, d).wait()
    top = 0
    for prev in prev_refs:
        acc[top : top + prev.shape[0], :] = prev[...]
        top += prev.shape[0]
    span = lines_of * pieces
    for n in range(here):
        source = lax.rem(place[1] // 2 + outer - slots[n // 2], outer)
        owner = source * 2 + (lax.rem(place[1], 2) ^ (n % 2))
        deep = pl.ds(pl.multiple_of(owner * span, span), span)
        for p in range(pieces):
            w_copy(n, p).wait()
        part = jnp.dot(lhs[:, deep], wbuf[n], preferred_element_type=F32)
        if n > 0 or before:
            part = acc[...] + part
        if n < here - 1:
            acc[...] = part
        elif not final:
            out_ref[...] = part
        else:
            acc[...] = part
            order = row_order(True)
            for m in range(acc.shape[0] // BLOCK):
                lines = slice(m * BLOCK, (m + 1) * BLOCK)
                rounded = acc[lines, :].astype(BF16)
                moved = jnp.dot(order, rounded, preferred_element_type=F32)
                out_ref[lines, :] = moved.astype(BF16)


def mix_rows(place, blocks, weights, slots, prev, final, whole, first, total_rows, pieces):
    groups, group = len(blocks), len(blocks[0])
    depth = blocks[0][0].shape[1]
    lines_of, width = weights[0].shape
    peers = len(weights) // pieces
    rows = sum(g[0].shape[0] for g in blocks)
    used = [weights[(s * 2 + i) * pieces + p] for s in slots for i in range(2) for p in range(pieces)]
    args = [place] + [b for g in blocks for b in g] + used
    in_specs = [pl.BlockSpec(memory_space=pl.ANY)] * (groups * group)
    in_specs += [pl.BlockSpec(memory_space=pltpu.HBM)] * len(used)
    args += prev
    in_specs += [pl.BlockSpec((q.shape[0], width), lambda n, p: (0, 0)) for q in prev]
    aliases = {}
    if whole is not None:
        aliases = {len(args): 0}
        args.append(whole)
        in_specs.append(pl.BlockSpec(memory_space=pl.ANY))
    deep = len(slots) * 2 * pieces * lines_of
    if final:
        out_shape = jax.ShapeDtypeStruct((total_rows, width), BF16)
        out_spec = pl.BlockSpec((rows, width), lambda n, p: (first // rows, 0))
    else:
        out_shape = jax.ShapeDtypeStruct((rows, width), F32)
        out_spec = pl.BlockSpec((rows, width), lambda n, p: (0, 0))
    return pl.pallas_call(
        functools.partial(
            mix_kernel, groups, group, pieces, peers, tuple(slots), final, len(prev)
        ),
        out_shape=out_shape,
        grid_spec=pltpu.PrefetchScalarGridSpec(
            num_scalar_prefetch=1,
            grid=(1,),
            in_specs=in_specs,
            out_specs=out_spec,
            scratch_shapes=[
                pltpu.VMEM((rows, group * depth), BF16),
                pltpu.VMEM((len(slots) * 2, lines_of * pieces, width), BF16),
                pltpu.VMEM((rows, width), F32),
                pltpu.SemaphoreType.DMA((groups, group)),
                pltpu.SemaphoreType.DMA((len(slots) * 2, pieces)),
            ],
        ),
        input_output_aliases=aliases,
        compiler_params=params(40 if peers <= 8 else 62),
        cost_estimate=cost(2 * rows * deep * width, 2 * deep * (width + rows) + 4 * rows * width),
    )(*args)


EARLY = 5
SHARES = (2, 1, 1)


def pieces_of(lines_of):
    return 2 if lines_of % (4 * LANES) == 0 else 1


class Ring:
    def __init__(self, w_output):
        self.peers = lax.axis_size("ctx")
        self.outer = self.peers // 2
        self.pieces = pieces_of(w_output.shape[0])
        lines_of = w_output.shape[0] // self.pieces
        self.held = {}
        for p in range(self.pieces):
            self.held[0, 0, p] = w_output[p * lines_of : (p + 1) * lines_of]

    def ring_step(self, n, gate=None):
        s, p = n // self.pieces + 1, n % self.pieces
        block = self.held[s - 1, 0, p]
        if gate is not None:
            block, _ = lax.optimization_barrier((block, gate))
        route = [(i, (i + 2) % self.peers) for i in range(self.peers)]
        self.held[s, 0, p] = lax.ppermute(block, "ctx", route)

    def swap_step(self, n, gate=None):
        s, p = n // self.pieces, n % self.pieces
        block = self.held[s, 0, p]
        if gate is not None:
            block, _ = lax.optimization_barrier((block, gate))
        self.held[s, 1, p] = swap(block, "ctx", 1)

    def run(self, gate):
        rings, swaps = (self.outer - 1) * self.pieces, self.outer * self.pieces
        for n in range(max(rings, swaps)):
            g = gate if n >= EARLY else None
            if n < rings:
                self.ring_step(n, g)
            if n < swaps:
                self.swap_step(n, g)

    def blocks(self):
        steps = [(s, i) for s in range(self.outer) for i in range(2)]
        return [self.held[s, i, p] for s, i in steps for p in range(self.pieces)]


def layer(tokens, w_input, w_output, bias_update, bias_cand, recur_gain, start_state):
    peers = lax.axis_size("ctx")
    group = lax.axis_size("ch")
    half = group // 2
    total_rows = tokens.shape[0]
    chunks = len(SHARES)
    sizes = [total_rows * share // sum(SHARES) for share in SHARES]
    firsts = [sum(sizes[:c]) for c in range(chunks)]
    place = jnp.stack([lax.axis_index("ch"), lax.axis_index("ctx")]).astype(jnp.int32)
    biases = jnp.stack([bias_update, bias_cand], axis=0)
    gain = recur_gain[None, :]
    start = start_state[None, :]

    (head,) = split_rows(tokens, 0, sizes[:1], False)
    *others, tail = split_rows(tokens, sizes[0], sizes[1:], True)
    far = []
    for piece in [head, *others]:
        far.append([swap(piece, "ch", half)])
    near = [[head, tail]]
    for d in range(1, half):
        near.append([swap(head, "ch", d)])
        near[d].append(swap(tail, "ch", d))
    for c in range(chunks):
        for d in range(1, half):
            far[c].append(swap(far[c][0], "ch", d))

    partial = near_product(place, near, w_input)
    gates, maps = [], []
    for c in range(chunks):
        last = c == chunks - 1
        out = gate_chunk(
            place,
            far[c],
            partial,
            w_input,
            biases,
            gain,
            start,
            maps if last else [],
            firsts[c],
            last,
            peers,
        )
        gates.append(out[0])
        maps.append(out[1])
    peer_maps = lax.all_to_all(out[2], "ctx", 0, 0, tiled=True)
    run, run_maps, totals = bend_all(place, gates, maps, peer_maps, gain, start)
    peer_maps = lax.all_to_all(totals, "ctx", 0, 0, tiled=True)
    ring = Ring(w_output)
    ring.run(peer_maps)

    blocks = []
    for c in range(chunks):
        own = state_chunk(place, run, run_maps, peer_maps, start, firsts[c], sizes[c])
        across = swap(own, "ch", half)
        blocks.append([own, across])
    for c in range(chunks):
        own, across = blocks[c]
        lows, highs = [own], [across]
        for d in range(1, half):
            lows.append(swap(own, "ch", d))
            highs.append(swap(across, "ch", d))
        blocks[c] = lows + highs
    weights = ring.blocks()
    late = max(1, ring.outer // 4)
    slots = list(range(ring.outer))

    def mix(part, used, prev, final, whole):
        return mix_rows(
            place,
            blocks[part],
            weights,
            used,
            prev,
            final,
            whole,
            firsts[part][0],
            total_rows,
            ring.pieces,
        )

    early, late_slots = slots[:-late], slots[-late:]
    partials = [mix(slice(c, c + 1), early, [], False, None) for c in range(chunks - 1)]
    mixed = mix(slice(0, chunks - 1), late_slots, partials, True, None)
    mixed = mix(slice(chunks - 1, chunks), slots, [], True, mixed)
    return mixed


def solution(mesh):
    return jax.shard_map(
        layer,
        mesh=mesh,
        in_specs=(
            P("ctx", "ch"),
            P(None, None, "ch"),
            P("ctx", "ch"),
            P("ch"),
            P("ch"),
            P("ch"),
            P("ch"),
        ),
        out_specs=P("ctx", "ch"),
        check_vma=False,
    )
```

```python
import functools
import math

import jax
import jax.numpy as jnp
from jax import lax
from jax.experimental import pallas as pl
from jax.experimental.pallas import tpu as pltpu
from jax.sharding import PartitionSpec as P


SEGS = 8
LANES = 128
BLOCK = 256
F32 = jnp.float32
BF16 = jnp.bfloat16
MIB = 1024 * 1024


def swap(block, axis, bits):
    return lax.ppermute(block, axis, [(i, i ^ bits) for i in range(lax.axis_size(axis))])


def tile_of(width, most):
    return math.gcd(width, most)


def params(mib):
    return pltpu.CompilerParams(vmem_limit_bytes=mib * MIB)


def cost(flops, nbytes, trans=0):
    return pl.CostEstimate(flops=int(flops), bytes_accessed=int(nbytes), transcendentals=int(trans))


def near_kernel(half, tiles, heights, place, *refs):
    count = len(heights)
    blocks = refs[: half * count]
    w_ref, out_ref, lhs, wbuf, lsem, wsem = refs[half * count :]
    depth = blocks[0].shape[1]
    span = wbuf.shape[2]
    slot = lax.rem(place[0], half)
    base = (place[0] // half) * (half * depth)

    def w_copy(n):
        lines = pl.ds(pl.multiple_of(base, half * depth), half * depth)
        wide = pl.ds(pl.multiple_of(lax.rem(n, tiles) * span, span), span)
        return pltpu.make_async_copy(w_ref.at[n // tiles, lines, wide], wbuf.at[n], wsem.at[n])

    def l_copy(d, k):
        deep = pl.ds(pl.multiple_of((slot ^ d) * depth, depth), depth)
        top = sum(heights[:k])
        dst = lhs.at[top : top + heights[k], deep]
        return pltpu.make_async_copy(blocks[d * count + k], dst, lsem.at[d, k])

    steps = wbuf.shape[0]
    for n in range(steps):
        w_copy(n).start()
    for d in range(half):
        for k in range(count):
            l_copy(d, k).start()
    for d in range(half):
        for k in range(count):
            l_copy(d, k).wait()

    def body(n, carry):
        w_copy(n).wait()
        wide = pl.ds(pl.multiple_of(lax.rem(n, tiles) * span, span), span)
        total = None
        for d in range(half):
            deep = slice(d * depth, (d + 1) * depth)
            part = jnp.dot(lhs[:, deep], wbuf[n, deep, :], preferred_element_type=F32)
            total = part if total is None else total + part
        out_ref[n // tiles, :, wide] = total
        return carry

    lax.fori_loop(0, steps, body, 0)


def near_product(place, blocks, weights):
    half = len(blocks)
    heights = tuple(b.shape[0] for b in blocks[0])
    rows, depth = sum(heights), blocks[0][0].shape[1]
    gates, _, width = weights.shape
    span = tile_of(width, 512)
    tiles = width // span
    return pl.pallas_call(
        functools.partial(near_kernel, half, tiles, heights),
        out_shape=jax.ShapeDtypeStruct((gates, rows, width), F32),
        in_specs=[pl.BlockSpec(memory_space=pltpu.SMEM)]
        + [pl.BlockSpec(memory_space=pl.ANY)] * (half * len(heights))
        + [pl.BlockSpec(memory_space=pltpu.HBM)],
        out_specs=pl.BlockSpec(memory_space=pltpu.VMEM),
        scratch_shapes=[
            pltpu.VMEM((rows, half * depth), BF16),
            pltpu.VMEM((gates * tiles, half * depth, span), BF16),
            pltpu.SemaphoreType.DMA((half, len(heights))),
            pltpu.SemaphoreType.DMA((gates * tiles,)),
        ],
        compiler_params=params(28),
        cost_estimate=cost(
            2 * gates * rows * half * depth * width,
            gates * width * (half * depth * 2 + rows * 4) + half * rows * depth * 2,
        ),
    )(place, *[piece for block in blocks for piece in block], weights)


def row_order(transposed):
    shape = (BLOCK, BLOCK)
    row = lax.broadcasted_iota(jnp.int32, shape, 1 if transposed else 0)
    token = lax.broadcasted_iota(jnp.int32, shape, 0 if transposed else 1)
    chosen = lax.rem(row, SEGS) * (BLOCK // SEGS) + row // SEGS == token
    return jnp.where(chosen, 1.0, 0.0).astype(BF16)


def split_kernel(first, sizes, joined, src, *refs):
    count = len(sizes)
    outs = refs[:count]
    buf, sem = refs[-2:]
    blocks = sum(sizes) // BLOCK
    copies = []
    for k in range(blocks):
        lines = pl.ds(first + k * BLOCK, BLOCK)
        copies.append(pltpu.make_async_copy(src.at[lines, :], buf.at[k], sem.at[k]))
    for copy in copies:
        copy.start()
    order = row_order(False)
    k = 0
    for c in range(count):
        for r in range(sizes[c] // BLOCK):
            copies[k].wait()
            moved = jnp.dot(order, buf[k], preferred_element_type=F32).astype(BF16)
            outs[c][r * BLOCK : (r + 1) * BLOCK, :] = moved
            if joined:
                refs[count][k * BLOCK : (k + 1) * BLOCK, :] = moved
            k += 1


def split_rows(array, first, sizes, joined):
    vmem = pl.BlockSpec(memory_space=pltpu.VMEM)
    rows, width = sum(sizes), array.shape[1]
    shapes = list(sizes) + ([rows] if joined else [])
    return pl.pallas_call(
        functools.partial(split_kernel, first, tuple(sizes), joined),
        out_shape=[jax.ShapeDtypeStruct((r, width), array.dtype) for r in shapes],
        in_specs=[pl.BlockSpec(memory_space=pltpu.HBM)],
        out_specs=[vmem] * len(shapes),
        scratch_shapes=[
            pltpu.VMEM((rows // BLOCK, BLOCK, width), BF16),
            pltpu.SemaphoreType.DMA((rows // BLOCK,)),
        ],
        compiler_params=params(60),
        cost_estimate=cost(2 * rows * BLOCK * width, 4 * rows * width),
    )(array)


def compose_rows(maps, count, a, b):
    for k in range(count):
        slope = maps[0, k : k + 1, :]
        shift = maps[1, k : k + 1, :]
        b = slope * b + shift
        a = slope * a
    return a, b


def first_slopes(pre, cand, gain):
    update = jax.nn.sigmoid(pre)
    keep = 1.0 - update
    scaled = update * gain
    squashed = jnp.tanh(cand)
    slope = keep + (scaled - scaled * squashed * squashed)
    return update, keep, scaled, slope, update * squashed


def lead_row(place, start, shape):
    lead = lax.broadcasted_iota(jnp.int32, shape, 0) == 0
    return jnp.where(lead & (place[1] == 0), start, 0.0)


def around(update, keep, scaled, cand, gain, prev):
    squashed = jnp.tanh(cand + gain * prev)
    bend = scaled - scaled * squashed * squashed
    return keep + bend, update * squashed - bend * prev


def gate_kernel(half, first_row, rows, before, last, place, *refs):
    blocks = refs[:half]
    part_ref, w_ref, bias_ref, gain_ref, start_ref = refs[half : half + 5]
    earlier = refs[half + 5 : half + 5 + before]
    rest = refs[half + 5 + before :]
    if last:
        gates_ref, maps_ref, total_ref = rest[:3]
    else:
        gates_ref, maps_ref = rest[:2]
    wbuf, acc, wsem = rest[-3:]
    depth = blocks[0].shape[1]
    width = gain_ref.shape[1]
    seg = BLOCK // SEGS
    count = rows // BLOCK
    lines_of = wbuf.shape[3]
    parts = depth // lines_of
    slot = lax.rem(place[0], half)
    base = ((place[0] // half) ^ 1) * (half * depth)

    def w_copy(g, d, q):
        top = base + (slot ^ d) * depth + q * lines_of
        lines = pl.ds(pl.multiple_of(top, lines_of), lines_of)
        return pltpu.make_async_copy(w_ref.at[g, lines, :], wbuf.at[g, d, q], wsem.at[g, d, q])

    every = [(d, q) for d in range(half) for q in range(parts)]
    for g in range(2):
        for d, q in every:
            w_copy(g, d, q).start()
    for g in range(2):
        for d, q in every:
            w_copy(g, d, q).wait()
            deep = slice(q * lines_of, (q + 1) * lines_of)
            part = jnp.dot(blocks[d][:, deep], wbuf[g, d, q], preferred_element_type=F32)
            if (d, q) == (0, 0):
                acc[g] = part
            else:
                acc[g] += part

    span = tile_of(width, 512)

    def columns(n, carry_out):
        wide = pl.ds(pl.multiple_of(n * span, span), span)
        gain = jnp.broadcast_to(gain_ref[:, wide], (SEGS, span))
        bias = [jnp.broadcast_to(bias_ref[g : g + 1, wide], (2 * SEGS, span)) for g in range(2)]

        def pair(jj, carry, first):
            out = []
            for c in range(count):
                a, b = carry[c]
                lines = pl.ds(pl.multiple_of(c * BLOCK + jj * 2 * SEGS, 2 * SEGS), 2 * SEGS)
                deep = pl.ds(
                    pl.multiple_of(first_row + c * BLOCK + jj * 2 * SEGS, 2 * SEGS), 2 * SEGS
                )
                held = []
                for g in range(2):
                    total = acc[g, lines, wide] + part_ref[g, deep, wide] + bias[g]
                    rounded = total.astype(BF16)
                    gates_ref[g, lines, wide] = rounded
                    held.append(rounded.astype(F32))
                for k in range(2):
                    pre = held[0][k * SEGS : (k + 1) * SEGS]
                    cand = held[1][k * SEGS : (k + 1) * SEGS]
                    update, keep, scaled, slope, offset = first_slopes(pre, cand, gain)
                    if first and k == 0 and c == 0:
                        prev = lead_row(place, start_ref[:, wide], (SEGS, span))
                        slope, offset = around(update, keep, scaled, cand, gain, prev)
                    b = slope * b + offset
                    a = slope * a
                out.append((a, b))
            return tuple(out)

        carry = ((jnp.ones((SEGS, span), F32), jnp.zeros((SEGS, span), F32)),) * count
        begin = 0
        if first_row == 0:
            carry = pair(0, carry, True)
            begin = 1
        carry = lax.fori_loop(begin, seg // 2, lambda jj, c: pair(jj, c, False), carry)
        for c in range(count):
            maps_ref[0, c * SEGS : (c + 1) * SEGS, wide] = carry[c][0]
            maps_ref[1, c * SEGS : (c + 1) * SEGS, wide] = carry[c][1]
        return carry_out

    lax.fori_loop(0, width // span, columns, 0)
    if last:
        ta, tb = jnp.ones((1, width), F32), jnp.zeros((1, width), F32)
        for maps in list(earlier) + [maps_ref]:
            ta, tb = compose_rows(maps, maps.shape[1], ta, tb)
        for i in range(total_ref.shape[0]):
            total_ref[i, 0:1, :] = ta
            total_ref[i, 1:2, :] = tb


def gate_chunk(place, blocks, partial, weights, biases, gain, start, earlier, first_row, last, peers):
    half = len(blocks)
    rows, depth = blocks[0].shape
    gates, _, width = weights.shape
    lines_of = tile_of(depth, 512)
    vmem = pl.BlockSpec(memory_space=pltpu.VMEM)
    out_shape = [
        jax.ShapeDtypeStruct((2, rows, width), BF16),
        jax.ShapeDtypeStruct((2, rows // BLOCK * SEGS, width), F32),
    ]
    if last:
        out_shape.append(jax.ShapeDtypeStruct((peers, 2, width), F32))
    return pl.pallas_call(
        functools.partial(gate_kernel, half, first_row, rows, len(earlier), last),
        out_shape=out_shape,
        in_specs=[pl.BlockSpec(memory_space=pltpu.SMEM)]
        + [vmem] * (half + 1)
        + [pl.BlockSpec(memory_space=pltpu.HBM)]
        + [vmem] * (3 + len(earlier)),
        out_specs=[vmem] * len(out_shape),
        scratch_shapes=[
            pltpu.VMEM((gates, half, depth // lines_of, lines_of, width), BF16),
            pltpu.VMEM((gates, rows, width), F32),
            pltpu.SemaphoreType.DMA((gates, half, depth // lines_of)),
        ],
        compiler_params=params(32),
        cost_estimate=cost(
            2 * gates * rows * half * depth * width,
            gates * width * (half * depth * 2 + rows * 6) + half * rows * depth * 2,
            4 * rows * width,
        ),
    )(place, *blocks, partial, weights, biases, gain, start, *earlier)


def entering_state(place, peer_maps, start, peers):
    state = start
    for k in range(peers):
        moved = peer_maps[k, 0:1, :] * state + peer_maps[k, 1:2, :]
        state = jnp.where(place[1] > k, moved, state)
    return state


def enter_segments(maps_list, state, enter):
    row = 0
    for maps in maps_list:
        for k in range(maps.shape[1]):
            enter[row : row + 1, :] = state
            state = maps[0, k : k + 1, :] * state + maps[1, k : k + 1, :]
            row += 1


def bend_kernel(chunks, peers, place, *refs):
    gates = refs[:chunks]
    maps = refs[chunks : 2 * chunks]
    peer_ref, gain_ref, start_ref, run_ref, maps_ref, total_ref, enter = refs[2 * chunks :]
    span = gates[0].shape[2]
    width = gain_ref.shape[1]
    where = [(c, r * BLOCK) for c in range(chunks) for r in range(gates[c].shape[1] // BLOCK)]
    n = pl.program_id(0)

    @pl.when(n == 0)
    def _():
        enter_segments(maps, entering_state(place, peer_ref, start_ref[...], peers), enter)

    wide = pl.ds(pl.multiple_of(n * span, span), span)
    gain = jnp.broadcast_to(gain_ref[:, wide], (SEGS, span))

    def advance(block, jj, held, first):
        state, a, b = held
        c, top = where[block]
        lines = pl.ds(pl.multiple_of(top + jj * 2 * SEGS, 2 * SEGS), 2 * SEGS)
        pre2 = gates[c][0, lines, :].astype(F32)
        cand2 = gates[c][1, lines, :].astype(F32)
        for k in range(2):
            pre = pre2[k * SEGS : (k + 1) * SEGS]
            cand = cand2[k * SEGS : (k + 1) * SEGS]
            update, keep, scaled, slope, offset = first_slopes(pre, cand, gain)
            if first and k == 0 and block == 0:
                prev = lead_row(place, start_ref[:, wide], (SEGS, span))
                slope, offset = around(update, keep, scaled, cand, gain, prev)
            slope2, offset2 = around(update, keep, scaled, cand, gain, state)
            state = slope * state + offset
            b = slope2 * b + offset2
            a = slope2 * a
            row = pl.ds(pl.multiple_of(block * BLOCK + (2 * jj + k) * SEGS, SEGS), SEGS)
            run_ref[0, row, :] = a
            run_ref[1, row, :] = b
        return state, a, b

    def pair(jj, carry, first):
        return tuple(advance(m, jj, carry[m], first) for m in range(len(where)))

    one, zero = jnp.ones((SEGS, span), F32), jnp.zeros((SEGS, span), F32)
    carry = tuple((enter[m * SEGS : (m + 1) * SEGS, wide], one, zero) for m in range(len(where)))
    carry = pair(0, carry, True)
    carry = lax.fori_loop(1, BLOCK // SEGS // 2, lambda jj, c: pair(jj, c, False), carry)
    for m in range(len(where)):
        maps_ref[0, m * SEGS : (m + 1) * SEGS, wide] = carry[m][1]
        maps_ref[1, m * SEGS : (m + 1) * SEGS, wide] = carry[m][2]

    @pl.when(n == pl.num_programs(0) - 1)
    def _():
        ta, tb = jnp.ones((1, width), F32), jnp.zeros((1, width), F32)
        ta, tb = compose_rows(maps_ref, maps_ref.shape[1], ta, tb)
        for i in range(peers):
            total_ref[i, 0:1, :] = ta
            total_ref[i, 1:2, :] = tb


def bend_all(place, gates, maps, peer_maps, gain, start):
    chunks = len(gates)
    peers = peer_maps.shape[0]
    width = gates[0].shape[2]
    total_rows = sum(g.shape[1] for g in gates)
    segs = total_rows // BLOCK * SEGS
    tn = tile_of(width, 256)
    row_spec = pl.BlockSpec((1, width), lambda n, p: (0, 0))
    total_spec = pl.BlockSpec((peers, 2, width), lambda n, p: (0, 0, 0))
    return pl.pallas_call(
        functools.partial(bend_kernel, chunks, peers),
        out_shape=[
            jax.ShapeDtypeStruct((2, total_rows, width), F32),
            jax.ShapeDtypeStruct((2, segs, width), F32),
            jax.ShapeDtypeStruct((peers, 2, width), F32),
        ],
        grid_spec=pltpu.PrefetchScalarGridSpec(
            num_scalar_prefetch=1,
            grid=(width // tn,),
            in_specs=[pl.BlockSpec((2, g.shape[1], tn), lambda n, p: (0, 0, n)) for g in gates]
            + [pl.BlockSpec((2, m.shape[1], width), lambda n, p: (0, 0, 0)) for m in maps]
            + [total_spec, row_spec, row_spec],
            out_specs=[
                pl.BlockSpec((2, total_rows, tn), lambda n, p: (0, 0, n)),
                pl.BlockSpec((2, segs, width), lambda n, p: (0, 0, 0)),
                total_spec,
            ],
            scratch_shapes=[pltpu.VMEM((segs, width), F32)],
        ),
        compiler_params=params(16),
        cost_estimate=cost(
            40 * total_rows * width, 12 * total_rows * width, 5 * total_rows * width
        ),
        name="bend",
    )(place, *gates, *maps, peer_maps, gain, start)


def state_kernel(first_row, peers, place, run_ref, maps_ref, peer_ref, start_ref, out_ref, enter):
    rows = out_ref.shape[0]
    begin = first_row // BLOCK * SEGS
    state = entering_state(place, peer_ref, start_ref[...], peers)
    for k in range(begin + rows // BLOCK * SEGS):
        if k >= begin:
            enter[k - begin : k - begin + 1, :] = state
        state = maps_ref[0, k : k + 1, :] * state + maps_ref[1, k : k + 1, :]
    for c in range(rows // BLOCK):
        once = enter[c * SEGS : (c + 1) * SEGS, :]
        entered = jnp.concatenate([once, once], axis=0)

        def step(jj, carry):
            at = pl.multiple_of(c * BLOCK + jj * 2 * SEGS, 2 * SEGS)
            lines = pl.ds(at, 2 * SEGS)
            deep = pl.ds(pl.multiple_of(first_row + at, 2 * SEGS), 2 * SEGS)
            out_ref[lines, :] = (run_ref[0, deep, :] * entered + run_ref[1, deep, :]).astype(BF16)
            return carry

        lax.fori_loop(0, BLOCK // SEGS // 2, step, 0)


def state_chunk(place, run, maps, peer_maps, start, first_row, rows):
    width = run.shape[2]
    peers = peer_maps.shape[0]
    vmem = pl.BlockSpec(memory_space=pltpu.VMEM)
    return pl.pallas_call(
        functools.partial(state_kernel, first_row, peers),
        out_shape=jax.ShapeDtypeStruct((rows, width), BF16),
        in_specs=[pl.BlockSpec(memory_space=pltpu.SMEM)] + [vmem] * 4,
        out_specs=vmem,
        scratch_shapes=[pltpu.VMEM((rows // BLOCK * SEGS, width), F32)],
        compiler_params=params(16),
        cost_estimate=cost(2 * rows * width, 10 * rows * width),
    )(place, run, maps, peer_maps, start)


def mix_kernel(groups, group, cuts, peers, slots, final, before, place, *refs):
    count = groups * group
    blocks = refs[:count]
    starts = [sum(len(cut) for cut in cuts[:n]) for n in range(len(cuts) + 1)]
    weights = refs[count : count + starts[-1]]
    out_ref, lhs, wbuf, acc, lsem, wsem = refs[-6:]
    prev_refs = refs[count + len(weights) : count + len(weights) + before]
    depth = blocks[0].shape[1]
    heights = [blocks[c * group].shape[0] for c in range(groups)]
    outer = peers // 2
    here = len(slots) * 2

    def w_copy(n, p):
        w_ref = weights[starts[n] + p]
        top = sum(cuts[n][:p])
        dst = wbuf.at[n, top : top + cuts[n][p], :]
        return pltpu.make_async_copy(w_ref, dst, wsem.at[n, p])

    def l_copy(c, d):
        deep = pl.ds(pl.multiple_of((place[0] ^ d) * depth, depth), depth)
        top = sum(heights[:c])
        dst = lhs.at[top : top + heights[c], deep]
        return pltpu.make_async_copy(blocks[c * group + d], dst, lsem.at[c, d])

    for n in range(here):
        for p in range(len(cuts[n])):
            w_copy(n, p).start()
    for c in range(groups):
        for d in range(group):
            l_copy(c, d).start()
    for c in range(groups):
        for d in range(group):
            l_copy(c, d).wait()
    top = 0
    for prev in prev_refs:
        acc[top : top + prev.shape[0], :] = prev[...]
        top += prev.shape[0]
    span = wbuf.shape[1]
    for n in range(here):
        source = lax.rem(place[1] // 2 + outer - slots[n // 2], outer)
        owner = source * 2 + (lax.rem(place[1], 2) ^ (n % 2))
        deep = pl.ds(pl.multiple_of(owner * span, span), span)
        for p in range(len(cuts[n])):
            w_copy(n, p).wait()
        part = jnp.dot(lhs[:, deep], wbuf[n], preferred_element_type=F32)
        if n > 0 or before:
            part = acc[...] + part
        if n < here - 1:
            acc[...] = part
        elif not final:
            out_ref[...] = part
        else:
            acc[...] = part
            order = row_order(True)
            for m in range(acc.shape[0] // BLOCK):
                lines = slice(m * BLOCK, (m + 1) * BLOCK)
                rounded = acc[lines, :].astype(BF16)
                moved = jnp.dot(order, rounded, preferred_element_type=F32)
                out_ref[lines, :] = moved.astype(BF16)


def mix_rows(place, blocks, weights, slots, prev, final, whole, first, total_rows):
    groups, group = len(blocks), len(blocks[0])
    depth = blocks[0][0].shape[1]
    width = weights[0][0].shape[1]
    peers = len(weights)
    span = sum(piece.shape[0] for piece in weights[0])
    rows = sum(g[0].shape[0] for g in blocks)
    chosen = [weights[s * 2 + i] for s in slots for i in range(2)]
    cuts = tuple(tuple(piece.shape[0] for piece in pieces) for pieces in chosen)
    used = [piece for pieces in chosen for piece in pieces]
    most = max(len(cut) for cut in cuts)
    args = [place] + [b for g in blocks for b in g] + used
    in_specs = [pl.BlockSpec(memory_space=pl.ANY)] * (groups * group)
    in_specs += [pl.BlockSpec(memory_space=pltpu.HBM)] * len(used)
    args += prev
    in_specs += [pl.BlockSpec((q.shape[0], width), lambda n, p: (0, 0)) for q in prev]
    aliases = {}
    if whole is not None:
        aliases = {len(args): 0}
        args.append(whole)
        in_specs.append(pl.BlockSpec(memory_space=pl.ANY))
    deep = len(slots) * 2 * span
    if final:
        out_shape = jax.ShapeDtypeStruct((total_rows, width), BF16)
        out_spec = pl.BlockSpec((rows, width), lambda n, p: (first // rows, 0))
    else:
        out_shape = jax.ShapeDtypeStruct((rows, width), F32)
        out_spec = pl.BlockSpec((rows, width), lambda n, p: (0, 0))
    return pl.pallas_call(
        functools.partial(
            mix_kernel, groups, group, cuts, peers, tuple(slots), final, len(prev)
        ),
        out_shape=out_shape,
        grid_spec=pltpu.PrefetchScalarGridSpec(
            num_scalar_prefetch=1,
            grid=(1,),
            in_specs=in_specs,
            out_specs=out_spec,
            scratch_shapes=[
                pltpu.VMEM((rows, group * depth), BF16),
                pltpu.VMEM((len(slots) * 2, span, width), BF16),
                pltpu.VMEM((rows, width), F32),
                pltpu.SemaphoreType.DMA((groups, group)),
                pltpu.SemaphoreType.DMA((len(slots) * 2, most)),
            ],
        ),
        input_output_aliases=aliases,
        compiler_params=params(40 if peers <= 8 else 62),
        cost_estimate=cost(2 * rows * deep * width, 2 * deep * (width + rows) + 4 * rows * width),
    )(*args)


SHARES = (2, 1, 1)
RINGS_EARLY = 2
SWAPS_EARLY = 1


def cut_of(rows, shares):
    parts = [rows * share // sum(shares) for share in shares]
    return parts if min(parts) >= LANES else [rows]


def ring_cut(step, outer, rows):
    return cut_of(rows, (1, 1) if step == outer - 1 else (1,))


def swap_cut(step, outer, rows):
    if step == SWAPS_EARLY + 1 and step < outer - 1:
        return cut_of(rows, (1, 3))
    return ring_cut(step, outer, rows)


def recut(blocks, parts):
    if [b.shape[0] for b in blocks] == parts:
        return blocks
    (block,) = blocks
    tops = [sum(parts[:p]) for p in range(len(parts))]
    return [block[top : top + part] for top, part in zip(tops, parts)]


def behind(block, gate):
    return block if gate is None else lax.optimization_barrier((block, gate))[0]


def gather_early(w_output):
    peers = lax.axis_size("ctx")
    route = [(i, (i + 2) % peers) for i in range(peers)]
    held = {(0, 0): [w_output]}
    for step in range(1, min(RINGS_EARLY + 1, peers // 2)):
        held[step, 0] = [lax.ppermute(held[step - 1, 0][0], "ctx", route)]
    for step in range(SWAPS_EARLY + 1):
        held[step, 1] = [swap(held[step, 0][0], "ctx", 1)]
    return held


def next_cuts(outer, rows):
    return [ring_cut(RINGS_EARLY + 1, outer, rows), swap_cut(SWAPS_EARLY + 1, outer, rows)]


def gather_late(held, following, middle, late):
    peers = lax.axis_size("ctx")
    outer = peers // 2
    rows = held[0, 0][0].shape[0]
    route = [(i, (i + 2) % peers) for i in range(peers)]
    for step in range(RINGS_EARLY + 1, outer):
        held[step, 0] = []
        if step == RINGS_EARLY + 1:
            source = following[0]
        else:
            source = recut(held[step - 1, 0], ring_cut(step, outer, rows))
        for block in source:
            held[step, 0].append(lax.ppermute(behind(block, late), "ctx", route))
    for step in range(SWAPS_EARLY + 1, outer):
        held[step, 1] = []
        if step == SWAPS_EARLY + 1:
            source = following[1]
        else:
            source = recut(held[step, 0], swap_cut(step, outer, rows))
        for p, block in enumerate(source):
            gate = middle if step == SWAPS_EARLY + 1 and p == 0 else late
            held[step, 1].append(swap(behind(block, gate), "ctx", 1))
    return [held[step, i] for step in range(outer) for i in range(2)]


def layer(tokens, w_input, w_output, bias_update, bias_cand, recur_gain, start_state):
    peers = lax.axis_size("ctx")
    group = lax.axis_size("ch")
    half = group // 2
    total_rows = tokens.shape[0]
    chunks = len(SHARES)
    sizes = [total_rows * share // sum(SHARES) for share in SHARES]
    firsts = [sum(sizes[:c]) for c in range(chunks)]
    place = jnp.stack([lax.axis_index("ch"), lax.axis_index("ctx")]).astype(jnp.int32)
    biases = jnp.stack([bias_update, bias_cand], axis=0)
    gain = recur_gain[None, :]
    start = start_state[None, :]

    (head,) = split_rows(tokens, 0, sizes[:1], False)
    *others, tail = split_rows(tokens, sizes[0], sizes[1:], True)
    far = []
    for piece in [head, *others]:
        far.append([swap(piece, "ch", half)])
    near = [[head, tail]]
    for d in range(1, half):
        near.append([swap(head, "ch", d)])
        near[d].append(swap(tail, "ch", d))
    for c in range(chunks):
        for d in range(1, half):
            far[c].append(swap(far[c][0], "ch", d))

    partial = near_product(place, near, w_input)
    gates, maps = [], []
    for c in range(chunks):
        last = c == chunks - 1
        out = gate_chunk(
            place,
            far[c],
            partial,
            w_input,
            biases,
            gain,
            start,
            maps if last else [],
            firsts[c],
            last,
            peers,
        )
        gates.append(out[0])
        maps.append(out[1])
    held = gather_early(w_output)
    following = [recut(held[RINGS_EARLY, 0], cut) for cut in next_cuts(peers // 2, w_output.shape[0])]
    following, totals = lax.optimization_barrier((following, out[2]))
    first_maps = lax.all_to_all(totals, "ctx", 0, 0, tiled=True)
    run, run_maps, totals = bend_all(place, gates, maps, first_maps, gain, start)
    peer_maps = lax.all_to_all(totals, "ctx", 0, 0, tiled=True)
    weights = gather_late(held, following, first_maps, peer_maps)

    blocks = []
    for c in range(chunks):
        own = state_chunk(place, run, run_maps, peer_maps, start, firsts[c], sizes[c])
        across = swap(own, "ch", half)
        blocks.append([own, across])
    for c in range(chunks):
        own, across = blocks[c]
        lows, highs = [own], [across]
        for d in range(1, half):
            lows.append(swap(own, "ch", d))
            highs.append(swap(across, "ch", d))
        blocks[c] = lows + highs
    outer = peers // 2
    late = max(1, outer // 4)
    slots = list(range(outer))

    def mix(part, used, prev, final, whole):
        return mix_rows(
            place,
            blocks[part],
            weights,
            used,
            prev,
            final,
            whole,
            firsts[part][0],
            total_rows,
        )

    early, late_slots = slots[:-late], slots[-late:]
    partials = [mix(slice(c, c + 1), early, [], False, None) for c in range(chunks - 1)]
    mixed = mix(slice(0, chunks - 1), late_slots, partials, True, None)
    mixed = mix(slice(chunks - 1, chunks), slots, [], True, mixed)
    return mixed


def solution(mesh):
    return jax.shard_map(
        layer,
        mesh=mesh,
        in_specs=(
            P("ctx", "ch"),
            P(None, None, "ch"),
            P("ctx", "ch"),
            P("ch"),
            P("ch"),
            P("ch"),
            P("ch"),
        ),
        out_specs=P("ctx", "ch"),
        check_vma=False,
    )
```

```python
import functools
import math

import jax
import jax.numpy as jnp
from jax import lax
from jax.experimental import pallas as pl
from jax.experimental.pallas import tpu as pltpu
from jax.sharding import PartitionSpec as P


SEGS = 8
LANES = 128
BLOCK = 256
F32 = jnp.float32
BF16 = jnp.bfloat16
MIB = 1024 * 1024


def swap(block, axis, bits):
    return lax.ppermute(block, axis, [(i, i ^ bits) for i in range(lax.axis_size(axis))])


def tile_of(width, most):
    return math.gcd(width, most)


def params(mib):
    return pltpu.CompilerParams(vmem_limit_bytes=mib * MIB)


def cost(flops, nbytes, trans=0):
    return pl.CostEstimate(flops=int(flops), bytes_accessed=int(nbytes), transcendentals=int(trans))


def near_kernel(half, tiles, heights, place, *refs):
    count = len(heights)
    blocks = refs[: half * count]
    w_ref, out_ref, lhs, wbuf, lsem, wsem = refs[half * count :]
    depth = blocks[0].shape[1]
    span = wbuf.shape[2]
    slot = lax.rem(place[0], half)
    base = (place[0] // half) * (half * depth)

    def w_copy(n):
        lines = pl.ds(pl.multiple_of(base, half * depth), half * depth)
        wide = pl.ds(pl.multiple_of(lax.rem(n, tiles) * span, span), span)
        return pltpu.make_async_copy(w_ref.at[n // tiles, lines, wide], wbuf.at[n], wsem.at[n])

    def l_copy(d, k):
        deep = pl.ds(pl.multiple_of((slot ^ d) * depth, depth), depth)
        top = sum(heights[:k])
        dst = lhs.at[top : top + heights[k], deep]
        return pltpu.make_async_copy(blocks[d * count + k], dst, lsem.at[d, k])

    steps = wbuf.shape[0]
    for n in range(steps):
        w_copy(n).start()
    for d in range(half):
        for k in range(count):
            l_copy(d, k).start()
    for d in range(half):
        for k in range(count):
            l_copy(d, k).wait()

    def body(n, carry):
        w_copy(n).wait()
        wide = pl.ds(pl.multiple_of(lax.rem(n, tiles) * span, span), span)
        total = None
        for d in range(half):
            deep = slice(d * depth, (d + 1) * depth)
            part = jnp.dot(lhs[:, deep], wbuf[n, deep, :], preferred_element_type=F32)
            total = part if total is None else total + part
        out_ref[n // tiles, :, wide] = total
        return carry

    lax.fori_loop(0, steps, body, 0)


def near_product(place, blocks, weights):
    half = len(blocks)
    heights = tuple(b.shape[0] for b in blocks[0])
    rows, depth = sum(heights), blocks[0][0].shape[1]
    gates, _, width = weights.shape
    span = tile_of(width, 512)
    tiles = width // span
    return pl.pallas_call(
        functools.partial(near_kernel, half, tiles, heights),
        out_shape=jax.ShapeDtypeStruct((gates, rows, width), F32),
        in_specs=[pl.BlockSpec(memory_space=pltpu.SMEM)]
        + [pl.BlockSpec(memory_space=pl.ANY)] * (half * len(heights))
        + [pl.BlockSpec(memory_space=pltpu.HBM)],
        out_specs=pl.BlockSpec(memory_space=pltpu.VMEM),
        scratch_shapes=[
            pltpu.VMEM((rows, half * depth), BF16),
            pltpu.VMEM((gates * tiles, half * depth, span), BF16),
            pltpu.SemaphoreType.DMA((half, len(heights))),
            pltpu.SemaphoreType.DMA((gates * tiles,)),
        ],
        compiler_params=params(28),
        cost_estimate=cost(
            2 * gates * rows * half * depth * width,
            gates * width * (half * depth * 2 + rows * 4) + half * rows * depth * 2,
        ),
    )(place, *[piece for block in blocks for piece in block], weights)


def row_order(transposed):
    shape = (BLOCK, BLOCK)
    row = lax.broadcasted_iota(jnp.int32, shape, 1 if transposed else 0)
    token = lax.broadcasted_iota(jnp.int32, shape, 0 if transposed else 1)
    chosen = lax.rem(row, SEGS) * (BLOCK // SEGS) + row // SEGS == token
    return jnp.where(chosen, 1.0, 0.0).astype(BF16)


def split_kernel(first, sizes, joined, src, *refs):
    count = len(sizes)
    outs = refs[:count]
    buf, sem = refs[-2:]
    blocks = sum(sizes) // BLOCK
    copies = []
    for k in range(blocks):
        lines = pl.ds(first + k * BLOCK, BLOCK)
        copies.append(pltpu.make_async_copy(src.at[lines, :], buf.at[k], sem.at[k]))
    for copy in copies:
        copy.start()
    order = row_order(False)
    k = 0
    for c in range(count):
        for r in range(sizes[c] // BLOCK):
            copies[k].wait()
            moved = jnp.dot(order, buf[k], preferred_element_type=F32).astype(BF16)
            outs[c][r * BLOCK : (r + 1) * BLOCK, :] = moved
            if joined:
                refs[count][k * BLOCK : (k + 1) * BLOCK, :] = moved
            k += 1


def split_rows(array, first, sizes, joined):
    vmem = pl.BlockSpec(memory_space=pltpu.VMEM)
    rows, width = sum(sizes), array.shape[1]
    shapes = list(sizes) + ([rows] if joined else [])
    return pl.pallas_call(
        functools.partial(split_kernel, first, tuple(sizes), joined),
        out_shape=[jax.ShapeDtypeStruct((r, width), array.dtype) for r in shapes],
        in_specs=[pl.BlockSpec(memory_space=pltpu.HBM)],
        out_specs=[vmem] * len(shapes),
        scratch_shapes=[
            pltpu.VMEM((rows // BLOCK, BLOCK, width), BF16),
            pltpu.SemaphoreType.DMA((rows // BLOCK,)),
        ],
        compiler_params=params(60),
        cost_estimate=cost(2 * rows * BLOCK * width, 4 * rows * width),
    )(array)


def compose_rows(maps, count, a, b):
    for k in range(count):
        slope = maps[0, k : k + 1, :]
        shift = maps[1, k : k + 1, :]
        b = slope * b + shift
        a = slope * a
    return a, b


def first_slopes(pre, cand, gain):
    update = jax.nn.sigmoid(pre)
    keep = 1.0 - update
    scaled = update * gain
    squashed = jnp.tanh(cand)
    slope = keep + (scaled - scaled * squashed * squashed)
    return update, keep, scaled, slope, update * squashed


def lead_row(place, start, shape):
    lead = lax.broadcasted_iota(jnp.int32, shape, 0) == 0
    return jnp.where(lead & (place[1] == 0), start, 0.0)


def around(update, keep, scaled, cand, gain, prev):
    squashed = jnp.tanh(cand + gain * prev)
    bend = scaled - scaled * squashed * squashed
    return keep + bend, update * squashed - bend * prev


def gate_kernel(half, first_row, rows, before, last, place, *refs):
    blocks = refs[:half]
    part_ref, w_ref, bias_ref, gain_ref, start_ref = refs[half : half + 5]
    earlier = refs[half + 5 : half + 5 + before]
    rest = refs[half + 5 + before :]
    if last:
        gates_ref, maps_ref, total_ref = rest[:3]
    else:
        gates_ref, maps_ref = rest[:2]
    wbuf, acc, wsem = rest[-3:]
    depth = blocks[0].shape[1]
    width = gain_ref.shape[1]
    seg = BLOCK // SEGS
    count = rows // BLOCK
    lines_of = wbuf.shape[3]
    parts = depth // lines_of
    slot = lax.rem(place[0], half)
    base = ((place[0] // half) ^ 1) * (half * depth)

    def w_copy(g, d, q):
        top = base + (slot ^ d) * depth + q * lines_of
        lines = pl.ds(pl.multiple_of(top, lines_of), lines_of)
        return pltpu.make_async_copy(w_ref.at[g, lines, :], wbuf.at[g, d, q], wsem.at[g, d, q])

    every = [(d, q) for d in range(half) for q in range(parts)]
    for g in range(2):
        for d, q in every:
            w_copy(g, d, q).start()
    for g in range(2):
        for d, q in every:
            w_copy(g, d, q).wait()
            deep = slice(q * lines_of, (q + 1) * lines_of)
            part = jnp.dot(blocks[d][:, deep], wbuf[g, d, q], preferred_element_type=F32)
            if (d, q) == (0, 0):
                acc[g] = part
            else:
                acc[g] += part

    span = tile_of(width, 512)

    def columns(n, carry_out):
        wide = pl.ds(pl.multiple_of(n * span, span), span)
        gain = jnp.broadcast_to(gain_ref[:, wide], (SEGS, span))
        bias = [jnp.broadcast_to(bias_ref[g : g + 1, wide], (2 * SEGS, span)) for g in range(2)]

        def pair(jj, carry, first):
            out = []
            for c in range(count):
                a, b = carry[c]
                lines = pl.ds(pl.multiple_of(c * BLOCK + jj * 2 * SEGS, 2 * SEGS), 2 * SEGS)
                deep = pl.ds(
                    pl.multiple_of(first_row + c * BLOCK + jj * 2 * SEGS, 2 * SEGS), 2 * SEGS
                )
                held = []
                for g in range(2):
                    total = acc[g, lines, wide] + part_ref[g, deep, wide] + bias[g]
                    rounded = total.astype(BF16)
                    gates_ref[g, lines, wide] = rounded
                    held.append(rounded.astype(F32))
                for k in range(2):
                    pre = held[0][k * SEGS : (k + 1) * SEGS]
                    cand = held[1][k * SEGS : (k + 1) * SEGS]
                    update, keep, scaled, slope, offset = first_slopes(pre, cand, gain)
                    if first and k == 0 and c == 0:
                        prev = lead_row(place, start_ref[:, wide], (SEGS, span))
                        slope, offset = around(update, keep, scaled, cand, gain, prev)
                    b = slope * b + offset
                    a = slope * a
                out.append((a, b))
            return tuple(out)

        carry = ((jnp.ones((SEGS, span), F32), jnp.zeros((SEGS, span), F32)),) * count
        begin = 0
        if first_row == 0:
            carry = pair(0, carry, True)
            begin = 1
        carry = lax.fori_loop(begin, seg // 2, lambda jj, c: pair(jj, c, False), carry)
        for c in range(count):
            maps_ref[0, c * SEGS : (c + 1) * SEGS, wide] = carry[c][0]
            maps_ref[1, c * SEGS : (c + 1) * SEGS, wide] = carry[c][1]
        return carry_out

    lax.fori_loop(0, width // span, columns, 0)
    if last:
        ta, tb = jnp.ones((1, width), F32), jnp.zeros((1, width), F32)
        for maps in list(earlier) + [maps_ref]:
            ta, tb = compose_rows(maps, maps.shape[1], ta, tb)
        for i in range(total_ref.shape[0]):
            total_ref[i, 0:1, :] = ta
            total_ref[i, 1:2, :] = tb


def gate_chunk(place, blocks, partial, weights, biases, gain, start, earlier, first_row, last, peers):
    half = len(blocks)
    rows, depth = blocks[0].shape
    gates, _, width = weights.shape
    lines_of = tile_of(depth, 512)
    vmem = pl.BlockSpec(memory_space=pltpu.VMEM)
    out_shape = [
        jax.ShapeDtypeStruct((2, rows, width), BF16),
        jax.ShapeDtypeStruct((2, rows // BLOCK * SEGS, width), F32),
    ]
    if last:
        out_shape.append(jax.ShapeDtypeStruct((peers, 2, width), F32))
    return pl.pallas_call(
        functools.partial(gate_kernel, half, first_row, rows, len(earlier), last),
        out_shape=out_shape,
        in_specs=[pl.BlockSpec(memory_space=pltpu.SMEM)]
        + [vmem] * (half + 1)
        + [pl.BlockSpec(memory_space=pltpu.HBM)]
        + [vmem] * (3 + len(earlier)),
        out_specs=[vmem] * len(out_shape),
        scratch_shapes=[
            pltpu.VMEM((gates, half, depth // lines_of, lines_of, width), BF16),
            pltpu.VMEM((gates, rows, width), F32),
            pltpu.SemaphoreType.DMA((gates, half, depth // lines_of)),
        ],
        compiler_params=params(32),
        cost_estimate=cost(
            2 * gates * rows * half * depth * width,
            gates * width * (half * depth * 2 + rows * 6) + half * rows * depth * 2,
            4 * rows * width,
        ),
    )(place, *blocks, partial, weights, biases, gain, start, *earlier)


def entering_state(place, peer_maps, start, peers):
    state = start
    for k in range(peers):
        moved = peer_maps[k, 0:1, :] * state + peer_maps[k, 1:2, :]
        state = jnp.where(place[1] > k, moved, state)
    return state


def enter_segments(maps_list, state, enter):
    row = 0
    for maps in maps_list:
        for k in range(maps.shape[1]):
            enter[row : row + 1, :] = state
            state = maps[0, k : k + 1, :] * state + maps[1, k : k + 1, :]
            row += 1


def bend_kernel(chunks, peers, place, *refs):
    gates = refs[:chunks]
    maps = refs[chunks : 2 * chunks]
    peer_ref, gain_ref, start_ref, run_ref, maps_ref, total_ref, enter = refs[2 * chunks :]
    span = gates[0].shape[2]
    width = gain_ref.shape[1]
    where = [(c, r * BLOCK) for c in range(chunks) for r in range(gates[c].shape[1] // BLOCK)]
    n = pl.program_id(0)

    @pl.when(n == 0)
    def _():
        enter_segments(maps, entering_state(place, peer_ref, start_ref[...], peers), enter)

    wide = pl.ds(pl.multiple_of(n * span, span), span)
    gain = jnp.broadcast_to(gain_ref[:, wide], (SEGS, span))

    def advance(block, jj, held, first):
        state, a, b = held
        c, top = where[block]
        lines = pl.ds(pl.multiple_of(top + jj * 2 * SEGS, 2 * SEGS), 2 * SEGS)
        pre2 = gates[c][0, lines, :].astype(F32)
        cand2 = gates[c][1, lines, :].astype(F32)
        for k in range(2):
            pre = pre2[k * SEGS : (k + 1) * SEGS]
            cand = cand2[k * SEGS : (k + 1) * SEGS]
            update, keep, scaled, slope, offset = first_slopes(pre, cand, gain)
            if first and k == 0 and block == 0:
                prev = lead_row(place, start_ref[:, wide], (SEGS, span))
                slope, offset = around(update, keep, scaled, cand, gain, prev)
            slope2, offset2 = around(update, keep, scaled, cand, gain, state)
            state = slope * state + offset
            b = slope2 * b + offset2
            a = slope2 * a
            row = pl.ds(pl.multiple_of(block * BLOCK + (2 * jj + k) * SEGS, SEGS), SEGS)
            run_ref[0, row, :] = a
            run_ref[1, row, :] = b
        return state, a, b

    def pair(jj, carry, first):
        return tuple(advance(m, jj, carry[m], first) for m in range(len(where)))

    one, zero = jnp.ones((SEGS, span), F32), jnp.zeros((SEGS, span), F32)
    carry = tuple((enter[m * SEGS : (m + 1) * SEGS, wide], one, zero) for m in range(len(where)))
    carry = pair(0, carry, True)
    carry = lax.fori_loop(1, BLOCK // SEGS // 2, lambda jj, c: pair(jj, c, False), carry)
    for m in range(len(where)):
        maps_ref[0, m * SEGS : (m + 1) * SEGS, wide] = carry[m][1]
        maps_ref[1, m * SEGS : (m + 1) * SEGS, wide] = carry[m][2]

    @pl.when(n == pl.num_programs(0) - 1)
    def _():
        ta, tb = jnp.ones((1, width), F32), jnp.zeros((1, width), F32)
        ta, tb = compose_rows(maps_ref, maps_ref.shape[1], ta, tb)
        for i in range(peers):
            total_ref[i, 0:1, :] = ta
            total_ref[i, 1:2, :] = tb


def bend_all(place, gates, maps, peer_maps, gain, start):
    chunks = len(gates)
    peers = peer_maps.shape[0]
    width = gates[0].shape[2]
    total_rows = sum(g.shape[1] for g in gates)
    segs = total_rows // BLOCK * SEGS
    tn = tile_of(width, 256)
    row_spec = pl.BlockSpec((1, width), lambda n, p: (0, 0))
    total_spec = pl.BlockSpec((peers, 2, width), lambda n, p: (0, 0, 0))
    return pl.pallas_call(
        functools.partial(bend_kernel, chunks, peers),
        out_shape=[
            jax.ShapeDtypeStruct((2, total_rows, width), F32),
            jax.ShapeDtypeStruct((2, segs, width), F32),
            jax.ShapeDtypeStruct((peers, 2, width), F32),
        ],
        grid_spec=pltpu.PrefetchScalarGridSpec(
            num_scalar_prefetch=1,
            grid=(width // tn,),
            in_specs=[pl.BlockSpec((2, g.shape[1], tn), lambda n, p: (0, 0, n)) for g in gates]
            + [pl.BlockSpec((2, m.shape[1], width), lambda n, p: (0, 0, 0)) for m in maps]
            + [total_spec, row_spec, row_spec],
            out_specs=[
                pl.BlockSpec((2, total_rows, tn), lambda n, p: (0, 0, n)),
                pl.BlockSpec((2, segs, width), lambda n, p: (0, 0, 0)),
                total_spec,
            ],
            scratch_shapes=[pltpu.VMEM((segs, width), F32)],
        ),
        compiler_params=params(16),
        cost_estimate=cost(
            40 * total_rows * width, 12 * total_rows * width, 5 * total_rows * width
        ),
        name="bend",
    )(place, *gates, *maps, peer_maps, gain, start)


def state_kernel(first_row, peers, place, run_ref, maps_ref, peer_ref, start_ref, out_ref, enter):
    rows = out_ref.shape[0]
    begin = first_row // BLOCK * SEGS
    state = entering_state(place, peer_ref, start_ref[...], peers)
    for k in range(begin + rows // BLOCK * SEGS):
        if k >= begin:
            enter[k - begin : k - begin + 1, :] = state
        state = maps_ref[0, k : k + 1, :] * state + maps_ref[1, k : k + 1, :]
    for c in range(rows // BLOCK):
        once = enter[c * SEGS : (c + 1) * SEGS, :]
        entered = jnp.concatenate([once, once], axis=0)

        def step(jj, carry):
            at = pl.multiple_of(c * BLOCK + jj * 2 * SEGS, 2 * SEGS)
            lines = pl.ds(at, 2 * SEGS)
            deep = pl.ds(pl.multiple_of(first_row + at, 2 * SEGS), 2 * SEGS)
            out_ref[lines, :] = (run_ref[0, deep, :] * entered + run_ref[1, deep, :]).astype(BF16)
            return carry

        lax.fori_loop(0, BLOCK // SEGS // 2, step, 0)


def state_chunk(place, run, maps, peer_maps, start, first_row, rows):
    width = run.shape[2]
    peers = peer_maps.shape[0]
    vmem = pl.BlockSpec(memory_space=pltpu.VMEM)
    return pl.pallas_call(
        functools.partial(state_kernel, first_row, peers),
        out_shape=jax.ShapeDtypeStruct((rows, width), BF16),
        in_specs=[pl.BlockSpec(memory_space=pltpu.SMEM)] + [vmem] * 4,
        out_specs=vmem,
        scratch_shapes=[pltpu.VMEM((rows // BLOCK * SEGS, width), F32)],
        compiler_params=params(16),
        cost_estimate=cost(2 * rows * width, 10 * rows * width),
    )(place, run, maps, peer_maps, start)


def mix_kernel(groups, group, cuts, peers, slots, final, before, place, *refs):
    count = groups * group
    blocks = refs[:count]
    starts = [sum(len(cut) for cut in cuts[:n]) for n in range(len(cuts) + 1)]
    weights = refs[count : count + starts[-1]]
    out_ref, lhs, wbuf, acc, lsem, wsem = refs[-6:]
    prev_refs = refs[count + len(weights) : count + len(weights) + before]
    depth = blocks[0].shape[1]
    heights = [blocks[c * group].shape[0] for c in range(groups)]
    outer = peers // 2
    here = len(slots) * 2

    def w_copy(n, p):
        w_ref = weights[starts[n] + p]
        top = sum(cuts[n][:p])
        dst = wbuf.at[n, top : top + cuts[n][p], :]
        return pltpu.make_async_copy(w_ref, dst, wsem.at[n, p])

    def l_copy(c, d):
        deep = pl.ds(pl.multiple_of((place[0] ^ d) * depth, depth), depth)
        top = sum(heights[:c])
        dst = lhs.at[top : top + heights[c], deep]
        return pltpu.make_async_copy(blocks[c * group + d], dst, lsem.at[c, d])

    for n in range(here):
        for p in range(len(cuts[n])):
            w_copy(n, p).start()
    for c in range(groups):
        for d in range(group):
            l_copy(c, d).start()
    for c in range(groups):
        for d in range(group):
            l_copy(c, d).wait()
    top = 0
    for prev in prev_refs:
        acc[top : top + prev.shape[0], :] = prev[...]
        top += prev.shape[0]
    span = wbuf.shape[1]
    for n in range(here):
        source = lax.rem(place[1] // 2 + outer - slots[n // 2], outer)
        owner = source * 2 + (lax.rem(place[1], 2) ^ (n % 2))
        deep = pl.ds(pl.multiple_of(owner * span, span), span)
        for p in range(len(cuts[n])):
            w_copy(n, p).wait()
        part = jnp.dot(lhs[:, deep], wbuf[n], preferred_element_type=F32)
        if n > 0 or before:
            part = acc[...] + part
        if n < here - 1:
            acc[...] = part
        elif not final:
            out_ref[...] = part
        else:
            acc[...] = part
            order = row_order(True)
            for m in range(acc.shape[0] // BLOCK):
                lines = slice(m * BLOCK, (m + 1) * BLOCK)
                rounded = acc[lines, :].astype(BF16)
                moved = jnp.dot(order, rounded, preferred_element_type=F32)
                out_ref[lines, :] = moved.astype(BF16)


def mix_rows(place, blocks, weights, slots, prev, final, whole, first, total_rows):
    groups, group = len(blocks), len(blocks[0])
    depth = blocks[0][0].shape[1]
    width = weights[0][0].shape[1]
    peers = len(weights)
    span = sum(piece.shape[0] for piece in weights[0])
    rows = sum(g[0].shape[0] for g in blocks)
    chosen = [weights[s * 2 + i] for s in slots for i in range(2)]
    cuts = tuple(tuple(piece.shape[0] for piece in pieces) for pieces in chosen)
    used = [piece for pieces in chosen for piece in pieces]
    most = max(len(cut) for cut in cuts)
    args = [place] + [b for g in blocks for b in g] + used
    in_specs = [pl.BlockSpec(memory_space=pl.ANY)] * (groups * group)
    in_specs += [pl.BlockSpec(memory_space=pltpu.HBM)] * len(used)
    args += prev
    in_specs += [pl.BlockSpec((q.shape[0], width), lambda n, p: (0, 0)) for q in prev]
    aliases = {}
    if whole is not None:
        aliases = {len(args): 0}
        args.append(whole)
        in_specs.append(pl.BlockSpec(memory_space=pl.ANY))
    deep = len(slots) * 2 * span
    if final:
        out_shape = jax.ShapeDtypeStruct((total_rows, width), BF16)
        out_spec = pl.BlockSpec((rows, width), lambda n, p: (first // rows, 0))
    else:
        out_shape = jax.ShapeDtypeStruct((rows, width), F32)
        out_spec = pl.BlockSpec((rows, width), lambda n, p: (0, 0))
    return pl.pallas_call(
        functools.partial(
            mix_kernel, groups, group, cuts, peers, tuple(slots), final, len(prev)
        ),
        out_shape=out_shape,
        grid_spec=pltpu.PrefetchScalarGridSpec(
            num_scalar_prefetch=1,
            grid=(1,),
            in_specs=in_specs,
            out_specs=out_spec,
            scratch_shapes=[
                pltpu.VMEM((rows, group * depth), BF16),
                pltpu.VMEM((len(slots) * 2, span, width), BF16),
                pltpu.VMEM((rows, width), F32),
                pltpu.SemaphoreType.DMA((groups, group)),
                pltpu.SemaphoreType.DMA((len(slots) * 2, most)),
            ],
        ),
        input_output_aliases=aliases,
        compiler_params=params(40 if peers <= 8 else 62),
        cost_estimate=cost(2 * rows * deep * width, 2 * deep * (width + rows) + 4 * rows * width),
    )(*args)


SHARES = (2, 1, 1)
RINGS_EARLY = 2
SWAPS_EARLY = 1


def cut_of(rows, shares):
    parts = [rows * share // sum(shares) for share in shares]
    return parts if min(parts) >= LANES else [rows]


def ring_cut(step, outer, rows):
    return cut_of(rows, (1, 1) if step == outer - 1 else (1,))


def swap_cut(step, outer, rows):
    if step == SWAPS_EARLY + 1 and step < outer - 1:
        return cut_of(rows, (1, 3))
    return ring_cut(step, outer, rows)


def recut(blocks, parts):
    if [b.shape[0] for b in blocks] == parts:
        return blocks
    (block,) = blocks
    tops = [sum(parts[:p]) for p in range(len(parts))]
    return [block[top : top + part] for top, part in zip(tops, parts)]


def behind(block, gate):
    return block if gate is None else lax.optimization_barrier((block, gate))[0]


def gather_early(w_output):
    peers = lax.axis_size("ctx")
    route = [(i, (i + 2) % peers) for i in range(peers)]
    held = {(0, 0): [w_output]}
    for step in range(1, min(RINGS_EARLY + 1, peers // 2)):
        held[step, 0] = [lax.ppermute(held[step - 1, 0][0], "ctx", route)]
    for step in range(SWAPS_EARLY + 1):
        held[step, 1] = [swap(held[step, 0][0], "ctx", 1)]
    return held


def next_cuts(outer, rows):
    return [ring_cut(RINGS_EARLY + 1, outer, rows), swap_cut(SWAPS_EARLY + 1, outer, rows)]


def gather_late(held, following, middle, late):
    peers = lax.axis_size("ctx")
    outer = peers // 2
    rows = held[0, 0][0].shape[0]
    route = [(i, (i + 2) % peers) for i in range(peers)]
    for step in range(RINGS_EARLY + 1, outer):
        held[step, 0] = []
        if step == RINGS_EARLY + 1:
            source = following[0]
        else:
            source = recut(held[step - 1, 0], ring_cut(step, outer, rows))
        for block in source:
            held[step, 0].append(lax.ppermute(behind(block, late), "ctx", route))
    for step in range(SWAPS_EARLY + 1, outer):
        held[step, 1] = []
        if step == SWAPS_EARLY + 1:
            source = following[1]
        else:
            source = recut(held[step, 0], swap_cut(step, outer, rows))
        for p, block in enumerate(source):
            gate = middle if step == SWAPS_EARLY + 1 and p == 0 else late
            held[step, 1].append(swap(behind(block, gate), "ctx", 1))
    return [held[step, i] for step in range(outer) for i in range(2)]


def layer(tokens, w_input, w_output, bias_update, bias_cand, recur_gain, start_state):
    peers = lax.axis_size("ctx")
    group = lax.axis_size("ch")
    half = group // 2
    total_rows = tokens.shape[0]
    chunks = len(SHARES)
    sizes = [total_rows * share // sum(SHARES) for share in SHARES]
    firsts = [sum(sizes[:c]) for c in range(chunks)]
    place = jnp.stack([lax.axis_index("ch"), lax.axis_index("ctx")]).astype(jnp.int32)
    biases = jnp.stack([bias_update, bias_cand], axis=0)
    gain = recur_gain[None, :]
    start = start_state[None, :]

    *ordered, whole = split_rows(tokens, 0, sizes, True)
    far = []
    for piece in ordered:
        far.append([swap(piece, "ch", half)])
    near = [[whole]]
    for d in range(1, half):
        near.append([swap(whole, "ch", d)])
    for c in range(chunks):
        for d in range(1, half):
            far[c].append(swap(far[c][0], "ch", d))

    partial = near_product(place, near, w_input)
    gates, maps = [], []
    for c in range(chunks):
        last = c == chunks - 1
        out = gate_chunk(
            place,
            far[c],
            partial,
            w_input,
            biases,
            gain,
            start,
            maps if last else [],
            firsts[c],
            last,
            peers,
        )
        gates.append(out[0])
        maps.append(out[1])
    held = gather_early(w_output)
    following = [recut(held[RINGS_EARLY, 0], cut) for cut in next_cuts(peers // 2, w_output.shape[0])]
    following, totals = lax.optimization_barrier((following, out[2]))
    first_maps = lax.all_to_all(totals, "ctx", 0, 0, tiled=True)
    run, run_maps, totals = bend_all(place, gates, maps, first_maps, gain, start)
    peer_maps = lax.all_to_all(totals, "ctx", 0, 0, tiled=True)
    weights = gather_late(held, following, first_maps, peer_maps)

    blocks = []
    for c in range(chunks):
        own = state_chunk(place, run, run_maps, peer_maps, start, firsts[c], sizes[c])
        across = swap(own, "ch", half)
        blocks.append([own, across])
    for c in range(chunks):
        own, across = blocks[c]
        lows, highs = [own], [across]
        for d in range(1, half):
            lows.append(swap(own, "ch", d))
            highs.append(swap(across, "ch", d))
        blocks[c] = lows + highs
    outer = peers // 2
    late = max(1, outer // 4)
    slots = list(range(outer))

    def mix(part, used, prev, final, whole):
        return mix_rows(
            place,
            blocks[part],
            weights,
            used,
            prev,
            final,
            whole,
            firsts[part][0],
            total_rows,
        )

    early, late_slots = slots[:-late], slots[-late:]
    partials = [mix(slice(c, c + 1), early, [], False, None) for c in range(chunks - 1)]
    mixed = mix(slice(0, chunks - 1), late_slots, partials, True, None)
    mixed = mix(slice(chunks - 1, chunks), slots, [], True, mixed)
    return mixed


def solution(mesh):
    return jax.shard_map(
        layer,
        mesh=mesh,
        in_specs=(
            P("ctx", "ch"),
            P(None, None, "ch"),
            P("ctx", "ch"),
            P("ch"),
            P("ch"),
            P("ch"),
            P("ch"),
        ),
        out_specs=P("ctx", "ch"),
        check_vma=False,
    )
```

```python
import functools
import math

import jax
import jax.numpy as jnp
from jax import lax
from jax.experimental import pallas as pl
from jax.experimental.pallas import tpu as pltpu
from jax.sharding import PartitionSpec as P


SEGS = 8
LANES = 128
BLOCK = 256
F32 = jnp.float32
BF16 = jnp.bfloat16
MIB = 1024 * 1024


def swap(block, axis, bits):
    return lax.ppermute(block, axis, [(i, i ^ bits) for i in range(lax.axis_size(axis))])


def tile_of(width, most):
    return math.gcd(width, most)


def params(mib):
    return pltpu.CompilerParams(vmem_limit_bytes=mib * MIB)


def cost(flops, nbytes, trans=0):
    return pl.CostEstimate(flops=int(flops), bytes_accessed=int(nbytes), transcendentals=int(trans))


def near_kernel(half, tiles, heights, place, *refs):
    count = len(heights)
    blocks = refs[: half * count]
    w_ref, out_ref, lhs, wbuf, lsem, wsem = refs[half * count :]
    depth = blocks[0].shape[1]
    span = wbuf.shape[2]
    slot = lax.rem(place[0], half)
    base = (place[0] // half) * (half * depth)

    def w_copy(n):
        lines = pl.ds(pl.multiple_of(base, half * depth), half * depth)
        wide = pl.ds(pl.multiple_of(lax.rem(n, tiles) * span, span), span)
        return pltpu.make_async_copy(w_ref.at[n // tiles, lines, wide], wbuf.at[n], wsem.at[n])

    def l_copy(d, k):
        deep = pl.ds(pl.multiple_of((slot ^ d) * depth, depth), depth)
        top = sum(heights[:k])
        dst = lhs.at[top : top + heights[k], deep]
        return pltpu.make_async_copy(blocks[d * count + k], dst, lsem.at[d, k])

    steps = wbuf.shape[0]
    for n in range(steps):
        w_copy(n).start()
    for d in range(half):
        for k in range(count):
            l_copy(d, k).start()
    for d in range(half):
        for k in range(count):
            l_copy(d, k).wait()

    def body(n, carry):
        w_copy(n).wait()
        wide = pl.ds(pl.multiple_of(lax.rem(n, tiles) * span, span), span)
        total = None
        for d in range(half):
            deep = slice(d * depth, (d + 1) * depth)
            part = jnp.dot(lhs[:, deep], wbuf[n, deep, :], preferred_element_type=F32)
            total = part if total is None else total + part
        out_ref[n // tiles, :, wide] = total
        return carry

    lax.fori_loop(0, steps, body, 0)


def near_product(place, blocks, weights):
    half = len(blocks)
    heights = tuple(b.shape[0] for b in blocks[0])
    rows, depth = sum(heights), blocks[0][0].shape[1]
    gates, _, width = weights.shape
    span = tile_of(width, 512)
    tiles = width // span
    return pl.pallas_call(
        functools.partial(near_kernel, half, tiles, heights),
        out_shape=jax.ShapeDtypeStruct((gates, rows, width), F32),
        in_specs=[pl.BlockSpec(memory_space=pltpu.SMEM)]
        + [pl.BlockSpec(memory_space=pl.ANY)] * (half * len(heights))
        + [pl.BlockSpec(memory_space=pltpu.HBM)],
        out_specs=pl.BlockSpec(memory_space=pltpu.VMEM),
        scratch_shapes=[
            pltpu.VMEM((rows, half * depth), BF16),
            pltpu.VMEM((gates * tiles, half * depth, span), BF16),
            pltpu.SemaphoreType.DMA((half, len(heights))),
            pltpu.SemaphoreType.DMA((gates * tiles,)),
        ],
        compiler_params=params(28),
        cost_estimate=cost(
            2 * gates * rows * half * depth * width,
            gates * width * (half * depth * 2 + rows * 4) + half * rows * depth * 2,
        ),
    )(place, *[piece for block in blocks for piece in block], weights)


def row_order(transposed):
    shape = (BLOCK, BLOCK)
    row = lax.broadcasted_iota(jnp.int32, shape, 1 if transposed else 0)
    token = lax.broadcasted_iota(jnp.int32, shape, 0 if transposed else 1)
    chosen = lax.rem(row, SEGS) * (BLOCK // SEGS) + row // SEGS == token
    return jnp.where(chosen, 1.0, 0.0).astype(BF16)


def split_kernel(first, sizes, joined, src, *refs):
    count = len(sizes)
    if joined:
        head, refs = refs[0], refs[1:]
    outs = refs[:count]
    buf, sem, head_sem = refs[-3:]
    blocks = sum(sizes) // BLOCK
    copies = []
    for k in range(blocks):
        lines = pl.ds(first + k * BLOCK, BLOCK)
        copies.append(pltpu.make_async_copy(src.at[lines, :], buf.at[k], sem.at[k]))
    for copy in copies:
        copy.start()
    if joined:
        join = pltpu.make_async_copy(head, refs[count].at[0:first, :], head_sem)
        join.start()
    order = row_order(False)
    k = 0
    for c in range(count):
        for r in range(sizes[c] // BLOCK):
            copies[k].wait()
            moved = jnp.dot(order, buf[k], preferred_element_type=F32).astype(BF16)
            outs[c][r * BLOCK : (r + 1) * BLOCK, :] = moved
            if joined:
                refs[count][first + k * BLOCK : first + (k + 1) * BLOCK, :] = moved
            k += 1
    if joined:
        join.wait()


def split_rows(array, first, sizes, head):
    vmem = pl.BlockSpec(memory_space=pltpu.VMEM)
    rows, width = sum(sizes), array.shape[1]
    joined = head is not None
    shapes = list(sizes) + ([first + rows] if joined else [])
    args = [array] + ([head] if joined else [])
    return pl.pallas_call(
        functools.partial(split_kernel, first, tuple(sizes), joined),
        out_shape=[jax.ShapeDtypeStruct((r, width), array.dtype) for r in shapes],
        in_specs=[pl.BlockSpec(memory_space=pl.ANY)] * len(args),
        out_specs=[vmem] * len(shapes),
        scratch_shapes=[
            pltpu.VMEM((rows // BLOCK, BLOCK, width), BF16),
            pltpu.SemaphoreType.DMA((rows // BLOCK,)),
            pltpu.SemaphoreType.DMA,
        ],
        compiler_params=params(60),
        cost_estimate=cost(2 * rows * BLOCK * width, 4 * rows * width),
    )(*args)


def compose_rows(maps, count, a, b):
    for k in range(count):
        slope = maps[0, k : k + 1, :]
        shift = maps[1, k : k + 1, :]
        b = slope * b + shift
        a = slope * a
    return a, b


def first_slopes(pre, cand, gain):
    update = jax.nn.sigmoid(pre)
    keep = 1.0 - update
    scaled = update * gain
    squashed = jnp.tanh(cand)
    slope = keep + (scaled - scaled * squashed * squashed)
    return update, keep, scaled, slope, update * squashed


def lead_row(place, start, shape):
    lead = lax.broadcasted_iota(jnp.int32, shape, 0) == 0
    return jnp.where(lead & (place[1] == 0), start, 0.0)


def around(update, keep, scaled, cand, gain, prev):
    squashed = jnp.tanh(cand + gain * prev)
    bend = scaled - scaled * squashed * squashed
    return keep + bend, update * squashed - bend * prev


def gate_kernel(half, first_row, rows, before, last, place, *refs):
    blocks = refs[:half]
    part_ref, w_ref, bias_ref, gain_ref, start_ref = refs[half : half + 5]
    earlier = refs[half + 5 : half + 5 + before]
    rest = refs[half + 5 + before :]
    if last:
        gates_ref, maps_ref, total_ref = rest[:3]
    else:
        gates_ref, maps_ref = rest[:2]
    wbuf, acc, wsem = rest[-3:]
    depth = blocks[0].shape[1]
    width = gain_ref.shape[1]
    seg = BLOCK // SEGS
    count = rows // BLOCK
    lines_of = wbuf.shape[3]
    parts = depth // lines_of
    slot = lax.rem(place[0], half)
    base = ((place[0] // half) ^ 1) * (half * depth)

    def w_copy(g, d, q):
        top = base + (slot ^ d) * depth + q * lines_of
        lines = pl.ds(pl.multiple_of(top, lines_of), lines_of)
        return pltpu.make_async_copy(w_ref.at[g, lines, :], wbuf.at[g, d, q], wsem.at[g, d, q])

    every = [(d, q) for d in range(half) for q in range(parts)]
    for g in range(2):
        for d, q in every:
            w_copy(g, d, q).start()
    for g in range(2):
        for d, q in every:
            w_copy(g, d, q).wait()
            deep = slice(q * lines_of, (q + 1) * lines_of)
            part = jnp.dot(blocks[d][:, deep], wbuf[g, d, q], preferred_element_type=F32)
            if (d, q) == (0, 0):
                acc[g] = part
            else:
                acc[g] += part

    span = tile_of(width, 512)

    def columns(n, carry_out):
        wide = pl.ds(pl.multiple_of(n * span, span), span)
        gain = jnp.broadcast_to(gain_ref[:, wide], (SEGS, span))
        bias = [jnp.broadcast_to(bias_ref[g : g + 1, wide], (2 * SEGS, span)) for g in range(2)]

        def pair(jj, carry, first):
            out = []
            for c in range(count):
                a, b = carry[c]
                lines = pl.ds(pl.multiple_of(c * BLOCK + jj * 2 * SEGS, 2 * SEGS), 2 * SEGS)
                deep = pl.ds(
                    pl.multiple_of(first_row + c * BLOCK + jj * 2 * SEGS, 2 * SEGS), 2 * SEGS
                )
                held = []
                for g in range(2):
                    total = acc[g, lines, wide] + part_ref[g, deep, wide] + bias[g]
                    rounded = total.astype(BF16)
                    gates_ref[g, lines, wide] = rounded
                    held.append(rounded.astype(F32))
                for k in range(2):
                    pre = held[0][k * SEGS : (k + 1) * SEGS]
                    cand = held[1][k * SEGS : (k + 1) * SEGS]
                    update, keep, scaled, slope, offset = first_slopes(pre, cand, gain)
                    if first and k == 0 and c == 0:
                        prev = lead_row(place, start_ref[:, wide], (SEGS, span))
                        slope, offset = around(update, keep, scaled, cand, gain, prev)
                    b = slope * b + offset
                    a = slope * a
                out.append((a, b))
            return tuple(out)

        carry = ((jnp.ones((SEGS, span), F32), jnp.zeros((SEGS, span), F32)),) * count
        begin = 0
        if first_row == 0:
            carry = pair(0, carry, True)
            begin = 1
        carry = lax.fori_loop(begin, seg // 2, lambda jj, c: pair(jj, c, False), carry)
        for c in range(count):
            maps_ref[0, c * SEGS : (c + 1) * SEGS, wide] = carry[c][0]
            maps_ref[1, c * SEGS : (c + 1) * SEGS, wide] = carry[c][1]
        return carry_out

    lax.fori_loop(0, width // span, columns, 0)
    if last:
        ta, tb = jnp.ones((1, width), F32), jnp.zeros((1, width), F32)
        for maps in list(earlier) + [maps_ref]:
            ta, tb = compose_rows(maps, maps.shape[1], ta, tb)
        for i in range(total_ref.shape[0]):
            total_ref[i, 0:1, :] = ta
            total_ref[i, 1:2, :] = tb


def gate_chunk(place, blocks, partial, weights, biases, gain, start, earlier, first_row, last, peers):
    half = len(blocks)
    rows, depth = blocks[0].shape
    gates, _, width = weights.shape
    lines_of = tile_of(depth, 512)
    vmem = pl.BlockSpec(memory_space=pltpu.VMEM)
    out_shape = [
        jax.ShapeDtypeStruct((2, rows, width), BF16),
        jax.ShapeDtypeStruct((2, rows // BLOCK * SEGS, width), F32),
    ]
    if last:
        out_shape.append(jax.ShapeDtypeStruct((peers, 2, width), F32))
    return pl.pallas_call(
        functools.partial(gate_kernel, half, first_row, rows, len(earlier), last),
        out_shape=out_shape,
        in_specs=[pl.BlockSpec(memory_space=pltpu.SMEM)]
        + [vmem] * (half + 1)
        + [pl.BlockSpec(memory_space=pltpu.HBM)]
        + [vmem] * (3 + len(earlier)),
        out_specs=[vmem] * len(out_shape),
        scratch_shapes=[
            pltpu.VMEM((gates, half, depth // lines_of, lines_of, width), BF16),
            pltpu.VMEM((gates, rows, width), F32),
            pltpu.SemaphoreType.DMA((gates, half, depth // lines_of)),
        ],
        compiler_params=params(32),
        cost_estimate=cost(
            2 * gates * rows * half * depth * width,
            gates * width * (half * depth * 2 + rows * 6) + half * rows * depth * 2,
            4 * rows * width,
        ),
    )(place, *blocks, partial, weights, biases, gain, start, *earlier)


def entering_state(place, peer_maps, start, peers):
    state = start
    for k in range(peers):
        moved = peer_maps[k, 0:1, :] * state + peer_maps[k, 1:2, :]
        state = jnp.where(place[1] > k, moved, state)
    return state


def enter_segments(maps_list, state, enter):
    row = 0
    for maps in maps_list:
        for k in range(maps.shape[1]):
            enter[row : row + 1, :] = state
            state = maps[0, k : k + 1, :] * state + maps[1, k : k + 1, :]
            row += 1


def bend_kernel(chunks, peers, place, *refs):
    gates = refs[:chunks]
    maps = refs[chunks : 2 * chunks]
    peer_ref, gain_ref, start_ref, run_ref, maps_ref, total_ref, enter = refs[2 * chunks :]
    span = gates[0].shape[2]
    width = gain_ref.shape[1]
    where = [(c, r * BLOCK) for c in range(chunks) for r in range(gates[c].shape[1] // BLOCK)]
    n = pl.program_id(0)

    @pl.when(n == 0)
    def _():
        enter_segments(maps, entering_state(place, peer_ref, start_ref[...], peers), enter)

    wide = pl.ds(pl.multiple_of(n * span, span), span)
    gain = jnp.broadcast_to(gain_ref[:, wide], (SEGS, span))

    def advance(block, jj, held, first):
        state, a, b = held
        c, top = where[block]
        lines = pl.ds(pl.multiple_of(top + jj * 2 * SEGS, 2 * SEGS), 2 * SEGS)
        pre2 = gates[c][0, lines, :].astype(F32)
        cand2 = gates[c][1, lines, :].astype(F32)
        for k in range(2):
            pre = pre2[k * SEGS : (k + 1) * SEGS]
            cand = cand2[k * SEGS : (k + 1) * SEGS]
            update, keep, scaled, slope, offset = first_slopes(pre, cand, gain)
            if first and k == 0 and block == 0:
                prev = lead_row(place, start_ref[:, wide], (SEGS, span))
                slope, offset = around(update, keep, scaled, cand, gain, prev)
            slope2, offset2 = around(update, keep, scaled, cand, gain, state)
            state = slope * state + offset
            b = slope2 * b + offset2
            a = slope2 * a
            row = pl.ds(pl.multiple_of(block * BLOCK + (2 * jj + k) * SEGS, SEGS), SEGS)
            run_ref[0, row, :] = a
            run_ref[1, row, :] = b
        return state, a, b

    def pair(jj, carry, first):
        return tuple(advance(m, jj, carry[m], first) for m in range(len(where)))

    one, zero = jnp.ones((SEGS, span), F32), jnp.zeros((SEGS, span), F32)
    carry = tuple((enter[m * SEGS : (m + 1) * SEGS, wide], one, zero) for m in range(len(where)))
    carry = pair(0, carry, True)
    carry = lax.fori_loop(1, BLOCK // SEGS // 2, lambda jj, c: pair(jj, c, False), carry)
    for m in range(len(where)):
        maps_ref[0, m * SEGS : (m + 1) * SEGS, wide] = carry[m][1]
        maps_ref[1, m * SEGS : (m + 1) * SEGS, wide] = carry[m][2]

    @pl.when(n == pl.num_programs(0) - 1)
    def _():
        ta, tb = jnp.ones((1, width), F32), jnp.zeros((1, width), F32)
        ta, tb = compose_rows(maps_ref, maps_ref.shape[1], ta, tb)
        for i in range(peers):
            total_ref[i, 0:1, :] = ta
            total_ref[i, 1:2, :] = tb


def bend_all(place, gates, maps, peer_maps, gain, start):
    chunks = len(gates)
    peers = peer_maps.shape[0]
    width = gates[0].shape[2]
    total_rows = sum(g.shape[1] for g in gates)
    segs = total_rows // BLOCK * SEGS
    tn = tile_of(width, 256)
    row_spec = pl.BlockSpec((1, width), lambda n, p: (0, 0))
    total_spec = pl.BlockSpec((peers, 2, width), lambda n, p: (0, 0, 0))
    return pl.pallas_call(
        functools.partial(bend_kernel, chunks, peers),
        out_shape=[
            jax.ShapeDtypeStruct((2, total_rows, width), F32),
            jax.ShapeDtypeStruct((2, segs, width), F32),
            jax.ShapeDtypeStruct((peers, 2, width), F32),
        ],
        grid_spec=pltpu.PrefetchScalarGridSpec(
            num_scalar_prefetch=1,
            grid=(width // tn,),
            in_specs=[pl.BlockSpec((2, g.shape[1], tn), lambda n, p: (0, 0, n)) for g in gates]
            + [pl.BlockSpec((2, m.shape[1], width), lambda n, p: (0, 0, 0)) for m in maps]
            + [total_spec, row_spec, row_spec],
            out_specs=[
                pl.BlockSpec((2, total_rows, tn), lambda n, p: (0, 0, n)),
                pl.BlockSpec((2, segs, width), lambda n, p: (0, 0, 0)),
                total_spec,
            ],
            scratch_shapes=[pltpu.VMEM((segs, width), F32)],
        ),
        compiler_params=params(16),
        cost_estimate=cost(
            40 * total_rows * width, 12 * total_rows * width, 5 * total_rows * width
        ),
        name="bend",
    )(place, *gates, *maps, peer_maps, gain, start)


def state_kernel(first_row, peers, place, run_ref, maps_ref, peer_ref, start_ref, out_ref, enter):
    rows = out_ref.shape[0]
    begin = first_row // BLOCK * SEGS
    state = entering_state(place, peer_ref, start_ref[...], peers)
    for k in range(begin + rows // BLOCK * SEGS):
        if k >= begin:
            enter[k - begin : k - begin + 1, :] = state
        state = maps_ref[0, k : k + 1, :] * state + maps_ref[1, k : k + 1, :]
    for c in range(rows // BLOCK):
        once = enter[c * SEGS : (c + 1) * SEGS, :]
        entered = jnp.concatenate([once, once], axis=0)

        def step(jj, carry):
            at = pl.multiple_of(c * BLOCK + jj * 2 * SEGS, 2 * SEGS)
            lines = pl.ds(at, 2 * SEGS)
            deep = pl.ds(pl.multiple_of(first_row + at, 2 * SEGS), 2 * SEGS)
            out_ref[lines, :] = (run_ref[0, deep, :] * entered + run_ref[1, deep, :]).astype(BF16)
            return carry

        lax.fori_loop(0, BLOCK // SEGS // 2, step, 0)


def state_chunk(place, run, maps, peer_maps, start, first_row, rows):
    width = run.shape[2]
    peers = peer_maps.shape[0]
    vmem = pl.BlockSpec(memory_space=pltpu.VMEM)
    return pl.pallas_call(
        functools.partial(state_kernel, first_row, peers),
        out_shape=jax.ShapeDtypeStruct((rows, width), BF16),
        in_specs=[pl.BlockSpec(memory_space=pltpu.SMEM)] + [vmem] * 4,
        out_specs=vmem,
        scratch_shapes=[pltpu.VMEM((rows // BLOCK * SEGS, width), F32)],
        compiler_params=params(16),
        cost_estimate=cost(2 * rows * width, 10 * rows * width),
    )(place, run, maps, peer_maps, start)


def mix_kernel(groups, group, cuts, peers, slots, final, before, place, *refs):
    count = groups * group
    blocks = refs[:count]
    starts = [sum(len(cut) for cut in cuts[:n]) for n in range(len(cuts) + 1)]
    weights = refs[count : count + starts[-1]]
    out_ref, lhs, wbuf, acc, lsem, wsem = refs[-6:]
    prev_refs = refs[count + len(weights) : count + len(weights) + before]
    depth = blocks[0].shape[1]
    heights = [blocks[c * group].shape[0] for c in range(groups)]
    outer = peers // 2
    here = len(slots) * 2

    def w_copy(n, p):
        w_ref = weights[starts[n] + p]
        top = sum(cuts[n][:p])
        dst = wbuf.at[n, top : top + cuts[n][p], :]
        return pltpu.make_async_copy(w_ref, dst, wsem.at[n, p])

    def l_copy(c, d):
        deep = pl.ds(pl.multiple_of((place[0] ^ d) * depth, depth), depth)
        top = sum(heights[:c])
        dst = lhs.at[top : top + heights[c], deep]
        return pltpu.make_async_copy(blocks[c * group + d], dst, lsem.at[c, d])

    for n in range(here):
        for p in range(len(cuts[n])):
            w_copy(n, p).start()
    for c in range(groups):
        for d in range(group):
            l_copy(c, d).start()
    for c in range(groups):
        for d in range(group):
            l_copy(c, d).wait()
    top = 0
    for prev in prev_refs:
        acc[top : top + prev.shape[0], :] = prev[...]
        top += prev.shape[0]
    span = wbuf.shape[1]
    for n in range(here):
        source = lax.rem(place[1] // 2 + outer - slots[n // 2], outer)
        owner = source * 2 + (lax.rem(place[1], 2) ^ (n % 2))
        deep = pl.ds(pl.multiple_of(owner * span, span), span)
        for p in range(len(cuts[n])):
            w_copy(n, p).wait()
        part = jnp.dot(lhs[:, deep], wbuf[n], preferred_element_type=F32)
        if n > 0 or before:
            part = acc[...] + part
        if n < here - 1:
            acc[...] = part
        elif not final:
            out_ref[...] = part
        else:
            acc[...] = part
            order = row_order(True)
            for m in range(acc.shape[0] // BLOCK):
                lines = slice(m * BLOCK, (m + 1) * BLOCK)
                rounded = acc[lines, :].astype(BF16)
                moved = jnp.dot(order, rounded, preferred_element_type=F32)
                out_ref[lines, :] = moved.astype(BF16)


def mix_rows(place, blocks, weights, slots, prev, final, whole, first, total_rows):
    groups, group = len(blocks), len(blocks[0])
    depth = blocks[0][0].shape[1]
    width = weights[0][0].shape[1]
    peers = len(weights)
    span = sum(piece.shape[0] for piece in weights[0])
    rows = sum(g[0].shape[0] for g in blocks)
    chosen = [weights[s * 2 + i] for s in slots for i in range(2)]
    cuts = tuple(tuple(piece.shape[0] for piece in pieces) for pieces in chosen)
    used = [piece for pieces in chosen for piece in pieces]
    most = max(len(cut) for cut in cuts)
    args = [place] + [b for g in blocks for b in g] + used
    in_specs = [pl.BlockSpec(memory_space=pl.ANY)] * (groups * group)
    in_specs += [pl.BlockSpec(memory_space=pltpu.HBM)] * len(used)
    args += prev
    in_specs += [pl.BlockSpec(memory_space=pltpu.VMEM)] * len(prev)
    aliases = {}
    if whole is not None:
        aliases = {len(args): 0}
        args.append(whole)
        in_specs.append(pl.BlockSpec(memory_space=pl.ANY))
    deep = len(slots) * 2 * span
    if final:
        out_shape = jax.ShapeDtypeStruct((total_rows, width), BF16)
        out_spec = pl.BlockSpec((rows, width), lambda n, p: (first // rows, 0))
    else:
        out_shape = jax.ShapeDtypeStruct((rows, width), F32)
        out_spec = pl.BlockSpec(memory_space=pltpu.VMEM)
    return pl.pallas_call(
        functools.partial(
            mix_kernel, groups, group, cuts, peers, tuple(slots), final, len(prev)
        ),
        out_shape=out_shape,
        grid_spec=pltpu.PrefetchScalarGridSpec(
            num_scalar_prefetch=1,
            grid=(1,),
            in_specs=in_specs,
            out_specs=out_spec,
            scratch_shapes=[
                pltpu.VMEM((rows, group * depth), BF16),
                pltpu.VMEM((len(slots) * 2, span, width), BF16),
                pltpu.VMEM((rows, width), F32),
                pltpu.SemaphoreType.DMA((groups, group)),
                pltpu.SemaphoreType.DMA((len(slots) * 2, most)),
            ],
        ),
        input_output_aliases=aliases,
        compiler_params=params(40 if peers <= 8 else 62),
        cost_estimate=cost(2 * rows * deep * width, 2 * deep * (width + rows) + 4 * rows * width),
    )(*args)


SHARES = (2, 1, 1)
RINGS_EARLY = 2
SWAPS_EARLY = 1


def cut_of(rows, shares):
    parts = [rows * share // sum(shares) for share in shares]
    return parts if min(parts) >= LANES else [rows]


def ring_cut(rows):
    return cut_of(rows, (1, 1))


def swap_cut(step, rows):
    return cut_of(rows, (1,) if step == 0 else (1, 1))


def recut(blocks, parts):
    if [b.shape[0] for b in blocks] == parts:
        return blocks
    (block,) = blocks
    tops = [sum(parts[:p]) for p in range(len(parts))]
    return [block[top : top + part] for top, part in zip(tops, parts)]


def behind(block, gate):
    return block if gate is None else lax.optimization_barrier((block, gate))[0]


def gather_early(w_output):
    peers = lax.axis_size("ctx")
    rows = w_output.shape[0]
    route = [(i, (i + 2) % peers) for i in range(peers)]
    held = {(0, 0): [w_output]}
    for step in range(1, RINGS_EARLY + 1):
        held[step, 0] = []
        for block in recut(held[step - 1, 0], ring_cut(rows)):
            held[step, 0].append(lax.ppermute(block, "ctx", route))
    for step in range(SWAPS_EARLY + 1):
        held[step, 1] = []
        for block in recut(held[step, 0], swap_cut(step, rows)):
            held[step, 1].append(swap(block, "ctx", 1))
    return held


def next_cuts(rows):
    return [ring_cut(rows), swap_cut(SWAPS_EARLY + 1, rows)]


def gather_late(held, following, late):
    peers = lax.axis_size("ctx")
    outer = peers // 2
    rows = held[0, 0][0].shape[0]
    route = [(i, (i + 2) % peers) for i in range(peers)]
    for step in range(RINGS_EARLY + 1, outer):
        held[step, 0] = []
        if step == RINGS_EARLY + 1:
            source = following[0]
        else:
            source = recut(held[step - 1, 0], ring_cut(rows))
        for p, block in enumerate(source):
            ahead = step == RINGS_EARLY + 1 and p < len(source) - 1
            gate = None if ahead else late
            held[step, 0].append(lax.ppermute(behind(block, gate), "ctx", route))
    for step in range(SWAPS_EARLY + 1, outer):
        held[step, 1] = []
        if step == SWAPS_EARLY + 1:
            source = following[1]
        else:
            source = recut(held[step, 0], swap_cut(step, rows))
        for p, block in enumerate(source):
            ahead = step == SWAPS_EARLY + 1 and p < len(source) - 1
            gate = None if ahead else late
            held[step, 1].append(swap(behind(block, gate), "ctx", 1))
    return [held[step, i] for step in range(outer) for i in range(2)]


def layer(tokens, w_input, w_output, bias_update, bias_cand, recur_gain, start_state):
    peers = lax.axis_size("ctx")
    group = lax.axis_size("ch")
    half = group // 2
    total_rows = tokens.shape[0]
    chunks = len(SHARES)
    sizes = [total_rows * share // sum(SHARES) for share in SHARES]
    firsts = [sum(sizes[:c]) for c in range(chunks)]
    place = jnp.stack([lax.axis_index("ch"), lax.axis_index("ctx")]).astype(jnp.int32)
    biases = jnp.stack([bias_update, bias_cand], axis=0)
    gain = recur_gain[None, :]
    start = start_state[None, :]

    ordered = split_rows(tokens, 0, sizes[:1], None)
    *others, whole = split_rows(tokens, sizes[0], sizes[1:], ordered[0])
    ordered = [*ordered, *others]
    far = []
    for piece in ordered:
        far.append([swap(piece, "ch", half)])
    near = [[whole]]
    for d in range(1, half):
        near.append([swap(whole, "ch", d)])
    for c in range(chunks):
        for d in range(1, half):
            far[c].append(swap(far[c][0], "ch", d))

    partial = near_product(place, near, w_input)
    gates, maps = [], []
    for c in range(chunks):
        last = c == chunks - 1
        out = gate_chunk(
            place,
            far[c],
            partial,
            w_input,
            biases,
            gain,
            start,
            maps if last else [],
            firsts[c],
            last,
            peers,
        )
        gates.append(out[0])
        maps.append(out[1])
    held = gather_early(w_output)
    following = [recut(held[RINGS_EARLY, 0], cut) for cut in next_cuts(w_output.shape[0])]
    ready = [len(pieces) - 1 for pieces in following]
    waiting = [pieces[n:] for pieces, n in zip(following, ready)]
    waiting, totals = lax.optimization_barrier((waiting, out[2]))
    following = [pieces[:n] + rest for pieces, n, rest in zip(following, ready, waiting)]
    first_maps = lax.all_to_all(totals, "ctx", 0, 0, tiled=True)
    run, run_maps, totals = bend_all(place, gates, maps, first_maps, gain, start)
    peer_maps = lax.all_to_all(totals, "ctx", 0, 0, tiled=True)
    weights = gather_late(held, following, peer_maps)

    blocks = []
    for c in range(chunks):
        own = state_chunk(place, run, run_maps, peer_maps, start, firsts[c], sizes[c])
        across = swap(own, "ch", half)
        blocks.append([own, across])
    for c in range(chunks):
        own, across = blocks[c]
        lows, highs = [own], [across]
        for d in range(1, half):
            lows.append(swap(own, "ch", d))
            highs.append(swap(across, "ch", d))
        blocks[c] = lows + highs
    outer = peers // 2
    late = max(1, outer // 4)
    slots = list(range(outer))

    def mix(part, used, prev, final, whole):
        return mix_rows(
            place,
            blocks[part],
            weights,
            used,
            prev,
            final,
            whole,
            firsts[part][0],
            total_rows,
        )

    early, late_slots = slots[:-late], slots[-late:]
    partials = [mix(slice(c, c + 1), early, [], False, None) for c in range(chunks - 1)]
    mixed = mix(slice(0, chunks - 1), late_slots, partials, True, None)
    mixed = mix(slice(chunks - 1, chunks), slots, [], True, mixed)
    return mixed


def solution(mesh):
    return jax.shard_map(
        layer,
        mesh=mesh,
        in_specs=(
            P("ctx", "ch"),
            P(None, None, "ch"),
            P("ctx", "ch"),
            P("ch"),
            P("ch"),
            P("ch"),
            P("ch"),
        ),
        out_specs=P("ctx", "ch"),
        check_vma=False,
    )
```

```python
import functools
import math

import jax
import jax.numpy as jnp
from jax import lax
from jax.experimental import pallas as pl
from jax.experimental.pallas import tpu as pltpu
from jax.sharding import PartitionSpec as P


SEGS = 8
LANES = 128
BLOCK = 256
F32 = jnp.float32
BF16 = jnp.bfloat16
MIB = 1024 * 1024


def swap(block, axis, bits):
    return lax.ppermute(block, axis, [(i, i ^ bits) for i in range(lax.axis_size(axis))])


def tile_of(width, most):
    return math.gcd(width, most)


def params(mib):
    return pltpu.CompilerParams(vmem_limit_bytes=mib * MIB)


def cost(flops, nbytes, trans=0):
    return pl.CostEstimate(flops=int(flops), bytes_accessed=int(nbytes), transcendentals=int(trans))


def near_kernel(half, tiles, heights, place, *refs):
    count = len(heights)
    blocks = refs[: half * count]
    w_ref, out_ref, lhs, wbuf, lsem, wsem = refs[half * count :]
    depth = blocks[0].shape[1]
    span = wbuf.shape[2]
    slot = lax.rem(place[0], half)
    base = (place[0] // half) * (half * depth)

    def w_copy(n):
        lines = pl.ds(pl.multiple_of(base, half * depth), half * depth)
        wide = pl.ds(pl.multiple_of(lax.rem(n, tiles) * span, span), span)
        return pltpu.make_async_copy(w_ref.at[n // tiles, lines, wide], wbuf.at[n], wsem.at[n])

    def l_copy(d, k):
        deep = pl.ds(pl.multiple_of((slot ^ d) * depth, depth), depth)
        top = sum(heights[:k])
        dst = lhs.at[top : top + heights[k], deep]
        return pltpu.make_async_copy(blocks[d * count + k], dst, lsem.at[d, k])

    steps = wbuf.shape[0]
    for n in range(steps):
        w_copy(n).start()
    for d in range(half):
        for k in range(count):
            l_copy(d, k).start()
    for d in range(half):
        for k in range(count):
            l_copy(d, k).wait()

    def body(n, carry):
        w_copy(n).wait()
        wide = pl.ds(pl.multiple_of(lax.rem(n, tiles) * span, span), span)
        total = None
        for d in range(half):
            deep = slice(d * depth, (d + 1) * depth)
            part = jnp.dot(lhs[:, deep], wbuf[n, deep, :], preferred_element_type=F32)
            total = part if total is None else total + part
        out_ref[n // tiles, :, wide] = total
        return carry

    lax.fori_loop(0, steps, body, 0)


def near_product(place, blocks, weights):
    half = len(blocks)
    heights = tuple(b.shape[0] for b in blocks[0])
    rows, depth = sum(heights), blocks[0][0].shape[1]
    gates, _, width = weights.shape
    span = tile_of(width, 512)
    tiles = width // span
    return pl.pallas_call(
        functools.partial(near_kernel, half, tiles, heights),
        out_shape=jax.ShapeDtypeStruct((gates, rows, width), F32),
        in_specs=[pl.BlockSpec(memory_space=pltpu.SMEM)]
        + [pl.BlockSpec(memory_space=pl.ANY)] * (half * len(heights))
        + [pl.BlockSpec(memory_space=pltpu.HBM)],
        out_specs=pl.BlockSpec(memory_space=pltpu.VMEM),
        scratch_shapes=[
            pltpu.VMEM((rows, half * depth), BF16),
            pltpu.VMEM((gates * tiles, half * depth, span), BF16),
            pltpu.SemaphoreType.DMA((half, len(heights))),
            pltpu.SemaphoreType.DMA((gates * tiles,)),
        ],
        compiler_params=params(28),
        cost_estimate=cost(
            2 * gates * rows * half * depth * width,
            gates * width * (half * depth * 2 + rows * 4) + half * rows * depth * 2,
        ),
    )(place, *[piece for block in blocks for piece in block], weights)


def row_order(transposed):
    shape = (BLOCK, BLOCK)
    row = lax.broadcasted_iota(jnp.int32, shape, 1 if transposed else 0)
    token = lax.broadcasted_iota(jnp.int32, shape, 0 if transposed else 1)
    chosen = lax.rem(row, SEGS) * (BLOCK // SEGS) + row // SEGS == token
    return jnp.where(chosen, 1.0, 0.0).astype(BF16)


def split_kernel(first, sizes, joined, src, *refs):
    count = len(sizes)
    if joined:
        head, refs = refs[0], refs[1:]
    outs = refs[:count]
    buf, sem, head_sem = refs[-3:]
    blocks = sum(sizes) // BLOCK
    copies = []
    for k in range(blocks):
        lines = pl.ds(first + k * BLOCK, BLOCK)
        copies.append(pltpu.make_async_copy(src.at[lines, :], buf.at[k], sem.at[k]))
    for copy in copies:
        copy.start()
    if joined:
        join = pltpu.make_async_copy(head, refs[count].at[0:first, :], head_sem)
        join.start()
    order = row_order(False)
    k = 0
    for c in range(count):
        for r in range(sizes[c] // BLOCK):
            copies[k].wait()
            moved = jnp.dot(order, buf[k], preferred_element_type=F32).astype(BF16)
            outs[c][r * BLOCK : (r + 1) * BLOCK, :] = moved
            if joined:
                refs[count][first + k * BLOCK : first + (k + 1) * BLOCK, :] = moved
            k += 1
    if joined:
        join.wait()


def split_rows(array, first, sizes, head):
    vmem = pl.BlockSpec(memory_space=pltpu.VMEM)
    rows, width = sum(sizes), array.shape[1]
    joined = head is not None
    shapes = list(sizes) + ([first + rows] if joined else [])
    args = [array] + ([head] if joined else [])
    return pl.pallas_call(
        functools.partial(split_kernel, first, tuple(sizes), joined),
        out_shape=[jax.ShapeDtypeStruct((r, width), array.dtype) for r in shapes],
        in_specs=[pl.BlockSpec(memory_space=pl.ANY)] * len(args),
        out_specs=[vmem] * len(shapes),
        scratch_shapes=[
            pltpu.VMEM((rows // BLOCK, BLOCK, width), BF16),
            pltpu.SemaphoreType.DMA((rows // BLOCK,)),
            pltpu.SemaphoreType.DMA,
        ],
        compiler_params=params(60),
        cost_estimate=cost(2 * rows * BLOCK * width, 4 * rows * width),
    )(*args)


def compose_rows(maps, count, a, b):
    for k in range(count):
        slope = maps[0, k : k + 1, :]
        shift = maps[1, k : k + 1, :]
        b = slope * b + shift
        a = slope * a
    return a, b


def first_slopes(pre, cand, gain):
    update = jax.nn.sigmoid(pre)
    keep = 1.0 - update
    scaled = update * gain
    squashed = jnp.tanh(cand)
    slope = keep + (scaled - scaled * squashed * squashed)
    return update, keep, scaled, slope, update * squashed


def lead_row(place, start, shape):
    lead = lax.broadcasted_iota(jnp.int32, shape, 0) == 0
    return jnp.where(lead & (place[1] == 0), start, 0.0)


def around(update, keep, scaled, cand, gain, prev):
    squashed = jnp.tanh(cand + gain * prev)
    bend = scaled - scaled * squashed * squashed
    return keep + bend, update * squashed - bend * prev


def gate_kernel(half, first_row, rows, before, last, place, *refs):
    blocks = refs[:half]
    part_ref, w_ref, bias_ref, gain_ref, start_ref = refs[half : half + 5]
    earlier = refs[half + 5 : half + 5 + before]
    rest = refs[half + 5 + before :]
    if last:
        gates_ref, maps_ref, total_ref = rest[:3]
    else:
        gates_ref, maps_ref = rest[:2]
    wbuf, acc, wsem = rest[-3:]
    depth = blocks[0].shape[1]
    width = gain_ref.shape[1]
    seg = BLOCK // SEGS
    count = rows // BLOCK
    lines_of = wbuf.shape[3]
    parts = depth // lines_of
    slot = lax.rem(place[0], half)
    base = ((place[0] // half) ^ 1) * (half * depth)

    def w_copy(g, d, q):
        top = base + (slot ^ d) * depth + q * lines_of
        lines = pl.ds(pl.multiple_of(top, lines_of), lines_of)
        return pltpu.make_async_copy(w_ref.at[g, lines, :], wbuf.at[g, d, q], wsem.at[g, d, q])

    every = [(d, q) for d in range(half) for q in range(parts)]
    for g in range(2):
        for d, q in every:
            w_copy(g, d, q).start()
    for g in range(2):
        for d, q in every:
            w_copy(g, d, q).wait()
            deep = slice(q * lines_of, (q + 1) * lines_of)
            part = jnp.dot(blocks[d][:, deep], wbuf[g, d, q], preferred_element_type=F32)
            if (d, q) == (0, 0):
                acc[g] = part
            else:
                acc[g] += part

    span = tile_of(width, 512)

    def columns(n, carry_out):
        wide = pl.ds(pl.multiple_of(n * span, span), span)
        gain = jnp.broadcast_to(gain_ref[:, wide], (SEGS, span))
        bias = [jnp.broadcast_to(bias_ref[g : g + 1, wide], (2 * SEGS, span)) for g in range(2)]

        def pair(jj, carry, first):
            out = []
            for c in range(count):
                a, b = carry[c]
                lines = pl.ds(pl.multiple_of(c * BLOCK + jj * 2 * SEGS, 2 * SEGS), 2 * SEGS)
                deep = pl.ds(
                    pl.multiple_of(first_row + c * BLOCK + jj * 2 * SEGS, 2 * SEGS), 2 * SEGS
                )
                held = []
                for g in range(2):
                    total = acc[g, lines, wide] + part_ref[g, deep, wide] + bias[g]
                    rounded = total.astype(BF16)
                    gates_ref[g, lines, wide] = rounded
                    held.append(rounded.astype(F32))
                for k in range(2):
                    pre = held[0][k * SEGS : (k + 1) * SEGS]
                    cand = held[1][k * SEGS : (k + 1) * SEGS]
                    update, keep, scaled, slope, offset = first_slopes(pre, cand, gain)
                    if first and k == 0 and c == 0:
                        prev = lead_row(place, start_ref[:, wide], (SEGS, span))
                        slope, offset = around(update, keep, scaled, cand, gain, prev)
                    b = slope * b + offset
                    a = slope * a
                out.append((a, b))
            return tuple(out)

        carry = ((jnp.ones((SEGS, span), F32), jnp.zeros((SEGS, span), F32)),) * count
        begin = 0
        if first_row == 0:
            carry = pair(0, carry, True)
            begin = 1
        carry = lax.fori_loop(begin, seg // 2, lambda jj, c: pair(jj, c, False), carry)
        for c in range(count):
            maps_ref[0, c * SEGS : (c + 1) * SEGS, wide] = carry[c][0]
            maps_ref[1, c * SEGS : (c + 1) * SEGS, wide] = carry[c][1]
        return carry_out

    lax.fori_loop(0, width // span, columns, 0)
    if last:
        ta, tb = jnp.ones((1, width), F32), jnp.zeros((1, width), F32)
        for maps in list(earlier) + [maps_ref]:
            ta, tb = compose_rows(maps, maps.shape[1], ta, tb)
        for i in range(total_ref.shape[0]):
            total_ref[i, 0:1, :] = ta
            total_ref[i, 1:2, :] = tb


def gate_chunk(place, blocks, partial, weights, biases, gain, start, earlier, first_row, last, peers):
    half = len(blocks)
    rows, depth = blocks[0].shape
    gates, _, width = weights.shape
    lines_of = tile_of(depth, 512)
    vmem = pl.BlockSpec(memory_space=pltpu.VMEM)
    out_shape = [
        jax.ShapeDtypeStruct((2, rows, width), BF16),
        jax.ShapeDtypeStruct((2, rows // BLOCK * SEGS, width), F32),
    ]
    if last:
        out_shape.append(jax.ShapeDtypeStruct((peers, 2, width), F32))
    return pl.pallas_call(
        functools.partial(gate_kernel, half, first_row, rows, len(earlier), last),
        out_shape=out_shape,
        in_specs=[pl.BlockSpec(memory_space=pltpu.SMEM)]
        + [vmem] * (half + 1)
        + [pl.BlockSpec(memory_space=pltpu.HBM)]
        + [vmem] * (3 + len(earlier)),
        out_specs=[vmem] * len(out_shape),
        scratch_shapes=[
            pltpu.VMEM((gates, half, depth // lines_of, lines_of, width), BF16),
            pltpu.VMEM((gates, rows, width), F32),
            pltpu.SemaphoreType.DMA((gates, half, depth // lines_of)),
        ],
        compiler_params=params(32),
        cost_estimate=cost(
            2 * gates * rows * half * depth * width,
            gates * width * (half * depth * 2 + rows * 6) + half * rows * depth * 2,
            4 * rows * width,
        ),
    )(place, *blocks, partial, weights, biases, gain, start, *earlier)


def entering_state(place, peer_maps, start, peers):
    state = start
    for k in range(peers):
        moved = peer_maps[k, 0:1, :] * state + peer_maps[k, 1:2, :]
        state = jnp.where(place[1] > k, moved, state)
    return state


def enter_segments(maps_list, state, enter):
    row = 0
    for maps in maps_list:
        for k in range(maps.shape[1]):
            enter[row : row + 1, :] = state
            state = maps[0, k : k + 1, :] * state + maps[1, k : k + 1, :]
            row += 1


def bend_kernel(chunks, peers, place, *refs):
    gates = refs[:chunks]
    maps = refs[chunks : 2 * chunks]
    peer_ref, gain_ref, start_ref, run_ref, maps_ref, total_ref, enter = refs[2 * chunks :]
    span = gates[0].shape[2]
    width = gain_ref.shape[1]
    where = [(c, r * BLOCK) for c in range(chunks) for r in range(gates[c].shape[1] // BLOCK)]
    n = pl.program_id(0)

    @pl.when(n == 0)
    def _():
        enter_segments(maps, entering_state(place, peer_ref, start_ref[...], peers), enter)

    wide = pl.ds(pl.multiple_of(n * span, span), span)
    gain = jnp.broadcast_to(gain_ref[:, wide], (SEGS, span))

    def advance(block, jj, held, first):
        state, a, b = held
        c, top = where[block]
        lines = pl.ds(pl.multiple_of(top + jj * 2 * SEGS, 2 * SEGS), 2 * SEGS)
        pre2 = gates[c][0, lines, :].astype(F32)
        cand2 = gates[c][1, lines, :].astype(F32)
        for k in range(2):
            pre = pre2[k * SEGS : (k + 1) * SEGS]
            cand = cand2[k * SEGS : (k + 1) * SEGS]
            update, keep, scaled, slope, offset = first_slopes(pre, cand, gain)
            if first and k == 0 and block == 0:
                prev = lead_row(place, start_ref[:, wide], (SEGS, span))
                slope, offset = around(update, keep, scaled, cand, gain, prev)
            slope2, offset2 = around(update, keep, scaled, cand, gain, state)
            state = slope * state + offset
            b = slope2 * b + offset2
            a = slope2 * a
            row = pl.ds(pl.multiple_of(block * BLOCK + (2 * jj + k) * SEGS, SEGS), SEGS)
            run_ref[0, row, :] = a
            run_ref[1, row, :] = b
        return state, a, b

    def pair(jj, carry, first):
        return tuple(advance(m, jj, carry[m], first) for m in range(len(where)))

    one, zero = jnp.ones((SEGS, span), F32), jnp.zeros((SEGS, span), F32)
    carry = tuple((enter[m * SEGS : (m + 1) * SEGS, wide], one, zero) for m in range(len(where)))
    carry = pair(0, carry, True)
    carry = lax.fori_loop(1, BLOCK // SEGS // 2, lambda jj, c: pair(jj, c, False), carry)
    for m in range(len(where)):
        maps_ref[0, m * SEGS : (m + 1) * SEGS, wide] = carry[m][1]
        maps_ref[1, m * SEGS : (m + 1) * SEGS, wide] = carry[m][2]

    @pl.when(n == pl.num_programs(0) - 1)
    def _():
        ta, tb = jnp.ones((1, width), F32), jnp.zeros((1, width), F32)
        ta, tb = compose_rows(maps_ref, maps_ref.shape[1], ta, tb)
        for i in range(peers):
            total_ref[i, 0:1, :] = ta
            total_ref[i, 1:2, :] = tb


def bend_all(place, gates, maps, peer_maps, gain, start):
    chunks = len(gates)
    peers = peer_maps.shape[0]
    width = gates[0].shape[2]
    total_rows = sum(g.shape[1] for g in gates)
    segs = total_rows // BLOCK * SEGS
    tn = tile_of(width, 256)
    row_spec = pl.BlockSpec((1, width), lambda n, p: (0, 0))
    total_spec = pl.BlockSpec((peers, 2, width), lambda n, p: (0, 0, 0))
    return pl.pallas_call(
        functools.partial(bend_kernel, chunks, peers),
        out_shape=[
            jax.ShapeDtypeStruct((2, total_rows, width), F32),
            jax.ShapeDtypeStruct((2, segs, width), F32),
            jax.ShapeDtypeStruct((peers, 2, width), F32),
        ],
        grid_spec=pltpu.PrefetchScalarGridSpec(
            num_scalar_prefetch=1,
            grid=(width // tn,),
            in_specs=[pl.BlockSpec((2, g.shape[1], tn), lambda n, p: (0, 0, n)) for g in gates]
            + [pl.BlockSpec((2, m.shape[1], width), lambda n, p: (0, 0, 0)) for m in maps]
            + [total_spec, row_spec, row_spec],
            out_specs=[
                pl.BlockSpec((2, total_rows, tn), lambda n, p: (0, 0, n)),
                pl.BlockSpec((2, segs, width), lambda n, p: (0, 0, 0)),
                total_spec,
            ],
            scratch_shapes=[pltpu.VMEM((segs, width), F32)],
        ),
        compiler_params=params(16),
        cost_estimate=cost(
            40 * total_rows * width, 12 * total_rows * width, 5 * total_rows * width
        ),
        name="bend",
    )(place, *gates, *maps, peer_maps, gain, start)


def state_kernel(first_row, peers, place, run_ref, maps_ref, peer_ref, start_ref, out_ref, enter):
    rows = out_ref.shape[0]
    begin = first_row // BLOCK * SEGS
    state = entering_state(place, peer_ref, start_ref[...], peers)
    for k in range(begin + rows // BLOCK * SEGS):
        if k >= begin:
            enter[k - begin : k - begin + 1, :] = state
        state = maps_ref[0, k : k + 1, :] * state + maps_ref[1, k : k + 1, :]
    for c in range(rows // BLOCK):
        once = enter[c * SEGS : (c + 1) * SEGS, :]
        entered = jnp.concatenate([once, once], axis=0)

        def step(jj, carry):
            at = pl.multiple_of(c * BLOCK + jj * 2 * SEGS, 2 * SEGS)
            lines = pl.ds(at, 2 * SEGS)
            deep = pl.ds(pl.multiple_of(first_row + at, 2 * SEGS), 2 * SEGS)
            out_ref[lines, :] = (run_ref[0, deep, :] * entered + run_ref[1, deep, :]).astype(BF16)
            return carry

        lax.fori_loop(0, BLOCK // SEGS // 2, step, 0)


def state_chunk(place, run, maps, peer_maps, start, first_row, rows):
    width = run.shape[2]
    peers = peer_maps.shape[0]
    vmem = pl.BlockSpec(memory_space=pltpu.VMEM)
    return pl.pallas_call(
        functools.partial(state_kernel, first_row, peers),
        out_shape=jax.ShapeDtypeStruct((rows, width), BF16),
        in_specs=[pl.BlockSpec(memory_space=pltpu.SMEM)] + [vmem] * 4,
        out_specs=vmem,
        scratch_shapes=[pltpu.VMEM((rows // BLOCK * SEGS, width), F32)],
        compiler_params=params(16),
        cost_estimate=cost(2 * rows * width, 10 * rows * width),
    )(place, run, maps, peer_maps, start)


def mix_kernel(groups, group, cuts, peers, slots, final, before, place, *refs):
    count = groups * group
    blocks = refs[:count]
    starts = [sum(len(cut) for cut in cuts[:n]) for n in range(len(cuts) + 1)]
    weights = refs[count : count + starts[-1]]
    out_ref, lhs, wbuf, acc, lsem, wsem = refs[-6:]
    prev_refs = refs[count + len(weights) : count + len(weights) + before]
    depth = blocks[0].shape[1]
    heights = [blocks[c * group].shape[0] for c in range(groups)]
    outer = peers // 2
    here = len(slots) * 2

    def w_copy(n, p):
        w_ref = weights[starts[n] + p]
        top = sum(cuts[n][:p])
        dst = wbuf.at[n, top : top + cuts[n][p], :]
        return pltpu.make_async_copy(w_ref, dst, wsem.at[n, p])

    def l_copy(c, d):
        deep = pl.ds(pl.multiple_of((place[0] ^ d) * depth, depth), depth)
        top = sum(heights[:c])
        dst = lhs.at[top : top + heights[c], deep]
        return pltpu.make_async_copy(blocks[c * group + d], dst, lsem.at[c, d])

    for n in range(here):
        for p in range(len(cuts[n])):
            w_copy(n, p).start()
    for c in range(groups):
        for d in range(group):
            l_copy(c, d).start()
    for c in range(groups):
        for d in range(group):
            l_copy(c, d).wait()
    top = 0
    for prev in prev_refs:
        acc[top : top + prev.shape[0], :] = prev[...]
        top += prev.shape[0]
    span = wbuf.shape[1]
    for n in range(here):
        source = lax.rem(place[1] // 2 + outer - slots[n // 2], outer)
        owner = source * 2 + (lax.rem(place[1], 2) ^ (n % 2))
        deep = pl.ds(pl.multiple_of(owner * span, span), span)
        for p in range(len(cuts[n])):
            w_copy(n, p).wait()
        part = jnp.dot(lhs[:, deep], wbuf[n], preferred_element_type=F32)
        if n > 0 or before:
            part = acc[...] + part
        if n < here - 1:
            acc[...] = part
        elif not final:
            out_ref[...] = part
        else:
            acc[...] = part
            order = row_order(True)
            for m in range(acc.shape[0] // BLOCK):
                lines = slice(m * BLOCK, (m + 1) * BLOCK)
                rounded = acc[lines, :].astype(BF16)
                moved = jnp.dot(order, rounded, preferred_element_type=F32)
                out_ref[lines, :] = moved.astype(BF16)


def mix_rows(place, blocks, weights, slots, prev, final, whole, first, total_rows):
    groups, group = len(blocks), len(blocks[0])
    depth = blocks[0][0].shape[1]
    width = weights[0][0].shape[1]
    peers = len(weights)
    span = sum(piece.shape[0] for piece in weights[0])
    rows = sum(g[0].shape[0] for g in blocks)
    chosen = [weights[s * 2 + i] for s in slots for i in range(2)]
    cuts = tuple(tuple(piece.shape[0] for piece in pieces) for pieces in chosen)
    used = [piece for pieces in chosen for piece in pieces]
    most = max(len(cut) for cut in cuts)
    args = [place] + [b for g in blocks for b in g] + used
    in_specs = [pl.BlockSpec(memory_space=pl.ANY)] * (groups * group)
    in_specs += [pl.BlockSpec(memory_space=pltpu.HBM)] * len(used)
    args += prev
    in_specs += [pl.BlockSpec(memory_space=pltpu.VMEM)] * len(prev)
    aliases = {}
    if whole is not None:
        aliases = {len(args): 0}
        args.append(whole)
        in_specs.append(pl.BlockSpec(memory_space=pl.ANY))
    deep = len(slots) * 2 * span
    if final:
        out_shape = jax.ShapeDtypeStruct((total_rows, width), BF16)
        out_spec = pl.BlockSpec((rows, width), lambda n, p: (first // rows, 0))
    else:
        out_shape = jax.ShapeDtypeStruct((rows, width), F32)
        out_spec = pl.BlockSpec(memory_space=pltpu.VMEM)
    return pl.pallas_call(
        functools.partial(
            mix_kernel, groups, group, cuts, peers, tuple(slots), final, len(prev)
        ),
        out_shape=out_shape,
        grid_spec=pltpu.PrefetchScalarGridSpec(
            num_scalar_prefetch=1,
            grid=(1,),
            in_specs=in_specs,
            out_specs=out_spec,
            scratch_shapes=[
                pltpu.VMEM((rows, group * depth), BF16),
                pltpu.VMEM((len(slots) * 2, span, width), BF16),
                pltpu.VMEM((rows, width), F32),
                pltpu.SemaphoreType.DMA((groups, group)),
                pltpu.SemaphoreType.DMA((len(slots) * 2, most)),
            ],
        ),
        input_output_aliases=aliases,
        compiler_params=params(40 if peers <= 8 else 62),
        cost_estimate=cost(2 * rows * deep * width, 2 * deep * (width + rows) + 4 * rows * width),
    )(*args)


SHARES = (2, 1, 1)
RINGS_EARLY = 2
SWAPS_EARLY = 1


def cut_of(rows, shares):
    parts = [rows * share // sum(shares) for share in shares]
    return parts if min(parts) >= LANES else [rows]


def ring_cut(rows):
    return cut_of(rows, (1, 1))


def swap_cut(step, rows):
    return cut_of(rows, (1,) if step == 0 else (1, 1))


def recut(blocks, parts):
    if [b.shape[0] for b in blocks] == parts:
        return blocks
    (block,) = blocks
    tops = [sum(parts[:p]) for p in range(len(parts))]
    return [block[top : top + part] for top, part in zip(tops, parts)]


def behind(block, gate):
    return block if gate is None else lax.optimization_barrier((block, gate))[0]


def gather_early(w_output):
    peers = lax.axis_size("ctx")
    rows = w_output.shape[0]
    route = [(i, (i + 2) % peers) for i in range(peers)]
    held = {(0, 0): [w_output]}
    for step in range(1, RINGS_EARLY + 1):
        held[step, 0] = []
        for block in recut(held[step - 1, 0], ring_cut(rows)):
            held[step, 0].append(lax.ppermute(block, "ctx", route))
    for step in range(SWAPS_EARLY + 1):
        held[step, 1] = []
        for block in recut(held[step, 0], swap_cut(step, rows)):
            held[step, 1].append(swap(block, "ctx", 1))
    return held


def next_cuts(rows):
    return [ring_cut(rows), swap_cut(SWAPS_EARLY + 1, rows)]


def gather_late(held, following, middle, late):
    peers = lax.axis_size("ctx")
    outer = peers // 2
    rows = held[0, 0][0].shape[0]
    route = [(i, (i + 2) % peers) for i in range(peers)]
    for step in range(RINGS_EARLY + 1, outer):
        held[step, 0] = []
        if step == RINGS_EARLY + 1:
            source = following[0]
        else:
            source = recut(held[step - 1, 0], ring_cut(rows))
        for block in source:
            held[step, 0].append(lax.ppermute(behind(block, late), "ctx", route))
    for step in range(SWAPS_EARLY + 1, outer):
        held[step, 1] = []
        if step == SWAPS_EARLY + 1:
            source = following[1]
        else:
            source = recut(held[step, 0], swap_cut(step, rows))
        for p, block in enumerate(source):
            ahead = step == SWAPS_EARLY + 1 and p < len(source) - 1
            gate = middle if ahead else late
            held[step, 1].append(swap(behind(block, gate), "ctx", 1))
    return [held[step, i] for step in range(outer) for i in range(2)]


def layer(tokens, w_input, w_output, bias_update, bias_cand, recur_gain, start_state):
    peers = lax.axis_size("ctx")
    group = lax.axis_size("ch")
    half = group // 2
    total_rows = tokens.shape[0]
    chunks = len(SHARES)
    sizes = [total_rows * share // sum(SHARES) for share in SHARES]
    firsts = [sum(sizes[:c]) for c in range(chunks)]
    place = jnp.stack([lax.axis_index("ch"), lax.axis_index("ctx")]).astype(jnp.int32)
    biases = jnp.stack([bias_update, bias_cand], axis=0)
    gain = recur_gain[None, :]
    start = start_state[None, :]

    ordered = split_rows(tokens, 0, sizes[:1], None)
    *others, whole = split_rows(tokens, sizes[0], sizes[1:], ordered[0])
    ordered = [*ordered, *others]
    far = []
    for piece in ordered:
        far.append([swap(piece, "ch", half)])
    near = [[whole]]
    for d in range(1, half):
        near.append([swap(whole, "ch", d)])
    for c in range(chunks):
        for d in range(1, half):
            far[c].append(swap(far[c][0], "ch", d))

    partial = near_product(place, near, w_input)
    gates, maps = [], []
    for c in range(chunks):
        last = c == chunks - 1
        out = gate_chunk(
            place,
            far[c],
            partial,
            w_input,
            biases,
            gain,
            start,
            maps if last else [],
            firsts[c],
            last,
            peers,
        )
        gates.append(out[0])
        maps.append(out[1])
    held = gather_early(w_output)
    following = [recut(held[RINGS_EARLY, 0], cut) for cut in next_cuts(w_output.shape[0])]
    following, totals = lax.optimization_barrier((following, out[2]))
    first_maps = lax.all_to_all(totals, "ctx", 0, 0, tiled=True)
    run, run_maps, totals = bend_all(place, gates, maps, first_maps, gain, start)
    peer_maps = lax.all_to_all(totals, "ctx", 0, 0, tiled=True)
    weights = gather_late(held, following, first_maps, peer_maps)

    blocks = []
    for c in range(chunks):
        own = state_chunk(place, run, run_maps, peer_maps, start, firsts[c], sizes[c])
        across = swap(own, "ch", half)
        blocks.append([own, across])
    for c in range(chunks):
        own, across = blocks[c]
        lows, highs = [own], [across]
        for d in range(1, half):
            lows.append(swap(own, "ch", d))
            highs.append(swap(across, "ch", d))
        blocks[c] = lows + highs
    outer = peers // 2
    late = max(1, outer // 4)
    slots = list(range(outer))

    def mix(part, used, prev, final, whole):
        return mix_rows(
            place,
            blocks[part],
            weights,
            used,
            prev,
            final,
            whole,
            firsts[part][0],
            total_rows,
        )

    early, late_slots = slots[:-late], slots[-late:]
    partials = [mix(slice(c, c + 1), early, [], False, None) for c in range(chunks - 1)]
    mixed = mix(slice(0, chunks - 1), late_slots, partials, True, None)
    mixed = mix(slice(chunks - 1, chunks), slots, [], True, mixed)
    return mixed


def solution(mesh):
    return jax.shard_map(
        layer,
        mesh=mesh,
        in_specs=(
            P("ctx", "ch"),
            P(None, None, "ch"),
            P("ctx", "ch"),
            P("ch"),
            P("ch"),
            P("ch"),
            P("ch"),
        ),
        out_specs=P("ctx", "ch"),
        check_vma=False,
    )
```

```python
import functools
import math

import jax
import jax.numpy as jnp
from jax import lax
from jax.experimental import pallas as pl
from jax.experimental.pallas import tpu as pltpu
from jax.sharding import PartitionSpec as P


SEGS = 8
LANES = 128
BLOCK = 256
F32 = jnp.float32
BF16 = jnp.bfloat16
MIB = 1024 * 1024


def swap(block, axis, bits):
    return lax.ppermute(block, axis, [(i, i ^ bits) for i in range(lax.axis_size(axis))])


def tile_of(width, most):
    return math.gcd(width, most)


def params(mib):
    return pltpu.CompilerParams(vmem_limit_bytes=mib * MIB)


def cost(flops, nbytes, trans=0):
    return pl.CostEstimate(flops=int(flops), bytes_accessed=int(nbytes), transcendentals=int(trans))


def near_kernel(half, tiles, heights, place, *refs):
    count = len(heights)
    blocks = refs[: half * count]
    w_ref, out_ref, lhs, wbuf, lsem, wsem = refs[half * count :]
    depth = blocks[0].shape[1]
    span = wbuf.shape[2]
    slot = lax.rem(place[0], half)
    base = (place[0] // half) * (half * depth)

    def w_copy(n):
        lines = pl.ds(pl.multiple_of(base, half * depth), half * depth)
        wide = pl.ds(pl.multiple_of(lax.rem(n, tiles) * span, span), span)
        return pltpu.make_async_copy(w_ref.at[n // tiles, lines, wide], wbuf.at[n], wsem.at[n])

    def l_copy(d, k):
        deep = pl.ds(pl.multiple_of((slot ^ d) * depth, depth), depth)
        top = sum(heights[:k])
        dst = lhs.at[top : top + heights[k], deep]
        return pltpu.make_async_copy(blocks[d * count + k], dst, lsem.at[d, k])

    steps = wbuf.shape[0]
    for n in range(steps):
        w_copy(n).start()
    for d in range(half):
        for k in range(count):
            l_copy(d, k).start()
    for d in range(half):
        for k in range(count):
            l_copy(d, k).wait()

    def body(n, carry):
        w_copy(n).wait()
        wide = pl.ds(pl.multiple_of(lax.rem(n, tiles) * span, span), span)
        total = None
        for d in range(half):
            deep = slice(d * depth, (d + 1) * depth)
            part = jnp.dot(lhs[:, deep], wbuf[n, deep, :], preferred_element_type=F32)
            total = part if total is None else total + part
        out_ref[n // tiles, :, wide] = total
        return carry

    lax.fori_loop(0, steps, body, 0)


def near_product(place, blocks, weights):
    half = len(blocks)
    heights = tuple(b.shape[0] for b in blocks[0])
    rows, depth = sum(heights), blocks[0][0].shape[1]
    gates, _, width = weights.shape
    span = tile_of(width, 512)
    tiles = width // span
    return pl.pallas_call(
        functools.partial(near_kernel, half, tiles, heights),
        out_shape=jax.ShapeDtypeStruct((gates, rows, width), F32),
        in_specs=[pl.BlockSpec(memory_space=pltpu.SMEM)]
        + [pl.BlockSpec(memory_space=pl.ANY)] * (half * len(heights))
        + [pl.BlockSpec(memory_space=pltpu.HBM)],
        out_specs=pl.BlockSpec(memory_space=pltpu.VMEM),
        scratch_shapes=[
            pltpu.VMEM((rows, half * depth), BF16),
            pltpu.VMEM((gates * tiles, half * depth, span), BF16),
            pltpu.SemaphoreType.DMA((half, len(heights))),
            pltpu.SemaphoreType.DMA((gates * tiles,)),
        ],
        compiler_params=params(28),
        cost_estimate=cost(
            2 * gates * rows * half * depth * width,
            gates * width * (half * depth * 2 + rows * 4) + half * rows * depth * 2,
        ),
    )(place, *[piece for block in blocks for piece in block], weights)


def row_order(transposed):
    shape = (BLOCK, BLOCK)
    row = lax.broadcasted_iota(jnp.int32, shape, 1 if transposed else 0)
    token = lax.broadcasted_iota(jnp.int32, shape, 0 if transposed else 1)
    chosen = lax.rem(row, SEGS) * (BLOCK // SEGS) + row // SEGS == token
    return jnp.where(chosen, 1.0, 0.0).astype(BF16)


def split_kernel(first, sizes, joined, src, *refs):
    count = len(sizes)
    if joined:
        head, refs = refs[0], refs[1:]
    outs = refs[:count]
    buf, sem, head_sem = refs[-3:]
    blocks = sum(sizes) // BLOCK
    copies = []
    for k in range(blocks):
        lines = pl.ds(first + k * BLOCK, BLOCK)
        copies.append(pltpu.make_async_copy(src.at[lines, :], buf.at[k], sem.at[k]))
    for copy in copies:
        copy.start()
    if joined:
        join = pltpu.make_async_copy(head, refs[count].at[0:first, :], head_sem)
        join.start()
    order = row_order(False)
    k = 0
    for c in range(count):
        for r in range(sizes[c] // BLOCK):
            copies[k].wait()
            moved = jnp.dot(order, buf[k], preferred_element_type=F32).astype(BF16)
            outs[c][r * BLOCK : (r + 1) * BLOCK, :] = moved
            if joined:
                refs[count][first + k * BLOCK : first + (k + 1) * BLOCK, :] = moved
            k += 1
    if joined:
        join.wait()


def split_rows(array, first, sizes, head):
    vmem = pl.BlockSpec(memory_space=pltpu.VMEM)
    rows, width = sum(sizes), array.shape[1]
    joined = head is not None
    shapes = list(sizes) + ([first + rows] if joined else [])
    args = [array] + ([head] if joined else [])
    return pl.pallas_call(
        functools.partial(split_kernel, first, tuple(sizes), joined),
        out_shape=[jax.ShapeDtypeStruct((r, width), array.dtype) for r in shapes],
        in_specs=[pl.BlockSpec(memory_space=pl.ANY)] * len(args),
        out_specs=[vmem] * len(shapes),
        scratch_shapes=[
            pltpu.VMEM((rows // BLOCK, BLOCK, width), BF16),
            pltpu.SemaphoreType.DMA((rows // BLOCK,)),
            pltpu.SemaphoreType.DMA,
        ],
        compiler_params=params(60),
        cost_estimate=cost(2 * rows * BLOCK * width, 4 * rows * width),
    )(*args)


def compose_rows(maps, count, a, b):
    for k in range(count):
        slope = maps[0, k : k + 1, :]
        shift = maps[1, k : k + 1, :]
        b = slope * b + shift
        a = slope * a
    return a, b


def first_slopes(pre, cand, gain):
    update = jax.nn.sigmoid(pre)
    keep = 1.0 - update
    scaled = update * gain
    squashed = jnp.tanh(cand)
    slope = keep + (scaled - scaled * squashed * squashed)
    return update, keep, scaled, slope, update * squashed


def lead_row(place, start, shape):
    lead = lax.broadcasted_iota(jnp.int32, shape, 0) == 0
    return jnp.where(lead & (place[1] == 0), start, 0.0)


def around(update, keep, scaled, cand, gain, prev):
    squashed = jnp.tanh(cand + gain * prev)
    bend = scaled - scaled * squashed * squashed
    return keep + bend, update * squashed - bend * prev


def gate_kernel(half, first_row, rows, before, last, place, *refs):
    blocks = refs[:half]
    part_ref, w_ref, bias_ref, gain_ref, start_ref = refs[half : half + 5]
    earlier = refs[half + 5 : half + 5 + before]
    rest = refs[half + 5 + before :]
    if last:
        gates_ref, maps_ref, total_ref = rest[:3]
    else:
        gates_ref, maps_ref = rest[:2]
    wbuf, acc, wsem = rest[-3:]
    depth = blocks[0].shape[1]
    width = gain_ref.shape[1]
    seg = BLOCK // SEGS
    count = rows // BLOCK
    lines_of = wbuf.shape[3]
    parts = depth // lines_of
    slot = lax.rem(place[0], half)
    base = ((place[0] // half) ^ 1) * (half * depth)

    def w_copy(g, d, q):
        top = base + (slot ^ d) * depth + q * lines_of
        lines = pl.ds(pl.multiple_of(top, lines_of), lines_of)
        return pltpu.make_async_copy(w_ref.at[g, lines, :], wbuf.at[g, d, q], wsem.at[g, d, q])

    every = [(d, q) for d in range(half) for q in range(parts)]
    for g in range(2):
        for d, q in every:
            w_copy(g, d, q).start()
    for g in range(2):
        for d, q in every:
            w_copy(g, d, q).wait()
            deep = slice(q * lines_of, (q + 1) * lines_of)
            part = jnp.dot(blocks[d][:, deep], wbuf[g, d, q], preferred_element_type=F32)
            if (d, q) == (0, 0):
                acc[g] = part
            else:
                acc[g] += part

    span = tile_of(width, 512)

    def columns(n, carry_out):
        wide = pl.ds(pl.multiple_of(n * span, span), span)
        gain = jnp.broadcast_to(gain_ref[:, wide], (SEGS, span))
        bias = [jnp.broadcast_to(bias_ref[g : g + 1, wide], (2 * SEGS, span)) for g in range(2)]

        def pair(jj, carry, first):
            out = []
            for c in range(count):
                a, b = carry[c]
                lines = pl.ds(pl.multiple_of(c * BLOCK + jj * 2 * SEGS, 2 * SEGS), 2 * SEGS)
                deep = pl.ds(
                    pl.multiple_of(first_row + c * BLOCK + jj * 2 * SEGS, 2 * SEGS), 2 * SEGS
                )
                held = []
                for g in range(2):
                    total = acc[g, lines, wide] + part_ref[g, deep, wide] + bias[g]
                    rounded = total.astype(BF16)
                    gates_ref[g, lines, wide] = rounded
                    held.append(rounded.astype(F32))
                for k in range(2):
                    pre = held[0][k * SEGS : (k + 1) * SEGS]
                    cand = held[1][k * SEGS : (k + 1) * SEGS]
                    update, keep, scaled, slope, offset = first_slopes(pre, cand, gain)
                    if first and k == 0 and c == 0:
                        prev = lead_row(place, start_ref[:, wide], (SEGS, span))
                        slope, offset = around(update, keep, scaled, cand, gain, prev)
                    b = slope * b + offset
                    a = slope * a
                out.append((a, b))
            return tuple(out)

        carry = ((jnp.ones((SEGS, span), F32), jnp.zeros((SEGS, span), F32)),) * count
        begin = 0
        if first_row == 0:
            carry = pair(0, carry, True)
            begin = 1
        carry = lax.fori_loop(begin, seg // 2, lambda jj, c: pair(jj, c, False), carry)
        for c in range(count):
            maps_ref[0, c * SEGS : (c + 1) * SEGS, wide] = carry[c][0]
            maps_ref[1, c * SEGS : (c + 1) * SEGS, wide] = carry[c][1]
        return carry_out

    lax.fori_loop(0, width // span, columns, 0)
    if last:
        ta, tb = jnp.ones((1, width), F32), jnp.zeros((1, width), F32)
        for maps in list(earlier) + [maps_ref]:
            ta, tb = compose_rows(maps, maps.shape[1], ta, tb)
        for i in range(total_ref.shape[0]):
            total_ref[i, 0:1, :] = ta
            total_ref[i, 1:2, :] = tb


def gate_chunk(place, blocks, partial, weights, biases, gain, start, earlier, first_row, last, peers):
    half = len(blocks)
    rows, depth = blocks[0].shape
    gates, _, width = weights.shape
    lines_of = tile_of(depth, 512)
    vmem = pl.BlockSpec(memory_space=pltpu.VMEM)
    out_shape = [
        jax.ShapeDtypeStruct((2, rows, width), BF16),
        jax.ShapeDtypeStruct((2, rows // BLOCK * SEGS, width), F32),
    ]
    if last:
        out_shape.append(jax.ShapeDtypeStruct((peers, 2, width), F32))
    return pl.pallas_call(
        functools.partial(gate_kernel, half, first_row, rows, len(earlier), last),
        out_shape=out_shape,
        in_specs=[pl.BlockSpec(memory_space=pltpu.SMEM)]
        + [vmem] * (half + 1)
        + [pl.BlockSpec(memory_space=pltpu.HBM)]
        + [vmem] * (3 + len(earlier)),
        out_specs=[vmem] * len(out_shape),
        scratch_shapes=[
            pltpu.VMEM((gates, half, depth // lines_of, lines_of, width), BF16),
            pltpu.VMEM((gates, rows, width), F32),
            pltpu.SemaphoreType.DMA((gates, half, depth // lines_of)),
        ],
        compiler_params=params(32),
        cost_estimate=cost(
            2 * gates * rows * half * depth * width,
            gates * width * (half * depth * 2 + rows * 6) + half * rows * depth * 2,
            4 * rows * width,
        ),
    )(place, *blocks, partial, weights, biases, gain, start, *earlier)


def entering_state(place, peer_maps, start, peers):
    state = start
    for k in range(peers):
        moved = peer_maps[k, 0:1, :] * state + peer_maps[k, 1:2, :]
        state = jnp.where(place[1] > k, moved, state)
    return state


def enter_segments(maps_list, state, enter):
    row = 0
    for maps in maps_list:
        for k in range(maps.shape[1]):
            enter[row : row + 1, :] = state
            state = maps[0, k : k + 1, :] * state + maps[1, k : k + 1, :]
            row += 1


def bend_kernel(chunks, peers, place, *refs):
    gates = refs[:chunks]
    maps = refs[chunks : 2 * chunks]
    peer_ref, gain_ref, start_ref, run_ref, maps_ref, total_ref, enter = refs[2 * chunks :]
    span = gates[0].shape[2]
    width = gain_ref.shape[1]
    where = [(c, r * BLOCK) for c in range(chunks) for r in range(gates[c].shape[1] // BLOCK)]
    n = pl.program_id(0)

    @pl.when(n == 0)
    def _():
        enter_segments(maps, entering_state(place, peer_ref, start_ref[...], peers), enter)

    wide = pl.ds(pl.multiple_of(n * span, span), span)
    gain = jnp.broadcast_to(gain_ref[:, wide], (SEGS, span))

    def advance(block, jj, held, first):
        state, a, b = held
        c, top = where[block]
        lines = pl.ds(pl.multiple_of(top + jj * 2 * SEGS, 2 * SEGS), 2 * SEGS)
        pre2 = gates[c][0, lines, :].astype(F32)
        cand2 = gates[c][1, lines, :].astype(F32)
        for k in range(2):
            pre = pre2[k * SEGS : (k + 1) * SEGS]
            cand = cand2[k * SEGS : (k + 1) * SEGS]
            update, keep, scaled, slope, offset = first_slopes(pre, cand, gain)
            if first and k == 0 and block == 0:
                prev = lead_row(place, start_ref[:, wide], (SEGS, span))
                slope, offset = around(update, keep, scaled, cand, gain, prev)
            slope2, offset2 = around(update, keep, scaled, cand, gain, state)
            state = slope * state + offset
            b = slope2 * b + offset2
            a = slope2 * a
            row = pl.ds(pl.multiple_of(block * BLOCK + (2 * jj + k) * SEGS, SEGS), SEGS)
            run_ref[0, row, :] = a
            run_ref[1, row, :] = b
        return state, a, b

    def pair(jj, carry, first):
        return tuple(advance(m, jj, carry[m], first) for m in range(len(where)))

    one, zero = jnp.ones((SEGS, span), F32), jnp.zeros((SEGS, span), F32)
    carry = tuple((enter[m * SEGS : (m + 1) * SEGS, wide], one, zero) for m in range(len(where)))
    carry = pair(0, carry, True)
    carry = lax.fori_loop(1, BLOCK // SEGS // 2, lambda jj, c: pair(jj, c, False), carry)
    for m in range(len(where)):
        maps_ref[0, m * SEGS : (m + 1) * SEGS, wide] = carry[m][1]
        maps_ref[1, m * SEGS : (m + 1) * SEGS, wide] = carry[m][2]

    @pl.when(n == pl.num_programs(0) - 1)
    def _():
        ta, tb = jnp.ones((1, width), F32), jnp.zeros((1, width), F32)
        ta, tb = compose_rows(maps_ref, maps_ref.shape[1], ta, tb)
        for i in range(peers):
            total_ref[i, 0:1, :] = ta
            total_ref[i, 1:2, :] = tb


def bend_all(place, gates, maps, peer_maps, gain, start):
    chunks = len(gates)
    peers = peer_maps.shape[0]
    width = gates[0].shape[2]
    total_rows = sum(g.shape[1] for g in gates)
    segs = total_rows // BLOCK * SEGS
    tn = tile_of(width, 256)
    row_spec = pl.BlockSpec((1, width), lambda n, p: (0, 0))
    total_spec = pl.BlockSpec((peers, 2, width), lambda n, p: (0, 0, 0))
    return pl.pallas_call(
        functools.partial(bend_kernel, chunks, peers),
        out_shape=[
            jax.ShapeDtypeStruct((2, total_rows, width), F32),
            jax.ShapeDtypeStruct((2, segs, width), F32),
            jax.ShapeDtypeStruct((peers, 2, width), F32),
        ],
        grid_spec=pltpu.PrefetchScalarGridSpec(
            num_scalar_prefetch=1,
            grid=(width // tn,),
            in_specs=[pl.BlockSpec((2, g.shape[1], tn), lambda n, p: (0, 0, n)) for g in gates]
            + [pl.BlockSpec((2, m.shape[1], width), lambda n, p: (0, 0, 0)) for m in maps]
            + [total_spec, row_spec, row_spec],
            out_specs=[
                pl.BlockSpec((2, total_rows, tn), lambda n, p: (0, 0, n)),
                pl.BlockSpec((2, segs, width), lambda n, p: (0, 0, 0)),
                total_spec,
            ],
            scratch_shapes=[pltpu.VMEM((segs, width), F32)],
        ),
        compiler_params=params(16),
        cost_estimate=cost(
            40 * total_rows * width, 12 * total_rows * width, 5 * total_rows * width
        ),
        name="bend",
    )(place, *gates, *maps, peer_maps, gain, start)


def state_kernel(first_row, peers, place, run_ref, maps_ref, peer_ref, start_ref, out_ref, enter):
    rows = out_ref.shape[0]
    begin = first_row // BLOCK * SEGS
    state = entering_state(place, peer_ref, start_ref[...], peers)
    for k in range(begin + rows // BLOCK * SEGS):
        if k >= begin:
            enter[k - begin : k - begin + 1, :] = state
        state = maps_ref[0, k : k + 1, :] * state + maps_ref[1, k : k + 1, :]
    for c in range(rows // BLOCK):
        once = enter[c * SEGS : (c + 1) * SEGS, :]
        entered = jnp.concatenate([once, once], axis=0)

        def step(jj, carry):
            at = pl.multiple_of(c * BLOCK + jj * 2 * SEGS, 2 * SEGS)
            lines = pl.ds(at, 2 * SEGS)
            deep = pl.ds(pl.multiple_of(first_row + at, 2 * SEGS), 2 * SEGS)
            out_ref[lines, :] = (run_ref[0, deep, :] * entered + run_ref[1, deep, :]).astype(BF16)
            return carry

        lax.fori_loop(0, BLOCK // SEGS // 2, step, 0)


def state_chunk(place, run, maps, peer_maps, start, first_row, rows):
    width = run.shape[2]
    peers = peer_maps.shape[0]
    vmem = pl.BlockSpec(memory_space=pltpu.VMEM)
    return pl.pallas_call(
        functools.partial(state_kernel, first_row, peers),
        out_shape=jax.ShapeDtypeStruct((rows, width), BF16),
        in_specs=[pl.BlockSpec(memory_space=pltpu.SMEM)] + [vmem] * 4,
        out_specs=vmem,
        scratch_shapes=[pltpu.VMEM((rows // BLOCK * SEGS, width), F32)],
        compiler_params=params(16),
        cost_estimate=cost(2 * rows * width, 10 * rows * width),
    )(place, run, maps, peer_maps, start)


def mix_kernel(groups, group, cuts, peers, slots, final, before, place, *refs):
    count = groups * group
    blocks = refs[:count]
    starts = [sum(len(cut) for cut in cuts[:n]) for n in range(len(cuts) + 1)]
    weights = refs[count : count + starts[-1]]
    out_ref, lhs, wbuf, acc, lsem, wsem = refs[-6:]
    prev_refs = refs[count + len(weights) : count + len(weights) + before]
    depth = blocks[0].shape[1]
    heights = [blocks[c * group].shape[0] for c in range(groups)]
    outer = peers // 2
    here = len(slots) * 2

    def w_copy(n, p):
        w_ref = weights[starts[n] + p]
        top = sum(cuts[n][:p])
        dst = wbuf.at[n, top : top + cuts[n][p], :]
        return pltpu.make_async_copy(w_ref, dst, wsem.at[n, p])

    def l_copy(c, d):
        deep = pl.ds(pl.multiple_of((place[0] ^ d) * depth, depth), depth)
        top = sum(heights[:c])
        dst = lhs.at[top : top + heights[c], deep]
        return pltpu.make_async_copy(blocks[c * group + d], dst, lsem.at[c, d])

    for n in range(here):
        for p in range(len(cuts[n])):
            w_copy(n, p).start()
    pairs_of = max(1, depth // (2 * wbuf.shape[1]))

    def used(d):
        found = None
        for r in range(pairs_of):
            source = (place[0] ^ d) * pairs_of + r
            slot = lax.rem(place[1] // 2 + outer - source, outer)
            inside = (slot >= slots[0]) & (slot <= slots[-1])
            found = inside if found is None else found | inside
        return found

    for d in range(group):

        @pl.when(used(d))
        def _():
            for c in range(groups):
                l_copy(c, d).start()
            for c in range(groups):
                l_copy(c, d).wait()

    top = 0
    for prev in prev_refs:
        acc[top : top + prev.shape[0], :] = prev[...]
        top += prev.shape[0]
    span = wbuf.shape[1]
    for n in range(here):
        source = lax.rem(place[1] // 2 + outer - slots[n // 2], outer)
        owner = source * 2 + (lax.rem(place[1], 2) ^ (n % 2))
        deep = pl.ds(pl.multiple_of(owner * span, span), span)
        for p in range(len(cuts[n])):
            w_copy(n, p).wait()
        part = jnp.dot(lhs[:, deep], wbuf[n], preferred_element_type=F32)
        if n > 0 or before:
            part = acc[...] + part
        if n < here - 1:
            acc[...] = part
        elif not final:
            out_ref[...] = part
        else:
            acc[...] = part
            order = row_order(True)
            for m in range(acc.shape[0] // BLOCK):
                lines = slice(m * BLOCK, (m + 1) * BLOCK)
                rounded = acc[lines, :].astype(BF16)
                moved = jnp.dot(order, rounded, preferred_element_type=F32)
                out_ref[lines, :] = moved.astype(BF16)


def mix_rows(place, blocks, weights, slots, prev, final, whole, first, total_rows):
    groups, group = len(blocks), len(blocks[0])
    depth = blocks[0][0].shape[1]
    width = weights[0][0].shape[1]
    peers = len(weights)
    span = sum(piece.shape[0] for piece in weights[0])
    rows = sum(g[0].shape[0] for g in blocks)
    chosen = [weights[s * 2 + i] for s in slots for i in range(2)]
    cuts = tuple(tuple(piece.shape[0] for piece in pieces) for pieces in chosen)
    used = [piece for pieces in chosen for piece in pieces]
    most = max(len(cut) for cut in cuts)
    args = [place] + [b for g in blocks for b in g] + used
    in_specs = [pl.BlockSpec(memory_space=pl.ANY)] * (groups * group)
    in_specs += [pl.BlockSpec(memory_space=pltpu.HBM)] * len(used)
    args += prev
    in_specs += [pl.BlockSpec(memory_space=pltpu.VMEM)] * len(prev)
    aliases = {}
    if whole is not None:
        aliases = {len(args): 0}
        args.append(whole)
        in_specs.append(pl.BlockSpec(memory_space=pl.ANY))
    deep = len(slots) * 2 * span
    if final:
        out_shape = jax.ShapeDtypeStruct((total_rows, width), BF16)
        out_spec = pl.BlockSpec((rows, width), lambda n, p: (first // rows, 0))
    else:
        out_shape = jax.ShapeDtypeStruct((rows, width), F32)
        out_spec = pl.BlockSpec(memory_space=pltpu.VMEM)
    return pl.pallas_call(
        functools.partial(
            mix_kernel, groups, group, cuts, peers, tuple(slots), final, len(prev)
        ),
        out_shape=out_shape,
        grid_spec=pltpu.PrefetchScalarGridSpec(
            num_scalar_prefetch=1,
            grid=(1,),
            in_specs=in_specs,
            out_specs=out_spec,
            scratch_shapes=[
                pltpu.VMEM((rows, group * depth), BF16),
                pltpu.VMEM((len(slots) * 2, span, width), BF16),
                pltpu.VMEM((rows, width), F32),
                pltpu.SemaphoreType.DMA((groups, group)),
                pltpu.SemaphoreType.DMA((len(slots) * 2, most)),
            ],
        ),
        input_output_aliases=aliases,
        compiler_params=params(40 if peers <= 8 else 62),
        cost_estimate=cost(2 * rows * deep * width, 2 * deep * (width + rows) + 4 * rows * width),
    )(*args)


SHARES = (2, 1, 1)
RINGS_EARLY = 2
SWAPS_EARLY = 1


def cut_of(rows, shares):
    parts = [rows * share // sum(shares) for share in shares]
    return parts if min(parts) >= LANES else [rows]


def ring_cut(rows):
    return cut_of(rows, (1, 1))


def swap_cut(step, rows):
    return cut_of(rows, (1,) if step == 0 else (1, 1))


def recut(blocks, parts):
    if [b.shape[0] for b in blocks] == parts:
        return blocks
    (block,) = blocks
    tops = [sum(parts[:p]) for p in range(len(parts))]
    return [block[top : top + part] for top, part in zip(tops, parts)]


def behind(block, gate):
    return block if gate is None else lax.optimization_barrier((block, gate))[0]


def gather_early(w_output):
    peers = lax.axis_size("ctx")
    rows = w_output.shape[0]
    route = [(i, (i + 2) % peers) for i in range(peers)]
    held = {(0, 0): [w_output]}
    for step in range(1, RINGS_EARLY + 1):
        held[step, 0] = []
        for block in recut(held[step - 1, 0], ring_cut(rows)):
            held[step, 0].append(lax.ppermute(block, "ctx", route))
    for step in range(SWAPS_EARLY + 1):
        held[step, 1] = []
        for block in recut(held[step, 0], swap_cut(step, rows)):
            held[step, 1].append(swap(block, "ctx", 1))
    return held


def next_cuts(rows):
    return [ring_cut(rows), swap_cut(SWAPS_EARLY + 1, rows)]


def gather_late(held, following, middle, late):
    peers = lax.axis_size("ctx")
    outer = peers // 2
    rows = held[0, 0][0].shape[0]
    route = [(i, (i + 2) % peers) for i in range(peers)]
    for step in range(RINGS_EARLY + 1, outer):
        held[step, 0] = []
        if step == RINGS_EARLY + 1:
            source = following[0]
        else:
            source = recut(held[step - 1, 0], ring_cut(rows))
        for block in source:
            held[step, 0].append(lax.ppermute(behind(block, late), "ctx", route))
    for step in range(SWAPS_EARLY + 1, outer):
        held[step, 1] = []
        if step == SWAPS_EARLY + 1:
            source = following[1]
        else:
            source = recut(held[step, 0], swap_cut(step, rows))
        for p, block in enumerate(source):
            ahead = step == SWAPS_EARLY + 1 and p < len(source) - 1
            gate = middle if ahead else late
            held[step, 1].append(swap(behind(block, gate), "ctx", 1))
    return [held[step, i] for step in range(outer) for i in range(2)]


def layer(tokens, w_input, w_output, bias_update, bias_cand, recur_gain, start_state):
    peers = lax.axis_size("ctx")
    group = lax.axis_size("ch")
    half = group // 2
    total_rows = tokens.shape[0]
    chunks = len(SHARES)
    sizes = [total_rows * share // sum(SHARES) for share in SHARES]
    firsts = [sum(sizes[:c]) for c in range(chunks)]
    place = jnp.stack([lax.axis_index("ch"), lax.axis_index("ctx")]).astype(jnp.int32)
    biases = jnp.stack([bias_update, bias_cand], axis=0)
    gain = recur_gain[None, :]
    start = start_state[None, :]

    ordered = split_rows(tokens, 0, sizes[:1], None)
    *others, whole = split_rows(tokens, sizes[0], sizes[1:], ordered[0])
    ordered = [*ordered, *others]
    far = []
    for piece in ordered:
        far.append([swap(piece, "ch", half)])
    near = [[whole]]
    for d in range(1, half):
        near.append([swap(whole, "ch", d)])
    for c in range(chunks):
        for d in range(1, half):
            far[c].append(swap(far[c][0], "ch", d))

    partial = near_product(place, near, w_input)
    gates, maps = [], []
    for c in range(chunks):
        last = c == chunks - 1
        out = gate_chunk(
            place,
            far[c],
            partial,
            w_input,
            biases,
            gain,
            start,
            maps if last else [],
            firsts[c],
            last,
            peers,
        )
        gates.append(out[0])
        maps.append(out[1])
    held = gather_early(w_output)
    following = [recut(held[RINGS_EARLY, 0], cut) for cut in next_cuts(w_output.shape[0])]
    following, totals = lax.optimization_barrier((following, out[2]))
    first_maps = lax.all_to_all(totals, "ctx", 0, 0, tiled=True)
    run, run_maps, totals = bend_all(place, gates, maps, first_maps, gain, start)
    peer_maps = lax.all_to_all(totals, "ctx", 0, 0, tiled=True)
    weights = gather_late(held, following, first_maps, peer_maps)

    blocks = []
    for c in range(chunks):
        own = state_chunk(place, run, run_maps, peer_maps, start, firsts[c], sizes[c])
        across = swap(own, "ch", half)
        blocks.append([own, across])
    for c in range(chunks):
        own, across = blocks[c]
        lows, highs = [own], [across]
        for d in range(1, half):
            lows.append(swap(own, "ch", d))
            highs.append(swap(across, "ch", d))
        blocks[c] = lows + highs
    outer = peers // 2
    late = max(1, outer // 4)
    slots = list(range(outer))

    def mix(part, used, prev, final, whole):
        return mix_rows(
            place,
            blocks[part],
            weights,
            used,
            prev,
            final,
            whole,
            firsts[part][0],
            total_rows,
        )

    early, late_slots = slots[:-late], slots[-late:]
    partials = [mix(slice(c, c + 1), early, [], False, None) for c in range(chunks - 1)]
    mixed = mix(slice(0, chunks - 1), late_slots, partials, True, None)
    mixed = mix(slice(chunks - 1, chunks), slots, [], True, mixed)
    return mixed


def solution(mesh):
    return jax.shard_map(
        layer,
        mesh=mesh,
        in_specs=(
            P("ctx", "ch"),
            P(None, None, "ch"),
            P("ctx", "ch"),
            P("ch"),
            P("ch"),
            P("ch"),
            P("ch"),
        ),
        out_specs=P("ctx", "ch"),
        check_vma=False,
    )
```
